32 devices in a mesh: expert: 4 (over y, core), fsdp: 8 (over z, x).
Axes of the slice: x: 2, y: 2, z: 4, core: 2. Of those that a mesh axis runs over, the one named last changes fastest.
Arguments:
- tokens: bfloat16 [8, 1024, 768], P('fsdp', 'expert'), may hold values from -40 to 40
- gain_one: bfloat16 [768], P('fsdp'), may hold values from 0.5 to 1.5
- qkv_weight: bfloat16 [768, 2304], P('fsdp'), may hold values from -0.21875 to 0.21875
- out_weight: bfloat16 [768, 768], P('fsdp'), may hold values from -3.5 to 3.5
- gain_two: bfloat16 [768], P('fsdp'), may hold values from 0.5 to 1.5
- router_weight: bfloat16 [768, 8], P('fsdp'), may hold values from -0.109375 to 0.109375
- const_gate: bfloat16 [768, 4], P('fsdp'), may hold values from -0.21875 to 0.21875
- const_value: bfloat16 [768, 2], P('fsdp'), may hold values from -5 to 5
- expert_gate_up: bfloat16 [4, 768, 4096], P('expert', 'fsdp'), may hold values from -0.21875 to 0.21875
- expert_down: bfloat16 [4, 2048, 768], P('expert', 'fsdp'), may hold values from -0.125 to 0.125
- gate_residual: bfloat16 [8, 1024, 8], P('fsdp', 'expert'), may hold values from -3 to 3
- routes: int32 [8, 1024, 2], P('fsdp', 'expert'), may hold values from 0 to 7, all different within a row; in each aligned block of 256 rows (0 to 255, 256 to 511, ..., all dimensions but the last counted through in order) at most 80 rows name the same one
- cotangent: bfloat16 [8, 1024, 768], P('fsdp', 'expert'), may hold values from -6 to 6
Outputs:
- block_output: bfloat16 [8, 1024, 768], P('fsdp', 'expert')
- grad_tokens: bfloat16 [8, 1024, 768], P('fsdp', 'expert')
- grad_gain_one: float32 [768], P('fsdp')
- grad_qkv: float32 [768, 2304], P('fsdp')
- grad_out: float32 [768, 768], P('fsdp')
- grad_gain_two: float32 [768], P('fsdp')
- grad_router: float32 [768, 8], P('fsdp')
- grad_const_gate: float32 [768, 4], P('fsdp')
- grad_const_value: float32 [768, 2], P('fsdp')
- grad_gate_up: float32 [4, 768, 4096], P('expert', 'fsdp')
- grad_down: float32 [4, 2048, 768], P('expert', 'fsdp')
- grad_gate_residual: bfloat16 [8, 1024, 8], P('fsdp', 'expert')
- stream_rms: float32 [8, 2], P('fsdp')
The draws below stay inside these ranges and needn't reach their ends.
Inputs may be any that keep to these rules, and one draw needn't show every extreme that they name: In each aligned block of 256 rows (one sequence's positions on one index of expert) no expert is named by more than 80 routes; experts 4 to 7 are the zero, copy and constant experts.
All inputs are finite; a program needn't handle non-finite values.
Results may differ from the reference program's by a relative error of at most 0.024.
Values may be sent and summed in bfloat16 or wider, within the bound.
No kernel may reach another device: no remote copies, remote signals or barrier semaphores. Data moves between devices by JAX's collectives and lax.ppermute only.
A program may use at most 192 MiB of HBM per device.

```python
import math
import jax
import jax.numpy as jnp
import numpy as np
from jax import lax

D = 768
HEADS = 12
HEAD = 64
FF = 2048
NCONST = 2
TOK_SEQ = 256
NX = 4
NE = 8
MOST = 80
LEN = 1024
SEQS = 8


def draw_tokens(key, part):
    noise_key, scale_key = jax.random.split(key)
    position = jnp.arange(LEN, dtype=jnp.float32)[None, :, None]
    rising = 0.25 * 3.0 ** (position / LEN)
    spread = 10.0 ** jax.random.uniform(scale_key, (SEQS, LEN, 1), dtype=jnp.float32)
    entries = jnp.clip(jax.random.normal(noise_key, (SEQS, LEN, D), dtype=jnp.float32), -5.0, 5.0)
    return (entries * rising * spread).astype(jnp.bfloat16)


def strengthened(values, stream_key, source, target, blocks, factor):
    owner, partner = [(jnp.arange(values.shape[dim]) // (values.shape[dim] // blocks)).reshape([-1 if axis == dim else 1 for axis in range(values.ndim)]) for dim in (source, target)]
    chosen = jax.random.permutation(stream_key, blocks)[partner]
    strong = (owner == chosen) | (owner == (partner + blocks // 2) % blocks)
    return jnp.where(strong, factor * values, values)


def block_levels(stream_key, extent, cuts, low, top_value):
    level, own = 1.0, jax.random.fold_in(stream_key, 6)
    for axis_at, parts in cuts:
        draws = jnp.exp(jax.random.uniform(jax.random.fold_in(own, axis_at), (parts,), jnp.float32, low / len(cuts), top_value / len(cuts)))
        level = level * jnp.repeat(draws, extent[axis_at] // parts).reshape([-1 if axis == axis_at else 1 for axis in range(len(extent))])
    return level


def shared_out(stream_key, own, number, rows, count, top, most, lean):
    order = jax.random.permutation(stream_key, count)
    crowded, ordinary = shares(count, rows * top, most, lean, True), shares(count, rows * top, most, lean, False)
    places = jnp.arange(count)

    def named(lengths, turn):
        used = int((lengths > 0).sum())
        fixed = max(1, used // 4)
        shifted = fixed + (places - fixed + turn * (used - fixed)) % max(1, count - fixed)
        return jnp.zeros((count,), jnp.int32).at[order[jnp.where(places < fixed, places, shifted)]].set(jnp.asarray(lengths, jnp.int32))

    lengths = jnp.where(number % 4 == 0, named(crowded, number // 4), named(ordinary, number - number // 4 - 1))
    mixed = jax.random.permutation(jax.random.fold_in(own, 3), count)
    giver, receiver = mixed[0:count // 2 * 2:2], mixed[1:count // 2 * 2:2]
    room = jnp.minimum(lengths[giver] - 1, most - lengths[receiver]) // 2
    room = jnp.where((giver == order[0]) | (receiver == order[0]) | (lengths[receiver] == 0), 0, jnp.maximum(room, 0))
    shifted = jax.random.randint(jax.random.fold_in(own, 4), (count // 2,), 0, 1 << 20) % (room + 1)
    lengths = lengths.at[giver].add(-shifted).at[receiver].add(shifted)
    items = jnp.searchsorted(jnp.cumsum(lengths), jnp.arange(rows * top), side="right").astype(jnp.int32)
    table = items.reshape(top, rows).T
    table = table[jax.random.permutation(jax.random.fold_in(own, 1), rows)]
    turn = jax.random.randint(jax.random.fold_in(own, 2), (rows, 1), 0, top)
    return jnp.take_along_axis(table, (jnp.arange(top)[None, :] + turn) % top, axis=1)


def shares(amount, total, bound, skew, full):
    loads = [(1 << 20) // math.isqrt(rank ** skew) + 1 for rank in range(1, amount + 1)]
    largest = bound if full else min(bound, max(-(-total // amount), total * loads[0] // sum(loads)))
    least = 1 if total - largest >= amount - 1 else 0
    given, spare = [largest] + [least] * (amount - 1), total - largest - least * (amount - 1)
    while spare > 0:
        movable = [i for i in range(1, amount) if given[i] < largest] or [i for i in range(1, amount) if given[i] < bound]
        pool, budget = sum([loads[i] for i in movable]), spare
        for i in movable:
            addition = min(bound - given[i], max(1, budget * loads[i] // pool), spare)
            given[i] = given[i] + addition
            spare = spare - addition
    return np.array(given)


def scatter_about(own_key, shape, width, most, cuts=(), kind=jnp.bfloat16):
    gain = block_levels(own_key, shape, cuts, -0.22, 0.18) if cuts else 1.0
    drawn = jax.random.normal(own_key, shape, jnp.float32) * width * gain
    return jnp.minimum(jnp.maximum(drawn, -most), most).astype(kind)


def noise_with(key, shape, deviation, reach, cuts, heavy, held_as=jnp.bfloat16):
    drawn = deviation * jax.random.normal(key, shape, jnp.float32)
    if cuts:
        drawn = drawn * block_levels(key, shape, cuts, -0.22, 0.18)
    return jnp.clip(strengthened(drawn, jax.random.fold_in(key, 3), *heavy), -reach, reach).astype(held_as)


def setup_inputs(seed: int = 0) -> dict:
    key_of = jax.random.split(jax.random.key(seed), 14)
    tokens = draw_tokens(jax.random.fold_in(key_of[13], 71), 0)
    gain_one = jnp.clip(1.0 + 0.1 * jax.random.normal(key_of[1], (D,), jnp.float32), 0.5, 1.5).astype(jnp.bfloat16)
    qkv_weight = scatter_about(key_of[2], (D, 3 * D), D ** -0.5, 0.21875, ((0, 8),))
    out_weight = scatter_about(key_of[3], (D, D), (max(D // 256, 1)) ** -0.5, 3.5, ((0, 8),))
    gain_two = jnp.clip(1.0 + 0.1 * jax.random.normal(key_of[4], (D,), jnp.float32), 0.5, 1.5).astype(jnp.bfloat16)
    router_weight = scatter_about(key_of[5], (D, NE), (4 * D) ** -0.5, 0.109375, ((0, 8),))
    const_gate = scatter_about(key_of[6], (D, 2 * NCONST), D ** -0.5, 0.21875, ((0, 8),))
    const_value = scatter_about(key_of[7], (D, NCONST), 1.0, 5.0, ((0, 8),))
    expert_gate_up = scatter_about(key_of[8], (NX, D, 2 * FF), D ** -0.5, 0.21875, ((0, 4), (1, 8)))
    expert_down = scatter_about(key_of[9], (NX, FF, D), FF ** -0.5, 0.125, ((0, 4), (1, 8)))
    gate_residual = scatter_about(key_of[10], (SEQS, LEN, NE), 0.5, 3.0, ((0, 8), (1, 4)))
    routes_keys = jax.random.split(jax.random.fold_in(key_of[11], 1), SEQS * LEN // TOK_SEQ)
    routes_turns = jax.random.permutation(jax.random.fold_in(key_of[11], 3), SEQS * LEN // TOK_SEQ)
    routes = jax.vmap(lambda own, number: shared_out(jax.random.fold_in(key_of[11], 2), own, number, TOK_SEQ, NE, 2, MOST, 1))(routes_keys, routes_turns).reshape((SEQS, LEN, 2))
    cotangent = noise_with(key_of[12], (SEQS, LEN, D), 1.0, 6.0, ((0, 8), (1, 4)), (0, 2, 8, 2.0))
    return dict(tokens=tokens, gain_one=gain_one, qkv_weight=qkv_weight, out_weight=out_weight, gain_two=gain_two, router_weight=router_weight, const_gate=const_gate, const_value=const_value, expert_gate_up=expert_gate_up, expert_down=expert_down, gate_residual=gate_residual, routes=routes, cotangent=cotangent)


@jax.custom_vjp
def low(v):
    return lax.optimization_barrier(v.astype(jnp.bfloat16)).astype(jnp.float32)

@jax.custom_vjp
def low_back(v):
    return v

def low_keep(v):
    return (low(v), None)

def low_pass(kept, grad):
    return (grad,)

def back_keep(v):
    return (v, None)

def back_low(kept, grad):
    return (low(grad),)
low.defvjp(low_keep, low_pass)
low_back.defvjp(back_keep, back_low)
epsilon = 1e-06
highest = lax.Precision.HIGHEST
masked_score = -1e+30

def rms_scale(values):
    return lax.rsqrt(lax.optimization_barrier(jnp.mean(values * values, axis=-1, keepdims=True)) + epsilon)

def rotary(values, positions, direction):
    half_width = values.shape[-1] // 2
    frequency = 10000.0 ** (-jnp.arange(half_width, dtype=jnp.float32) / half_width)
    angles = positions.astype(jnp.float32)[:, None] * frequency[None, :]
    cosine = jnp.cos(angles)[:, None, :]
    sine_part = direction * jnp.sin(angles)[:, None, :]
    former = values[..., :half_width]
    latter = values[..., half_width:]
    return jnp.concatenate([former * cosine - latter * sine_part, latter * cosine + former * sine_part], axis=-1)

def local_mixture(normed_two, residual_gate, router_full, gate_full, value_full, returned, onehot, expert_count):
    logits = jnp.dot(normed_two, router_full, precision=highest) + residual_gate
    picked = lax.optimization_barrier(jnp.sum(onehot * logits[..., None, :], axis=-1))
    gates = jax.nn.softmax(picked, axis=-1)
    mix_logits = jnp.dot(normed_two, gate_full, precision=highest)
    mixing = jax.nn.softmax(mix_logits.reshape(mix_logits.shape[:-1] + (NCONST, 2)), axis=-1)
    const_out = mixing[..., 0:1] * normed_two[..., None, :] + mixing[..., 1:2] * value_full.T
    copy_out = onehot[..., expert_count + 1:expert_count + 2] * normed_two[..., None, :]
    chosen_const = jnp.einsum('...kc,...cd->...kd', onehot[..., expert_count + 2:], const_out, precision=highest)
    outputs = returned + copy_out + chosen_const
    return lax.optimization_barrier(jnp.sum(gates[..., None] * outputs, axis=-2))

def group_forward(weights, token_values, residual_group, routes_group):
    gain_one, qkv_weight, out_weight, gain_two, router_weight, const_gate, const_value, gate_up_weight, down_weight = weights
    group_size = token_values.shape[0]
    low_one = low(token_values * rms_scale(token_values) * gain_one)
    projected = low_back(jnp.einsum('gld,de->gle', low_one, qkv_weight, precision=highest))
    head_shape = (group_size, LEN, HEADS, HEAD)
    positions = jnp.arange(LEN, dtype=jnp.int32)
    queries = low(rotary(projected[..., :D].reshape(head_shape), positions, 1.0))
    key_rows = low(rotary(projected[..., D:2 * D].reshape(head_shape), positions, 1.0))
    value_rows = low(projected[..., 2 * D:].reshape(head_shape))
    query_block_rows = min(512, LEN)
    block_count = LEN // query_block_rows

    def attend_pair(pair):
        query_block, block_index = pair
        scores = low_back(jnp.einsum('gqhe,gkhe->ghqk', query_block, key_rows, precision=highest) * HEAD ** (-0.5))
        query_pos = block_index * query_block_rows + jnp.arange(query_block_rows, dtype=jnp.int32)
        visible = query_pos[:, None] >= positions[None, :]
        weights_now = jax.nn.softmax(jnp.where(visible, scores, masked_score), axis=-1)
        return jnp.einsum('ghqk,gkhe->gqhe', low(weights_now), value_rows, precision=highest)
    query_blocks = queries.reshape(group_size, block_count, query_block_rows, HEADS, HEAD).transpose(1, 0, 2, 3, 4)
    attended = lax.map(jax.checkpoint(attend_pair), (query_blocks, jnp.arange(block_count, dtype=jnp.int32)))
    attended = attended.transpose(1, 0, 2, 3, 4).reshape(group_size, LEN, D)
    attended = low(low_back(attended))
    branch = low_back(jnp.einsum('gld,de->gle', attended, out_weight, precision=highest))
    hidden = token_values + branch
    low_two = low(hidden * rms_scale(hidden) * gain_two)
    rows_all = group_size * LEN
    blocks = rows_all // TOK_SEQ
    capacity = blocks * MOST
    flat_routes = routes_group.reshape(blocks, TOK_SEQ * 2)
    ffn_hot = (flat_routes[..., None] == jnp.arange(NX, dtype=jnp.int32)).astype(jnp.int32)
    slot_rank = lax.optimization_barrier(jnp.sum((jnp.cumsum(ffn_hot, axis=1) - 1) * ffn_hot, axis=-1))
    block_index = jnp.arange(blocks, dtype=jnp.int32)[:, None]
    target = jnp.where(flat_routes < NX, flat_routes * capacity + block_index * MOST + slot_rank, NX * capacity).reshape(-1)
    route_rows = jnp.repeat(low_two.reshape(rows_all, D), 2, axis=0)
    buffer = jnp.zeros((NX * capacity, D), jnp.float32).at[target].add(route_rows, mode='drop')
    received = low_back(buffer.reshape(NX, capacity, D))
    gate_up = low_back(jnp.einsum('ecd,edf->ecf', received, gate_up_weight, precision=highest))
    activation = low(jax.nn.silu(gate_up[..., :FF]) * gate_up[..., FF:])
    expert_rows = low(low_back(jnp.einsum('ecf,efd->ecd', activation, down_weight, precision=highest)))
    returned = jnp.take(expert_rows.reshape(NX * capacity, D), target, axis=0, mode='fill', fill_value=0.0)
    returned = returned.reshape(group_size, LEN, 2, D)
    onehot = (routes_group[..., None] == jnp.arange(NE, dtype=jnp.int32)).astype(jnp.float32)
    mixture_out = local_mixture(low_two, residual_group, router_weight, const_gate, const_value, returned, onehot, NX)
    outputs = hidden + mixture_out
    stream_stats = jnp.stack([jnp.sqrt(lax.optimization_barrier(jnp.mean(hidden * hidden, axis=(1, 2)))), jnp.sqrt(lax.optimization_barrier(jnp.mean(outputs * outputs, axis=(1, 2))))], axis=-1)
    return (outputs, stream_stats)

def reference(tokens, gain_one, qkv_weight, out_weight, gain_two, router_weight, const_gate, const_value, expert_gate_up, expert_down, gate_residual, routes, cotangent):
    weights = (gain_one.astype(jnp.float32), qkv_weight.astype(jnp.float32), out_weight.astype(jnp.float32), gain_two.astype(jnp.float32), router_weight.astype(jnp.float32), const_gate.astype(jnp.float32), const_value.astype(jnp.float32), expert_gate_up.astype(jnp.float32), expert_down.astype(jnp.float32))
    token_values = tokens.astype(jnp.float32)
    residual_values = gate_residual.astype(jnp.float32)
    group_size = math.gcd(SEQS, max(1, 4096 // LEN))
    step_count = SEQS // group_size

    def forward(inputs, residual, weight_set):

        def one_group(state_in, pieces):
            result = jax.checkpoint(group_forward)(weight_set, pieces[0], pieces[1], pieces[2])
            return (state_in, result)
        grouped = (inputs.reshape(step_count, group_size, LEN, D), residual.reshape(step_count, group_size, LEN, NE), routes.reshape(step_count, group_size, LEN, 2))
        unused, results = lax.scan(one_group, None, grouped)
        return (results[0].reshape(SEQS, LEN, D), results[1].reshape(SEQS, 2))
    (outputs, stream_stats), pullback = jax.vjp(forward, token_values, residual_values, weights)
    grad_inputs, grad_residual, grad_weights = pullback((cotangent.astype(jnp.float32), jnp.zeros_like(stream_stats)))
    return (outputs.astype(jnp.bfloat16), grad_inputs.astype(jnp.bfloat16), grad_weights[0], grad_weights[1], grad_weights[2], grad_weights[3], grad_weights[4], grad_weights[5], grad_weights[6], grad_weights[7], grad_weights[8], grad_residual.astype(jnp.bfloat16), stream_stats)
```

```python
import functools

import jax
import jax.numpy as jnp
from jax import lax
from jax.experimental import pallas as pl
from jax.experimental.pallas import tpu as pltpu
from jax.sharding import PartitionSpec as P

HEAD = 64
FF = 2048
NCONST = 2
MOST = 80
PAIR = 2 * HEAD
SMALL = 128

epsilon = 1e-06
masked_score = -1e30
BF = jnp.bfloat16
F32 = jnp.float32


def mm(a, b):
    return jnp.dot(a, b, preferred_element_type=F32)


def mm_nt(a, b):
    return lax.dot_general(a, b, (((1,), (1,)), ((), ())), preferred_element_type=F32)


def mm_tn(a, b):
    return lax.dot_general(a, b, (((0,), (0,)), ((), ())), preferred_element_type=F32)


def split_low(values):
    high = values.astype(BF)
    return high, (values - high.astype(F32)).astype(BF)


def lanes(shape):
    return lax.broadcasted_iota(jnp.int32, shape, len(shape) - 1)


def rows_of(shape):
    return lax.broadcasted_iota(jnp.int32, shape, 0)


def rms_scale(values):
    return lax.rsqrt(jnp.mean(values * values, axis=-1, keepdims=True) + epsilon)


def turned(values, cosine, sine):
    lane = lanes(values.shape) % HEAD
    swapped = jnp.where(
        lane < HEAD // 2,
        pltpu.roll(values, PAIR - HEAD // 2, 1),
        pltpu.roll(values, HEAD // 2, 1),
    )
    return values * cosine + swapped * sine


def call(kernel, outs, args, grid=(), in_specs=None, out_specs=None, scratch=(), scalars=1, name=None):
    whole = pl.BlockSpec(memory_space=pltpu.VMEM)
    multi = isinstance(outs, (tuple, list))
    if in_specs is None:
        in_specs = [whole] * (len(args) - scalars)
    if out_specs is None:
        out_specs = [whole] * len(outs) if multi else whole
    return pl.pallas_call(
        kernel,
        out_shape=outs,
        grid_spec=pltpu.PrefetchScalarGridSpec(
            num_scalar_prefetch=scalars,
            grid=grid,
            in_specs=in_specs,
            out_specs=out_specs,
            scratch_shapes=list(scratch),
        ),
        compiler_params=pltpu.CompilerParams(vmem_limit_bytes=56 * 1024 * 1024),
        name=name,
    )(*args)


def shaped(shape, dtype):
    return jax.ShapeDtypeStruct(shape, dtype)


def swap(values, axis, bits):
    size = lax.axis_size(axis)
    return lax.ppermute(values, axis, [(i, i ^ bits) for i in range(size)])


def along(values, pairs):
    return lax.ppermute(
        values, "fsdp", [(2 * i + b, 2 * j + b) for i, j in pairs for b in (0, 1)]
    )


def after(values, *others):
    return lax.optimization_barrier((values,) + tuple(others))[0]


def major_gather(values):
    major = lax.axis_size("fsdp") // 2
    if major != 4:
        groups = [[2 * i + b for i in range(major)] for b in (0, 1)]
        return lax.all_gather(values, "fsdp", axis=0, tiled=True, axis_index_groups=groups)
    mine = lax.axis_index("fsdp") // 2
    far = along(values, [(0, 2), (2, 0), (1, 3), (3, 1)])
    middle = along(values, [(1, 2), (2, 1)])
    near = along(values, [(0, 1), (1, 0), (2, 3), (3, 2)])
    onward = along(far, [(2, 3), (1, 0)])
    inner = jnp.logical_or(mine == 1, mine == 2).astype(jnp.int32)
    scalars = jnp.stack([mine, mine ^ 1, mine ^ 2, mine ^ 3, inner]).astype(jnp.int32)
    rows = values.shape[0]

    def kernel(where, own, near_ref, far_ref, middle_ref, onward_ref, out):
        def put(slot, ref):
            out[pl.ds(pl.multiple_of(where[slot] * rows, rows), rows), :] = ref[...]

        put(0, own)
        put(1, near_ref)
        put(2, far_ref)

        @pl.when(where[4] == 1)
        def _():
            put(3, middle_ref)

        @pl.when(where[4] == 0)
        def _():
            put(3, onward_ref)

    return call(
        kernel,
        shaped((4 * rows,) + values.shape[1:], values.dtype),
        (scalars, values, near, far, middle, onward),
        name="place_parts",
    )


def major_scatter_sum(full):
    major = lax.axis_size("fsdp") // 2
    rows = full.shape[0] // major
    if major != 4:
        groups = [[2 * i + b for i in range(major)] for b in (0, 1)]
        return lax.psum_scatter(
            full, "fsdp", scatter_dimension=0, tiled=True, axis_index_groups=groups
        ).astype(F32)
    mine = lax.axis_index("fsdp") // 2

    def block(bits):
        return lax.dynamic_slice_in_dim(full, (mine ^ bits) * rows, rows, 0)

    third = block(3)
    first = along(third, [(0, 1), (3, 2)])
    far = along(block(2) + first, [(0, 2), (2, 0), (1, 3), (3, 1)])
    middle = along(third, [(1, 2), (2, 1)])
    near = along(block(1), [(0, 1), (1, 0), (2, 3), (3, 2)])
    return (
        block(0).astype(F32) + near.astype(F32) + far.astype(F32) + middle.astype(F32)
    )


def shared_gather(qkv, out, small):
    parts = lax.axis_size("fsdp")
    if parts != 8:
        return tuple(
            lax.all_gather(v, "fsdp", axis=0, tiled=True) for v in (qkv, out, small)
        ), None
    core = lax.axis_index("expert") % 2
    me = lax.axis_index("fsdp")
    half_qkv, half_out = qkv.shape[1] // 2, out.shape[1] // 2
    mine = jnp.concatenate(
        [
            lax.dynamic_slice_in_dim(qkv, core * half_qkv, half_qkv, 1),
            lax.dynamic_slice_in_dim(out, core * half_out, half_out, 1),
            small,
        ],
        axis=1,
    )
    major = [mine] + [swap(mine, "fsdp", 2 * j) for j in (1, 2, 3)]
    minor = [swap(v, "fsdp", 1) for v in major]
    slots = [2 * j for j in range(4)] + [2 * j + 1 for j in range(4)]
    own = jnp.concatenate(major + minor, axis=0)
    other = swap(own, "expert", 1)
    scalars = jnp.stack([me ^ s for s in slots] + [core]).astype(jnp.int32)
    rows = qkv.shape[0]

    def kernel(where, own_ref, other_ref, qkv_ref, out_ref, small_ref):
        first = where[8] == 0
        for index in range(8):
            source = pl.ds(index * rows, rows)
            target = pl.ds(pl.multiple_of(where[index] * rows, rows), rows)
            a, b = own_ref[source, :], other_ref[source, :]
            left = jnp.where(first, a, b)
            right = jnp.where(first, b, a)
            qkv_ref[target, :half_qkv] = left[:, :half_qkv]
            qkv_ref[target, half_qkv:] = right[:, :half_qkv]
            out_ref[target, :half_out] = left[:, half_qkv : half_qkv + half_out]
            out_ref[target, half_out:] = right[:, half_qkv : half_qkv + half_out]
            small_ref[target, :] = a[:, half_qkv + half_out :]

    full = call(
        kernel,
        [
            shaped((8 * rows, qkv.shape[1]), BF),
            shaped((8 * rows, out.shape[1]), BF),
            shaped((8 * rows, SMALL), BF),
        ],
        (scalars, own, other),
        name="place_shared",
    )
    return tuple(full), tuple(major)


def shared_scatter_sum(left, right):
    parts = lax.axis_size("fsdp")
    if parts != 8 or lax.axis_size("expert") != 4:
        full = jnp.concatenate([left, right], axis=1)
        shard = lax.psum_scatter(full, "fsdp", scatter_dimension=0, tiled=True)
        return lax.psum(shard, "expert").astype(F32)
    core = lax.axis_index("expert") % 2
    me = lax.axis_index("fsdp")
    minor, major = me % 2, me // 2
    first = core == 0
    away = jnp.where(first, right, left)
    kept = jnp.where(first, left, right)
    columns = left.shape[1]
    rows = left.shape[0] // 8
    both = (kept.astype(F32) + swap(away, "expert", 1).astype(F32)).astype(BF)
    both = both.reshape(4, 2, rows, columns)
    away = lax.dynamic_index_in_dim(both, 1 - minor, 1, False)
    kept = lax.dynamic_index_in_dim(both, minor, 1, False)
    both = (kept.astype(F32) + swap(away, "fsdp", 1).astype(F32)).astype(BF)
    total = lax.dynamic_index_in_dim(both, major, 0, False).astype(F32)
    for j in (1, 2, 3):
        total += swap(
            lax.dynamic_index_in_dim(both, major ^ j, 0, False), "fsdp", 2 * j
        ).astype(F32)
    total = total.astype(BF)
    total = (total.astype(F32) + swap(total, "expert", 2).astype(F32)).astype(BF)
    other = swap(total, "expert", 1)
    return jnp.concatenate(
        [jnp.where(first, total, other), jnp.where(first, other, total)], axis=1
    ).astype(F32)


def sequence_gather(values):
    size = lax.axis_size("expert")
    me = lax.axis_index("expert")
    if size != 4:
        return lax.all_gather(values, "expert", axis=0, tiled=True), list(range(size))
    pair = jnp.concatenate([values, swap(values, "expert", 2)], axis=0)
    return jnp.concatenate([pair, swap(pair, "expert", 1)], axis=0), [
        me,
        me ^ 2,
        me ^ 1,
        me ^ 3,
    ]


def sequence_scatter_sum(full, rows):
    size = lax.axis_size("expert")
    me = lax.axis_index("expert")
    if size != 4:
        return lax.psum_scatter(full, "expert", scatter_dimension=0, tiled=True).astype(F32)

    def block(bits):
        return lax.dynamic_slice_in_dim(full, (me ^ bits) * rows, rows, 0)

    away = jnp.concatenate([block(1), block(3)], axis=0)
    kept = jnp.concatenate([block(0), block(2)], axis=0)
    both = kept.astype(F32) + swap(away, "expert", 1).astype(F32)
    return both[:rows] + swap(both[rows:].astype(BF), "expert", 2).astype(F32)


def project_kernel(where, tok, weight, small_t, cosine, sine, q, k, v, normed, *, slots, gain_at):
    step = pl.program_id(0)
    rank = where[step]
    own = where[slots]
    width = tok.shape[1]

    @pl.when(rank > own)
    def _():
        k[...] = jnp.zeros_like(k)
        v[...] = jnp.zeros_like(v)
        normed[...] = jnp.zeros_like(normed)

    @pl.when(rank <= own)
    def _():
        x = tok[...].astype(F32)
        low = ((x * rms_scale(x)) * small_t[gain_at : gain_at + 1, :]).astype(BF)
        normed[...] = low
        cos, sin = cosine[...], sine[...]
        keys = mm(low, weight[:, width : 2 * width])
        for at in range(0, width, PAIR):
            k[:, at : at + PAIR] = turned(keys[:, at : at + PAIR], cos, sin).astype(BF)
        v[...] = mm(low, weight[:, 2 * width :]).astype(BF)

        @pl.when(rank == own)
        def _():
            queries = mm(low, weight[:, :width])
            for at in range(0, width, PAIR):
                q[:, at : at + PAIR] = turned(queries[:, at : at + PAIR], cos, sin).astype(BF)


def stacked_heads(values, scale=None):
    lane = lanes(values.shape)
    if scale is not None:
        values = values * jnp.asarray(scale, values.dtype)
    zero = jnp.zeros_like(values)
    return jnp.concatenate(
        [jnp.where(lane < HEAD, values, zero), jnp.where(lane < HEAD, zero, values)], axis=0
    )


def visible_keys(own, keys, count):
    key = lax.broadcasted_iota(jnp.int32, (keys, 2 * count), 0)
    query = lax.broadcasted_iota(jnp.int32, (keys, 2 * count), 1) % count
    return key <= query + own * count


def attend_kernel(where, q, k, v, attended, log_total, *, slots):
    own = where[slots]
    count, keys = q.shape[0], k.shape[0]
    query = stacked_heads(q[...], HEAD ** (-0.5))
    scores = mm_nt(k[...], query)
    scores = jnp.where(visible_keys(own, keys, count), scores, masked_score)
    top = jnp.max(scores, axis=0, keepdims=True)
    weights = jnp.exp(scores - top)
    total = jnp.sum(weights, axis=0, keepdims=True)
    log_total[...] = jnp.broadcast_to(top + jnp.log(total), (8, 2 * count))[None]
    weights = (weights * (1.0 / total)).astype(BF)
    both = mm_tn(weights, v[...])
    lane = lanes((count, PAIR))
    attended[...] = jnp.where(lane < HEAD, both[:count], both[count:]).astype(BF)


def attend_back_kernel(where, q, k, v, grad_att, log_total, cosine, sine, cos_own, sin_own, dq, dk, dv, *, slots):
    own = where[slots]
    count, keys = q.shape[0], k.shape[0]
    query = stacked_heads(q[...], HEAD ** (-0.5))
    grad_rows = stacked_heads(grad_att[...])
    key_rows = k[...]
    scores = mm_nt(key_rows, query)
    weights = jnp.where(
        visible_keys(own, keys, count), jnp.exp(scores - log_total[0, :1, :]), 0.0
    )
    grad_weights = mm_nt(v[...], grad_rows)
    delta = jnp.sum(weights * grad_weights, axis=0, keepdims=True)
    grad_scores = (weights * (grad_weights - delta)).astype(BF)
    dv[...] = mm(weights.astype(BF), grad_rows).astype(BF)
    dk[...] = turned(mm(grad_scores, query), cosine[...], -sine[...]).astype(BF)
    both = mm_tn(grad_scores, key_rows)
    lane = lanes((count, PAIR))
    grad_query = jnp.where(lane < HEAD, both[:count], both[count:]) * HEAD ** (-0.5)
    dq[...] = turned(grad_query, cos_own[...], -sin_own[...]).astype(BF)


def routing(routes, resid, logits, groups):
    count = routes.shape[0]
    lane = lanes((count, SMALL))
    kind = lanes(resid.shape)
    hot, picked = [], []
    for choice in range(2):
        route = routes[:, choice : choice + 1]
        hot.append(lane == route)
        picked.append(
            jnp.sum(jnp.where(hot[choice], logits, 0.0), axis=-1, keepdims=True)
            + jnp.sum(jnp.where(kind == route, resid, 0.0), axis=-1, keepdims=True)
        )
    top = jnp.maximum(picked[0], picked[1])
    first, second = jnp.exp(picked[0] - top), jnp.exp(picked[1] - top)
    gates = [first / (first + second), second / (first + second)]
    named = jnp.logical_or(hot[0], hot[1]).astype(BF)
    earlier = (lanes((count, count)) < rows_of((count, count))).astype(BF)
    place = mm(earlier, named)
    dispatch = []
    column = lanes((count, groups * MOST))
    for choice in range(2):
        route = routes[:, choice : choice + 1]
        slot = jnp.sum(jnp.where(hot[choice], place, 0.0), axis=-1, keepdims=True)
        target = jnp.where(route < groups, route * MOST + slot.astype(jnp.int32), -1)
        dispatch.append((column == target).astype(BF))
    return gates, hot, dispatch


def route_kernel(where, att, out_weight, tok, small, small_t, resid, routes, cot, hidden_ref, low_ref, *rest, groups, gain_at):
    sends = rest[:groups]
    rows_x, rows_g = rest[groups], rest[groups + 1]
    hidden = tok[...].astype(F32) + mm(att[...], out_weight[...])
    hidden_ref[...] = hidden
    low = ((hidden * rms_scale(hidden)) * small_t[gain_at : gain_at + 1, :]).astype(BF)
    low_ref[...] = low
    logits = mm(low, small[...])
    gates, _, dispatch = routing(routes[...], resid[...].astype(F32), logits, groups)
    grad = cot[...].astype(F32)
    rows_x[...] = mm_tn(dispatch[0] + dispatch[1], low).astype(BF)
    rows_g[...] = (
        mm_tn(dispatch[0], (gates[0] * grad).astype(BF))
        + mm_tn(dispatch[1], (gates[1] * grad).astype(BF))
    ).astype(BF)
    for slot in range(groups):
        source = pl.ds(pl.multiple_of(where[slot] * MOST, MOST), MOST)
        sends[slot][:MOST, :] = rows_x[source, :]
        sends[slot][MOST:, :] = rows_g[source, :]


def expert_kernel(*refs, groups, hidden_units):
    own, other = refs[:groups], refs[groups : 2 * groups]
    gate_up, down = refs[2 * groups], refs[2 * groups + 1]
    own_out = refs[2 * groups + 2 : 3 * groups + 2]
    other_out = refs[3 * groups + 2 : 4 * groups + 2]
    grad_gate_up, grad_down = refs[4 * groups + 2], refs[4 * groups + 3]
    rows, grads, out_rows, back_rows = refs[4 * groups + 4 :]
    for index, ref in enumerate(own + other):
        target = slice(index * MOST, (index + 1) * MOST)
        rows[target, :] = ref[:MOST, :]
        grads[target, :] = ref[MOST:, :]
    x, g = rows[...], grads[...]
    chunk = 256
    for at in range(0, hidden_units, chunk):
        gate_w = gate_up[:, at : at + chunk]
        up_w = gate_up[:, hidden_units + at : hidden_units + at + chunk]
        down_w = down[at : at + chunk, :]
        gate, up = mm(x, gate_w), mm(x, up_w)
        sig = 1.0 / (1.0 + jnp.exp(-gate))
        silu = gate * sig
        act = (silu * up).astype(BF)
        grad_act = mm_nt(g, down_w)
        grad_gate = (grad_act * up * sig * (1.0 + gate * (1.0 - sig))).astype(BF)
        grad_up = (grad_act * silu).astype(BF)
        part_out = mm(act, down_w)
        part_back = mm_nt(grad_gate, gate_w) + mm_nt(grad_up, up_w)
        if at == 0:
            out_rows[...] = part_out
            back_rows[...] = part_back
        else:
            out_rows[...] += part_out
            back_rows[...] += part_back
        grad_gate_up[:, at : at + chunk] = mm_tn(x, grad_gate).astype(BF)
        grad_gate_up[:, hidden_units + at : hidden_units + at + chunk] = mm_tn(x, grad_up).astype(BF)
        grad_down[at : at + chunk, :] = mm_tn(act, g).astype(BF)
    for index, ref in enumerate(own_out + other_out):
        source = slice(index * MOST, (index + 1) * MOST)
        ref[:MOST, :] = out_rows[source, :].astype(ref.dtype)
        ref[MOST:, :] = back_rows[source, :].astype(ref.dtype)


def combine_kernel(where, *refs, groups, columns, shard_rows):
    backs = refs[:groups]
    (hidden_ref, low_ref, cot, routes, resid, small, small_t, out_weight, att,
     out_ref, grad_hidden_ref, grad_att_ref, grad_left, grad_right, grad_small, grad_resid,
     rows_y, rows_d) = refs[groups:]
    kinds, mix_at, value_at, gain_one_at, gain_two_at, square_at = columns
    for slot in range(groups):
        target = pl.ds(pl.multiple_of(where[slot] * MOST, MOST), MOST)
        rows_y[target, :] = backs[slot][:MOST, :]
        rows_d[target, :] = backs[slot][MOST:, :]
    hidden, low = hidden_ref[...], low_ref[...]
    count = low.shape[0]
    normed_input = low.astype(F32)
    grad_low_type = cot[...]
    grad = grad_low_type.astype(F32)
    logits = mm(low, small[...])
    grad_small_dot = mm(grad_low_type, small[...])
    route = routes[...]
    gates, hot, dispatch = routing(route, resid[...].astype(F32), logits, groups)
    returned = [mm(dispatch[c], rows_y[...]) for c in range(2)]
    grad_back = mm(dispatch[0] + dispatch[1], rows_d[...])
    grad_dot = jnp.sum(grad * normed_input, axis=-1, keepdims=True)
    is_copy = [(route[:, c : c + 1] == groups + 1).astype(F32) for c in range(2)]
    grad_gates = [
        jnp.sum(grad * returned[c], axis=-1, keepdims=True) + is_copy[c] * grad_dot
        for c in range(2)
    ]
    direct = gates[0] * is_copy[0] + gates[1] * is_copy[1]
    mixture = gates[0] * returned[0] + gates[1] * returned[1]
    lane = lanes((count, SMALL))
    grad_logits = jnp.zeros((count, SMALL), F32)
    value_weights = jnp.zeros((count, SMALL), F32)
    for const in range(NCONST):
        first = logits[:, mix_at + 2 * const : mix_at + 2 * const + 1]
        second = logits[:, mix_at + 2 * const + 1 : mix_at + 2 * const + 2]
        top = jnp.maximum(first, second)
        first, second = jnp.exp(first - top), jnp.exp(second - top)
        mix = [first / (first + second), second / (first + second)]
        value_dot = grad_small_dot[:, value_at + const : value_at + const + 1]
        named = [(route[:, c : c + 1] == groups + 2 + const).astype(F32) for c in range(2)]
        for c in range(2):
            grad_gates[c] += named[c] * (mix[0] * grad_dot + mix[1] * value_dot)
        weight = gates[0] * named[0] + gates[1] * named[1]
        direct += weight * mix[0]
        of_value = weight * mix[1]
        mixture += of_value * small_t[value_at + const : value_at + const + 1, :]
        value_weights = jnp.where(lane == value_at + const, of_value, value_weights)
        grad_mix = [weight * grad_dot, weight * value_dot]
        common = mix[0] * grad_mix[0] + mix[1] * grad_mix[1]
        for c in range(2):
            grad_logits = jnp.where(
                lane == mix_at + 2 * const + c, mix[c] * (grad_mix[c] - common), grad_logits
            )
    outputs = hidden + mixture + direct * normed_input
    out_ref[...] = outputs.astype(BF)
    common = gates[0] * grad_gates[0] + gates[1] * grad_gates[1]
    for c in range(2):
        grad_logits = jnp.where(hot[c], gates[c] * (grad_gates[c] - common), grad_logits)
    grad_resid[...] = grad_logits[:, :kinds].astype(BF)
    high, rest = split_low(grad_logits)
    weights = small[...]
    grad_low = grad_back + direct * grad + mm_nt(high, weights) + mm_nt(rest, weights)
    scale = rms_scale(hidden)
    normed = hidden * scale
    of_gain = split_low(grad_low * normed)
    ones = (lane == gain_two_at).astype(BF)
    value_high, value_rest = split_low(value_weights)
    summed = (
        mm_tn(low, high)
        + mm_tn(low, rest)
        + mm_tn(grad_low_type, value_high)
        + mm_tn(grad_low_type, value_rest)
        + mm_tn(of_gain[0], ones)
        + mm_tn(of_gain[1], ones)
    )
    column, row = lanes(summed.shape), rows_of(summed.shape)
    mine = row // shard_rows == where[groups]
    for index, total in enumerate((jnp.sum(hidden * hidden), jnp.sum(outputs * outputs))):
        for part, value in enumerate(split_low(jnp.full((1, 1), total, F32))):
            spot = jnp.logical_and(mine, column == square_at + 2 * index + part)
            summed = jnp.where(spot, value.astype(F32), summed)
    grad_small[...] = summed.astype(BF)
    grad_normed = grad_low * small_t[gain_two_at : gain_two_at + 1, :]
    grad_hidden = grad + scale * (
        grad_normed - normed * jnp.mean(grad_normed * normed, axis=-1, keepdims=True)
    )
    grad_hidden_ref[...] = grad_hidden
    branch = grad_hidden.astype(BF)
    grad_att_ref[...] = mm_nt(branch, out_weight[...]).astype(BF)
    grad_out = mm_tn(att[...], branch).astype(BF)
    middle = grad_out.shape[1] // 2
    grad_left[...] = grad_out[:, :middle]
    grad_right[...] = grad_out[:, middle:]


def project_back_kernel(where, tok, normed, dq, dk, dv, weight, left, right, rows_back, own_back, total, gain_total, *, slots, gain_at):
    step = pl.program_id(0)
    rank = where[step]
    own = where[slots]
    width = tok.shape[1]

    @pl.when(step == 0)
    def _():
        total[...] = jnp.zeros_like(total)
        gain_total[...] = jnp.zeros_like(gain_total)

    @pl.when(rank > own)
    def _():
        rows_back[...] = jnp.zeros_like(rows_back)

    @pl.when(rank <= own)
    def _():
        low = normed[...]
        x = tok[...].astype(F32)
        unit = x * rms_scale(x)
        grad_k, grad_v = dk[...], dv[...]
        total[:, width : 2 * width] += mm_tn(low, grad_k)
        total[:, 2 * width :] += mm_tn(low, grad_v)
        back = mm_nt(grad_k, weight[:, width : 2 * width]) + mm_nt(grad_v, weight[:, 2 * width :])
        rows_back[...] = back.astype(BF)
        gain_total[...] += jnp.sum((back * unit).reshape(-1, 8, width), axis=0)

        @pl.when(rank == own)
        def _():
            grad_q = dq[...]
            total[:, :width] += mm_tn(low, grad_q)
            mine = mm_nt(grad_q, weight[:, :width])
            own_back[...] = mine
            gain_total[...] += jnp.sum((mine * unit).reshape(-1, 8, width), axis=0)

    @pl.when(step == slots - 1)
    def _():
        half = left.shape[1]
        ones = (lanes((8, SMALL)) == gain_at).astype(BF)
        high, rest = split_low(gain_total[...])
        extra = mm_tn(high, ones) + mm_tn(rest, ones)
        left[...] = total[:, :half].astype(BF)
        right[:, : 3 * width - half] = total[:, half:].astype(BF)
        right[:, 3 * width - half :] = extra.astype(BF)


def finish_kernel(tok, small_t, grad_hidden, own_back, rows_back, out, *, gain_at):
    x = tok[...].astype(F32)
    scale = rms_scale(x)
    normed = x * scale
    grad = (own_back[...] + rows_back[...]) * small_t[gain_at : gain_at + 1, :]
    out[...] = (
        grad_hidden[...]
        + scale * (grad - normed * jnp.mean(grad * normed, axis=-1, keepdims=True))
    ).astype(BF)


def on_device(
    tokens,
    gain_one,
    qkv_weight,
    out_weight,
    gain_two,
    router_weight,
    const_gate,
    const_value,
    expert_gate_up,
    expert_down,
    gate_residual,
    routes,
    cotangent,
):
    parts = lax.axis_size("fsdp")
    groups = lax.axis_size("expert")
    me_fsdp = lax.axis_index("fsdp")
    me_expert = lax.axis_index("expert")
    minor = me_fsdp % 2
    major_count = parts // 2
    tok = tokens[0]
    count, width = tok.shape
    length = groups * count
    pairs = width // PAIR
    kinds = router_weight.shape[1]
    mix_at, value_at = kinds, kinds + 2 * NCONST
    gain_one_at = value_at + NCONST
    gain_two_at = gain_one_at + 1
    square_at = gain_two_at + 1
    shard_rows = width // parts

    tok_all, ranks = sequence_gather(tok)
    where = jnp.stack([jnp.asarray(r, jnp.int32) for r in ranks] + [me_expert.astype(jnp.int32)])

    unit = FF // parts
    halves = expert_gate_up[0].reshape(shard_rows, 2, major_count, 2, unit)
    away = lax.dynamic_index_in_dim(halves, 1 - minor, 3, False).reshape(shard_rows, FF)
    kept = lax.dynamic_index_in_dim(halves, minor, 3, False).reshape(shard_rows, FF)
    arrived = swap(away, "fsdp", 1)
    gate_up_rows = jnp.concatenate(
        [jnp.where(minor == 0, kept, arrived), jnp.where(minor == 0, arrived, kept)], axis=0
    )

    small_shard = jnp.concatenate(
        [
            router_weight,
            const_gate,
            const_value,
            gain_one[:, None],
            gain_two[:, None],
            jnp.zeros((shard_rows, SMALL - square_at), BF),
        ],
        axis=1,
    )
    (qkv_full, out_full, small), stage = shared_gather(qkv_weight, out_weight, small_shard)
    small_t = small.astype(F32).T[:32]

    down_rows = expert_down[0]
    if stage is not None:
        gate_up_rows = after(gate_up_rows, *stage)
        down_rows = after(down_rows, *stage)
    gate_up_half = major_gather(gate_up_rows)
    down_half = major_gather(down_rows)

    frequency = 10000.0 ** (-jnp.arange(HEAD // 2, dtype=F32) / (HEAD // 2))
    angles = jnp.arange(length, dtype=F32)[:, None] * frequency[None, :]
    cosine, sine = jnp.cos(angles), jnp.sin(angles)
    cosine = jnp.concatenate([cosine, cosine, cosine, cosine], axis=1)
    sine = jnp.concatenate([-sine, sine, -sine, sine], axis=1)

    at_rank = lambda j, w: (w[j], 0)
    fixed = lambda j, w: (0, 0)
    q, k_all, v_all, normed_all = call(
        functools.partial(project_kernel, slots=groups, gain_at=gain_one_at),
        [
            shaped((count, width), BF),
            shaped((length, width), BF),
            shaped((length, width), BF),
            shaped((length, width), BF),
        ],
        (where, tok_all, qkv_full, small_t, cosine, sine),
        grid=(groups,),
        in_specs=[
            pl.BlockSpec((count, width), lambda j, w: (j, 0)),
            pl.BlockSpec((width, 3 * width), fixed),
            pl.BlockSpec((32, width), fixed),
            pl.BlockSpec((count, PAIR), at_rank),
            pl.BlockSpec((count, PAIR), at_rank),
        ],
        out_specs=[
            pl.BlockSpec((count, width), fixed),
            pl.BlockSpec((count, width), at_rank),
            pl.BlockSpec((count, width), at_rank),
            pl.BlockSpec((count, width), at_rank),
        ],
        name="project",
    )
    head_rows = pl.BlockSpec((count, PAIR), lambda h, w: (0, h))
    head_keys = pl.BlockSpec((length, PAIR), lambda h, w: (0, h))
    head_log = pl.BlockSpec((1, 8, 2 * count), lambda h, w: (h, 0, 0))
    attended, log_total = call(
        functools.partial(attend_kernel, slots=groups),
        [shaped((count, width), BF), shaped((pairs, 8, 2 * count), F32)],
        (where, q, k_all, v_all),
        grid=(pairs,),
        in_specs=[head_rows, head_keys, head_keys],
        out_specs=[head_rows, head_log],
        name="attend",
    )

    residual = gate_residual[0]
    route = routes[0]
    cot = cotangent[0]
    slots = jnp.stack([(me_expert ^ j).astype(jnp.int32) for j in range(groups)] + [me_fsdp.astype(jnp.int32)])
    packed = shaped((2 * MOST, width), BF)
    hidden, low_two, *sends = call(
        functools.partial(route_kernel, groups=groups, gain_at=gain_two_at),
        [shaped((count, width), F32), shaped((count, width), BF)] + [packed] * groups,
        (slots, attended, out_full, tok, small, small_t, residual, route, cot),
        scratch=[pltpu.VMEM((groups * MOST, width), BF)] * 2,
        name="route",
    )
    received = [sends[0]] + [swap(sends[j], "expert", j) for j in range(1, groups)]
    others = [swap(v, "fsdp", 1) for v in received]
    units = FF // 2
    rows_total = 2 * groups * MOST
    results = call(
        functools.partial(expert_kernel, groups=groups, hidden_units=units),
        [shaped((2 * MOST, width), F32)] * groups
        + [packed] * groups
        + [shaped((width, 2 * units), BF), shaped((units, width), BF)],
        tuple(received) + tuple(others) + (gate_up_half, down_half),
        scratch=[pltpu.VMEM((rows_total, width), BF)] * 2
        + [pltpu.VMEM((rows_total, width), F32)] * 2,
        scalars=0,
        name="expert",
    )
    own_part, other_part = results[:groups], results[groups : 2 * groups]
    grad_gate_up, grad_down = results[2 * groups :]
    joined = [
        (a + swap(b, "fsdp", 1).astype(F32)).astype(BF) for a, b in zip(own_part, other_part)
    ]
    backs = [joined[0]] + [swap(joined[j], "expert", j) for j in range(1, groups)]

    shard_down = major_scatter_sum(grad_down)
    part = major_scatter_sum(grad_gate_up).reshape(2, shard_rows, FF)
    away = lax.dynamic_index_in_dim(part, 1 - minor, 0, False).astype(BF)
    kept = lax.dynamic_index_in_dim(part, minor, 0, False)
    arrived = swap(away, "fsdp", 1).astype(F32)
    first = jnp.where(minor == 0, kept, arrived).reshape(shard_rows, 2, major_count, 1, unit)
    second = jnp.where(minor == 0, arrived, kept).reshape(shard_rows, 2, major_count, 1, unit)
    shard_gate_up = jnp.concatenate([first, second], axis=3).reshape(shard_rows, 2 * FF)

    columns = (kinds, mix_at, value_at, gain_one_at, gain_two_at, square_at)
    outputs, grad_hidden, grad_att, out_left, out_right, grad_small, grad_residual = call(
        functools.partial(combine_kernel, groups=groups, columns=columns, shard_rows=shard_rows),
        [
            shaped((count, width), BF),
            shaped((count, width), F32),
            shaped((count, width), BF),
            shaped((width, width // 2), BF),
            shaped((width, width // 2), BF),
            shaped((width, SMALL), BF),
            shaped((count, kinds), BF),
        ],
        (slots,) + tuple(backs)
        + (hidden, low_two, cot, route, residual, small, small_t, out_full, attended),
        scratch=[pltpu.VMEM((groups * MOST, width), BF)] * 2,
        name="combine",
    )
    out_sum = shared_scatter_sum(
        jnp.concatenate([out_left, grad_small], axis=1),
        jnp.concatenate([out_right, jnp.zeros_like(grad_small)], axis=1),
    )
    own_rows = pl.BlockSpec((count, PAIR), lambda h, w: (w[groups], 0))
    all_rows = pl.BlockSpec((length, PAIR), lambda h, w: (0, 0))
    dq, dk, dv = call(
        functools.partial(attend_back_kernel, slots=groups),
        [shaped((count, width), BF), shaped((length, width), BF), shaped((length, width), BF)],
        (where, q, k_all, v_all, grad_att, log_total, cosine, sine, cosine, sine),
        grid=(pairs,),
        in_specs=[head_rows, head_keys, head_keys, head_rows, head_log, all_rows, all_rows, own_rows, own_rows],
        out_specs=[head_rows, head_keys, head_keys],
        name="attend_back",
    )
    half = 3 * width // 2 + SMALL // 2
    half = (half + 127) // 128 * 128
    left, right, rows_back, own_back = call(
        functools.partial(project_back_kernel, slots=groups, gain_at=gain_one_at),
        [
            shaped((width, half), BF),
            shaped((width, 3 * width + SMALL - half), BF),
            shaped((length, width), BF),
            shaped((count, width), F32),
        ],
        (where, tok_all, normed_all, dq, dk, dv, qkv_full),
        grid=(groups,),
        in_specs=[
            pl.BlockSpec((count, width), lambda j, w: (j, 0)),
            pl.BlockSpec((count, width), at_rank),
            pl.BlockSpec((count, width), fixed),
            pl.BlockSpec((count, width), at_rank),
            pl.BlockSpec((count, width), at_rank),
            pl.BlockSpec((width, 3 * width), fixed),
        ],
        out_specs=[
            pl.BlockSpec((width, half), fixed),
            pl.BlockSpec((width, 3 * width + SMALL - half), fixed),
            pl.BlockSpec((count, width), at_rank),
            pl.BlockSpec((count, width), fixed),
        ],
        scratch=[pltpu.VMEM((width, 3 * width), F32), pltpu.VMEM((8, width), F32)],
        name="project_back",
    )
    if right.shape[1] < half:
        right = jnp.concatenate([right, jnp.zeros((width, half - right.shape[1]), BF)], axis=1)
    qkv_sum = shared_scatter_sum(left, right)
    rows_sum = sequence_scatter_sum(rows_back, count)
    grad_tokens = call(
        functools.partial(finish_kernel, gain_at=gain_one_at),
        shaped((count, width), BF),
        (tok, small_t, grad_hidden, own_back, rows_sum),
        scalars=0,
        name="finish",
    )

    small_sum = out_sum[:, width // 2 : width // 2 + SMALL]
    shard_out = jnp.concatenate(
        [out_sum[:, : width // 2], out_sum[:, width // 2 + SMALL : width + SMALL]], axis=1
    )
    squares = small_sum[0, square_at : square_at + 4]
    stream = jnp.sqrt(
        jnp.stack([squares[0] + squares[1], squares[2] + squares[3]]) / (length * width)
    )
    return (
        outputs[None],
        grad_tokens[None],
        qkv_sum[:, 3 * width + gain_one_at],
        qkv_sum[:, : 3 * width],
        shard_out,
        small_sum[:, gain_two_at],
        small_sum[:, :kinds],
        small_sum[:, mix_at : mix_at + 2 * NCONST],
        small_sum[:, value_at : value_at + NCONST],
        shard_gate_up[None],
        shard_down[None],
        grad_residual[None],
        stream[None],
    )


def solution(mesh):
    return jax.shard_map(
        on_device,
        mesh=mesh,
        in_specs=(
            P("fsdp", "expert", None),
            P("fsdp"),
            P("fsdp", None),
            P("fsdp", None),
            P("fsdp"),
            P("fsdp", None),
            P("fsdp", None),
            P("fsdp", None),
            P("expert", "fsdp", None),
            P("expert", "fsdp", None),
            P("fsdp", "expert", None),
            P("fsdp", "expert", None),
            P("fsdp", "expert", None),
        ),
        out_specs=(
            P("fsdp", "expert", None),
            P("fsdp", "expert", None),
            P("fsdp"),
            P("fsdp", None),
            P("fsdp", None),
            P("fsdp"),
            P("fsdp", None),
            P("fsdp", None),
            P("fsdp", None),
            P("expert", "fsdp", None),
            P("expert", "fsdp", None),
            P("fsdp", "expert", None),
            P("fsdp", None),
        ),
        check_vma=False,
    )
```

```python
import functools

import jax
import jax.numpy as jnp
from jax import lax
from jax.experimental import pallas as pl
from jax.experimental.pallas import tpu as pltpu
from jax.sharding import PartitionSpec as P

HEAD = 64
FF = 2048
NCONST = 2
MOST = 80
PAIR = 2 * HEAD
SMALL = 128

epsilon = 1e-06
masked_score = -1e30
BF = jnp.bfloat16
F32 = jnp.float32


def mm(a, b):
    return jnp.dot(a, b, preferred_element_type=F32)


def mm_nt(a, b):
    return lax.dot_general(a, b, (((1,), (1,)), ((), ())), preferred_element_type=F32)


def mm_tn(a, b):
    return lax.dot_general(a, b, (((0,), (0,)), ((), ())), preferred_element_type=F32)


def split_low(values):
    high = values.astype(BF)
    return high, (values - high.astype(F32)).astype(BF)


def lanes(shape):
    return lax.broadcasted_iota(jnp.int32, shape, len(shape) - 1)


def rows_of(shape):
    return lax.broadcasted_iota(jnp.int32, shape, 0)


def rms_scale(values):
    return lax.rsqrt(jnp.mean(values * values, axis=-1, keepdims=True) + epsilon)


def turned(values, cosine, sine):
    lane = lanes(values.shape) % HEAD
    swapped = jnp.where(
        lane < HEAD // 2,
        pltpu.roll(values, PAIR - HEAD // 2, 1),
        pltpu.roll(values, HEAD // 2, 1),
    )
    return values * cosine + swapped * sine


def call(kernel, outs, args, grid=(), in_specs=None, out_specs=None, scratch=(), scalars=1, name=None, micros=2):
    whole = pl.BlockSpec(memory_space=pltpu.VMEM)
    multi = isinstance(outs, (tuple, list))
    if in_specs is None:
        in_specs = [whole] * (len(args) - scalars)
    if out_specs is None:
        out_specs = [whole] * len(outs) if multi else whole
    return pl.pallas_call(
        kernel,
        out_shape=outs,
        grid_spec=pltpu.PrefetchScalarGridSpec(
            num_scalar_prefetch=scalars,
            grid=grid,
            in_specs=in_specs,
            out_specs=out_specs,
            scratch_shapes=list(scratch),
        ),
        compiler_params=pltpu.CompilerParams(vmem_limit_bytes=56 * 1024 * 1024),
        cost_estimate=pl.CostEstimate(
            flops=micros * 90_000_000, transcendentals=0, bytes_accessed=micros * 300_000
        ),
        name=name,
    )(*args)


def shaped(shape, dtype):
    return jax.ShapeDtypeStruct(shape, dtype)


def swap(values, axis, bits):
    size = lax.axis_size(axis)
    return lax.ppermute(values, axis, [(i, i ^ bits) for i in range(size)])


def along(values, pairs):
    return lax.ppermute(
        values, "fsdp", [(2 * i + b, 2 * j + b) for i, j in pairs for b in (0, 1)]
    )


def after(values, *others):
    return lax.optimization_barrier((values,) + tuple(others))[0]


FAR = ((0, 2), (2, 0), (1, 3), (3, 1))
NEAR = ((0, 1), (1, 0), (2, 3), (3, 2))
MIDDLE = ((1, 2), (2, 1))
OUTWARD = ((2, 3), (1, 0))
INWARD = ((0, 1), (3, 2))


def minor_groups(major):
    return [[2 * i + b for i in range(major)] for b in (0, 1)]


def blocks_kernel(where, gate_up, out):
    rows = gate_up.shape[0]
    for block in range(8):
        at = (2 * block + 1 - where[0]) * 256
        out[block * rows : (block + 1) * rows, :] = gate_up[:, pl.ds(pl.multiple_of(at, 256), 256)]


def pack_kernel(where, gate_up, arrived, down, out):
    rows = gate_up.shape[0]
    mine = where[0]
    for block in range(8):
        at = (2 * block + mine) * 256
        own = pl.ds(pl.multiple_of(2 * block * rows + mine * rows, rows), rows)
        other = pl.ds(pl.multiple_of(2 * block * rows + (1 - mine) * rows, rows), rows)
        out[own, :] = gate_up[:, pl.ds(pl.multiple_of(at, 256), 256)]
        out[other, :] = arrived[block * rows : (block + 1) * rows, :]
    base = 16 * rows
    for block in range(3):
        out[base + block * 256 : base + (block + 1) * 256, :] = down[:, block * 256 : (block + 1) * 256]


def sum_parts_kernel(where, a, b, c, early, late, away, kept, down):
    rows = away.shape[0] // 8
    mine = where[0]

    split = early.shape[0]

    def total(start, size, block):
        d, base = (early, 0) if block * 2 * rows < split else (late, split)
        source, shifted = pl.ds(start, size), pl.ds(start - base, size)
        return (
            a[source, :].astype(F32)
            + b[source, :].astype(F32)
            + c[source, :].astype(F32)
            + d[shifted, :].astype(F32)
        )

    for block in range(8):
        here = slice(block * rows, (block + 1) * rows)
        base = 2 * block * rows
        own = pl.multiple_of(base + mine * rows, rows)
        other = pl.multiple_of(base + (1 - mine) * rows, rows)
        away[here, :] = total(other, rows, block).astype(BF)
        kept[here, :] = total(own, rows, block)
    base = 16 * rows
    for block in range(3):
        down[:, block * 256 : (block + 1) * 256] = total(
            base + block * 256, 256, 8
        )


def unpack_kernel(where, kept, arrived, out):
    rows = out.shape[0]
    mine = where[0]
    for block in range(8):
        here = slice(block * rows, (block + 1) * rows)
        own = pl.ds(pl.multiple_of((2 * block + mine) * 256, 256), 256)
        other = pl.ds(pl.multiple_of((2 * block + 1 - mine) * 256, 256), 256)
        out[:, own] = kept[here, :]
        out[:, other] = arrived[here, :].astype(F32)


def shared_pack(qkv, out, small_rows):
    core = lax.axis_index("expert") % 2
    half_qkv, half_out = qkv.shape[1] // 2, out.shape[1] // 2
    rows = qkv.shape[0]

    def kernel(where, qkv_ref, out_ref, small_ref, packed):
        packed[:, :half_qkv] = qkv_ref[:, pl.ds(pl.multiple_of(where[0] * half_qkv, 128), half_qkv)]
        packed[:, half_qkv : half_qkv + half_out] = out_ref[
            :, pl.ds(pl.multiple_of(where[0] * half_out, 128), half_out)
        ]
        packed[:32, half_qkv + half_out :] = small_ref[...]
        packed[32:, half_qkv + half_out :] = jnp.zeros((rows - 32, SMALL), BF)

    return call(
        kernel,
        shaped((rows, half_qkv + half_out + SMALL), BF),
        (jnp.stack([core]).astype(jnp.int32), qkv, out, small_rows),
        name="pack_shared",
        micros=1,
    )


def shared_gather(mine, early):
    me = lax.axis_index("fsdp")
    major = [mine]
    for j in (1, 2, 3):
        major.append(swap(mine, "fsdp", 2 * j))
    minor = [swap(mine, "fsdp", 1)]
    for j in (1, 2, 3):
        minor.append(swap(after(major[j], *early[j - 1]), "fsdp", 1))
    slots = [2 * j for j in range(4)] + [2 * j + 1 for j in range(4)]
    own = jnp.concatenate(major + minor, axis=0)
    return own, swap(own, "expert", 1), [me ^ s for s in slots], major


def across_cores(away, kept):
    return (kept.astype(F32) + swap(away, "expert", 1).astype(F32)).astype(BF)


def minor_halves(both, rows):
    minor = lax.axis_index("fsdp") % 2
    both = both.reshape(4, 2, rows, both.shape[1])
    return (
        lax.dynamic_index_in_dim(both, 1 - minor, 1, False),
        lax.dynamic_index_in_dim(both, minor, 1, False),
    )


def added(kept, arrived):
    return (kept.astype(F32) + arrived.astype(F32)).astype(BF)


def across_rest(parts):
    major = lax.axis_index("fsdp") // 2
    total = lax.dynamic_index_in_dim(parts, major, 0, False).astype(F32)
    for j in (1, 2, 3):
        total += swap(
            lax.dynamic_index_in_dim(parts, major ^ j, 0, False), "fsdp", 2 * j
        ).astype(F32)
    total = total.astype(BF)
    total = (total.astype(F32) + swap(total, "expert", 2).astype(F32)).astype(BF)
    return total, swap(total, "expert", 1)


def sequence_gather(values, across):
    size = lax.axis_size("expert")
    me = lax.axis_index("expert")
    if size != 4:
        return lax.all_gather(values, "expert", axis=0, tiled=True), list(range(size))
    pair = jnp.concatenate([values, across], axis=0)
    return jnp.concatenate([pair, swap(pair, "expert", 1)], axis=0), [
        me,
        me ^ 2,
        me ^ 1,
        me ^ 3,
    ]


def sequence_scatter_sum(full, rows):
    size = lax.axis_size("expert")
    me = lax.axis_index("expert")
    if size != 4:
        return lax.psum_scatter(full, "expert", scatter_dimension=0, tiled=True).astype(F32)

    def block(bits):
        return lax.dynamic_slice_in_dim(full, (me ^ bits) * rows, rows, 0)

    away = jnp.concatenate([block(1), block(3)], axis=0)
    kept = jnp.concatenate([block(0), block(2)], axis=0)
    both = kept.astype(F32) + swap(away, "expert", 1).astype(F32)
    return both[:rows] + swap(both[rows:].astype(BF), "expert", 2).astype(F32)


def project_kernel(where, *refs, slots, gain_at, placed):
    if placed:
        tok, cosine, sine, weight, small_t, q, k, v, normed = refs
    else:
        tok, cosine, sine, own_ref, other_ref, q, k, v, normed, weight, out_ref, small_ref, small_t = refs
    step = pl.program_id(0)
    rank = where[step]
    own = where[slots]
    width = tok.shape[1]

    if not placed:

        @pl.when(step == 0)
        def _():
            first = where[slots + 9] == 0
            rows = width // 8
            half_qkv, half_out = 3 * width // 2, width // 2
            for index in range(8):
                source = pl.ds(index * rows, rows)
                target = pl.ds(pl.multiple_of(where[slots + 1 + index] * rows, rows), rows)
                a, b = own_ref[source, :], other_ref[source, :]
                left = jnp.where(first, a, b)
                right = jnp.where(first, b, a)
                weight[target, :half_qkv] = left[:, :half_qkv]
                weight[target, half_qkv:] = right[:, :half_qkv]
                out_ref[target, :half_out] = left[:, half_qkv : half_qkv + half_out]
                out_ref[target, half_out:] = right[:, half_qkv : half_qkv + half_out]
                of_rows = jnp.zeros((SMALL, SMALL), F32)
                of_rows = jnp.concatenate(
                    [a[:32, half_qkv + half_out :].astype(F32), of_rows[32:]], axis=0
                ).T
                small_ref[target, :] = of_rows[:rows].astype(BF)
            small_t[...] = small_ref[...].astype(F32).T[:32]

    @pl.when(rank > own)
    def _():
        k[...] = jnp.zeros_like(k)
        v[...] = jnp.zeros_like(v)
        normed[...] = jnp.zeros_like(normed)

    @pl.when(rank <= own)
    def _():
        x = tok[...].astype(F32)
        low = ((x * rms_scale(x)) * small_t[gain_at : gain_at + 1, :]).astype(BF)
        normed[...] = low
        cos, sin = cosine[...], sine[...]
        keys = mm(low, weight[:, width : 2 * width])
        for at in range(0, width, PAIR):
            k[:, at : at + PAIR] = turned(keys[:, at : at + PAIR], cos, sin).astype(BF)
        v[...] = mm(low, weight[:, 2 * width :]).astype(BF)

        @pl.when(rank == own)
        def _():
            queries = mm(low, weight[:, :width])
            for at in range(0, width, PAIR):
                q[:, at : at + PAIR] = turned(queries[:, at : at + PAIR], cos, sin).astype(BF)


def stacked_heads(values, scale=None):
    lane = lanes(values.shape)
    if scale is not None:
        values = values * jnp.asarray(scale, values.dtype)
    zero = jnp.zeros_like(values)
    return jnp.concatenate(
        [jnp.where(lane < HEAD, values, zero), jnp.where(lane < HEAD, zero, values)], axis=0
    )


def visible_keys(own, keys, count):
    key = lax.broadcasted_iota(jnp.int32, (keys, 2 * count), 0)
    query = lax.broadcasted_iota(jnp.int32, (keys, 2 * count), 1) % count
    return key <= query + own * count


def attend_kernel(where, q, k, v, attended, log_total, *, slots):
    own = where[slots]
    count, keys = q.shape[0], k.shape[0]
    query = stacked_heads(q[...], HEAD ** (-0.5))
    scores = mm_nt(k[...], query)
    scores = jnp.where(visible_keys(own, keys, count), scores, masked_score)
    top = jnp.max(scores, axis=0, keepdims=True)
    weights = jnp.exp(scores - top)
    total = jnp.sum(weights, axis=0, keepdims=True)
    log_total[...] = jnp.broadcast_to(top + jnp.log(total), (8, 2 * count))[None]
    weights = (weights * (1.0 / total)).astype(BF)
    both = mm_tn(weights, v[...])
    lane = lanes((count, PAIR))
    attended[...] = jnp.where(lane < HEAD, both[:count], both[count:]).astype(BF)


def attend_back_kernel(where, q, k, v, grad_att, log_total, cosine, sine, cos_own, sin_own, dq, dk, dv, *, slots):
    own = where[slots]
    count, keys = q.shape[0], k.shape[0]
    query = stacked_heads(q[...], HEAD ** (-0.5))
    grad_rows = stacked_heads(grad_att[...])
    key_rows = k[...]
    scores = mm_nt(key_rows, query)
    weights = jnp.where(
        visible_keys(own, keys, count), jnp.exp(scores - log_total[0, :1, :]), 0.0
    )
    grad_weights = mm_nt(v[...], grad_rows)
    delta = jnp.sum(weights * grad_weights, axis=0, keepdims=True)
    grad_scores = (weights * (grad_weights - delta)).astype(BF)
    dv[...] = mm(weights.astype(BF), grad_rows).astype(BF)
    dk[...] = turned(mm(grad_scores, query), cosine[...], -sine[...]).astype(BF)
    both = mm_tn(grad_scores, key_rows)
    lane = lanes((count, PAIR))
    grad_query = jnp.where(lane < HEAD, both[:count], both[count:]) * HEAD ** (-0.5)
    dq[...] = turned(grad_query, cos_own[...], -sin_own[...]).astype(BF)


def routing(routes, resid, logits, groups):
    count = routes.shape[0]
    lane = lanes((count, SMALL))
    kind = lanes(resid.shape)
    hot, picked = [], []
    for choice in range(2):
        route = routes[:, choice : choice + 1]
        hot.append(lane == route)
        picked.append(
            jnp.sum(jnp.where(hot[choice], logits, 0.0), axis=-1, keepdims=True)
            + jnp.sum(jnp.where(kind == route, resid, 0.0), axis=-1, keepdims=True)
        )
    top = jnp.maximum(picked[0], picked[1])
    first, second = jnp.exp(picked[0] - top), jnp.exp(picked[1] - top)
    gates = [first / (first + second), second / (first + second)]
    named = jnp.logical_or(hot[0], hot[1]).astype(BF)
    earlier = (lanes((count, count)) < rows_of((count, count))).astype(BF)
    place = mm(earlier, named)
    dispatch = []
    column = lanes((count, groups * MOST))
    for choice in range(2):
        route = routes[:, choice : choice + 1]
        slot = jnp.sum(jnp.where(hot[choice], place, 0.0), axis=-1, keepdims=True)
        target = jnp.where(route < groups, route * MOST + slot.astype(jnp.int32), -1)
        dispatch.append((column == target).astype(BF))
    return gates, hot, dispatch


def route_kernel(where, att, out_weight, tok, small, small_t, resid, routes, cot, hidden_ref, low_ref, *rest, groups, gain_at):
    sends = rest[:groups]
    rows_x, rows_g = rest[groups], rest[groups + 1]
    hidden = tok[...].astype(F32) + mm(att[...], out_weight[...])
    hidden_ref[...] = hidden
    low = ((hidden * rms_scale(hidden)) * small_t[gain_at : gain_at + 1, :]).astype(BF)
    low_ref[...] = low
    logits = mm(low, small[...])
    gates, _, dispatch = routing(routes[...], resid[...].astype(F32), logits, groups)
    grad = cot[...].astype(F32)
    rows_x[...] = mm_tn(dispatch[0] + dispatch[1], low).astype(BF)
    rows_g[...] = (
        mm_tn(dispatch[0], (gates[0] * grad).astype(BF))
        + mm_tn(dispatch[1], (gates[1] * grad).astype(BF))
    ).astype(BF)
    for slot in range(groups):
        source = pl.ds(pl.multiple_of(where[slot] * MOST, MOST), MOST)
        sends[slot][:MOST, :] = rows_x[source, :]
        sends[slot][MOST:, :] = rows_g[source, :]


def expert_kernel(where, *refs, groups, hidden_units, packed):
    refs = list(refs)

    def take(amount):
        taken = refs[:amount]
        del refs[:amount]
        return taken

    received = take(groups) + take(2)
    if packed:
        own_part, near, far, middle, onward = take(5)
    else:
        gate_up, down = take(2)
    own_out, other_out = take(2), take(2)
    if packed:
        messages = take(4)
    else:
        grad_gate_up, grad_down = take(2)
    rows, grads, out_rows, back_rows, acts, grad_units = take(6)
    if packed:
        gate_up, down = take(2)
    width = rows.shape[1]
    total = 2 * groups * MOST
    index = 0
    for ref in received:
        for base in range(0, ref.shape[0], 2 * MOST):
            target = slice(index * MOST, (index + 1) * MOST)
            rows[target, :] = ref[base : base + MOST, :]
            grads[target, :] = ref[base + MOST : base + 2 * MOST, :]
            index += 1
    if packed:
        part = width // 4

        def place(slot, ref):
            target = pl.ds(pl.multiple_of(where[slot] * part, part), part)
            for block in range(8):
                gate_up[target, block * 256 : (block + 1) * 256] = ref[
                    block * part : (block + 1) * part, :
                ]
            target = pl.ds(pl.multiple_of(where[slot] * 256, 256), 256)
            for block in range(3):
                base = 8 * part + block * 256
                down[target, block * 256 : (block + 1) * 256] = ref[base : base + 256, :]

        place(0, own_part)
        place(1, near)
        place(2, far)

        @pl.when(where[4] == 1)
        def _():
            place(3, middle)

        @pl.when(where[4] == 0)
        def _():
            place(3, onward)

    x, g = rows[...], grads[...]
    chunk = 256
    for at in range(0, hidden_units, chunk):
        gate_w = gate_up[:, at : at + chunk]
        up_w = gate_up[:, hidden_units + at : hidden_units + at + chunk]
        down_w = down[at : at + chunk, :]
        gate, up = mm(x, gate_w), mm(x, up_w)
        sig = 1.0 / (1.0 + jnp.exp(-gate))
        silu = gate * sig
        act = (silu * up).astype(BF)
        acts[:, at : at + chunk] = act
        grad_act = mm_nt(g, down_w)
        grad_gate = (grad_act * up * sig * (1.0 + gate * (1.0 - sig))).astype(BF)
        grad_up = (grad_act * silu).astype(BF)
        grad_units[:, at : at + chunk] = grad_gate
        grad_units[:, hidden_units + at : hidden_units + at + chunk] = grad_up
        part_out = mm(act, down_w)
        part_back = mm_nt(grad_gate, gate_w) + mm_nt(grad_up, up_w)
        if at == 0:
            out_rows[...] = part_out
            back_rows[...] = part_back
        else:
            out_rows[...] += part_out
            back_rows[...] += part_back
    index = 0
    for ref in own_out + other_out:
        for base in range(0, ref.shape[0], 2 * MOST):
            source = slice(index * MOST, (index + 1) * MOST)
            ref[base : base + MOST, :] = out_rows[source, :].astype(ref.dtype)
            ref[base + MOST : base + 2 * MOST, :] = back_rows[source, :].astype(ref.dtype)
            index += 1
    if not packed:
        grad_gate_up[...] = mm_tn(x, grad_units[...]).astype(BF)
        grad_down[...] = mm_tn(acts[...], g).astype(BF)
        return
    part = width // 4
    for block in range(8):
        of_block = mm_tn(x, grad_units[:, block * 256 : (block + 1) * 256])
        gate_up[:, block * 256 : (block + 1) * 256] = of_block.astype(BF)
    for slot, ref in enumerate(messages):
        source = pl.ds(pl.multiple_of(where[slot] * part, part), part)
        for block in range(8):
            ref[block * part : (block + 1) * part, :] = gate_up[
                source, block * 256 : (block + 1) * 256
            ]
        mine = acts[:, pl.ds(pl.multiple_of(where[slot] * 256, 256), 256)]
        of_down = mm_tn(mine, g).astype(BF)
        for block in range(3):
            base = 8 * part + block * 256
            ref[base : base + 256, :] = of_down[:, block * 256 : (block + 1) * 256]


def combine_kernel(where, *refs, groups, columns, shard_rows):
    backs = refs[:groups]
    (hidden_ref, low_ref, cot, routes, resid, small, small_t, out_weight, att,
     out_ref, grad_hidden_ref, grad_att_ref, grad_away, grad_kept, grad_resid,
     rows_y, rows_d) = refs[groups:]
    kinds, mix_at, value_at, gain_one_at, gain_two_at, square_at = columns
    for slot in range(groups):
        target = pl.ds(pl.multiple_of(where[slot] * MOST, MOST), MOST)
        rows_y[target, :] = backs[slot][:MOST, :]
        rows_d[target, :] = backs[slot][MOST:, :]
    hidden, low = hidden_ref[...], low_ref[...]
    count = low.shape[0]
    normed_input = low.astype(F32)
    grad_low_type = cot[...]
    grad = grad_low_type.astype(F32)
    logits = mm(low, small[...])
    grad_small_dot = mm(grad_low_type, small[...])
    route = routes[...]
    gates, hot, dispatch = routing(route, resid[...].astype(F32), logits, groups)
    returned = [mm(dispatch[c], rows_y[...]) for c in range(2)]
    grad_back = mm(dispatch[0] + dispatch[1], rows_d[...])
    grad_dot = jnp.sum(grad * normed_input, axis=-1, keepdims=True)
    is_copy = [(route[:, c : c + 1] == groups + 1).astype(F32) for c in range(2)]
    grad_gates = [
        jnp.sum(grad * returned[c], axis=-1, keepdims=True) + is_copy[c] * grad_dot
        for c in range(2)
    ]
    direct = gates[0] * is_copy[0] + gates[1] * is_copy[1]
    mixture = gates[0] * returned[0] + gates[1] * returned[1]
    lane = lanes((count, SMALL))
    grad_logits = jnp.zeros((count, SMALL), F32)
    value_weights = jnp.zeros((count, SMALL), F32)
    for const in range(NCONST):
        first = logits[:, mix_at + 2 * const : mix_at + 2 * const + 1]
        second = logits[:, mix_at + 2 * const + 1 : mix_at + 2 * const + 2]
        top = jnp.maximum(first, second)
        first, second = jnp.exp(first - top), jnp.exp(second - top)
        mix = [first / (first + second), second / (first + second)]
        value_dot = grad_small_dot[:, value_at + const : value_at + const + 1]
        named = [(route[:, c : c + 1] == groups + 2 + const).astype(F32) for c in range(2)]
        for c in range(2):
            grad_gates[c] += named[c] * (mix[0] * grad_dot + mix[1] * value_dot)
        weight = gates[0] * named[0] + gates[1] * named[1]
        direct += weight * mix[0]
        of_value = weight * mix[1]
        mixture += of_value * small_t[value_at + const : value_at + const + 1, :]
        value_weights = jnp.where(lane == value_at + const, of_value, value_weights)
        grad_mix = [weight * grad_dot, weight * value_dot]
        common = mix[0] * grad_mix[0] + mix[1] * grad_mix[1]
        for c in range(2):
            grad_logits = jnp.where(
                lane == mix_at + 2 * const + c, mix[c] * (grad_mix[c] - common), grad_logits
            )
    outputs = hidden + mixture + direct * normed_input
    out_ref[...] = outputs.astype(BF)
    common = gates[0] * grad_gates[0] + gates[1] * grad_gates[1]
    for c in range(2):
        grad_logits = jnp.where(hot[c], gates[c] * (grad_gates[c] - common), grad_logits)
    grad_resid[...] = grad_logits[:, :kinds].astype(BF)
    high, rest = split_low(grad_logits)
    weights = small[...]
    grad_low = grad_back + direct * grad + mm_nt(high, weights) + mm_nt(rest, weights)
    scale = rms_scale(hidden)
    normed = hidden * scale
    of_gain = split_low(grad_low * normed)
    ones = (lane == gain_two_at).astype(BF)
    value_high, value_rest = split_low(value_weights)
    summed = (
        mm_tn(low, high)
        + mm_tn(low, rest)
        + mm_tn(grad_low_type, value_high)
        + mm_tn(grad_low_type, value_rest)
        + mm_tn(of_gain[0], ones)
        + mm_tn(of_gain[1], ones)
    )
    column, row = lanes(summed.shape), rows_of(summed.shape)
    mine = row // shard_rows == where[groups]
    for index, total in enumerate((jnp.sum(hidden * hidden), jnp.sum(outputs * outputs))):
        for part, value in enumerate(split_low(jnp.full((1, 1), total, F32))):
            spot = jnp.logical_and(mine, column == square_at + 2 * index + part)
            summed = jnp.where(spot, value.astype(F32), summed)
    grad_normed = grad_low * small_t[gain_two_at : gain_two_at + 1, :]
    grad_hidden = grad + scale * (
        grad_normed - normed * jnp.mean(grad_normed * normed, axis=-1, keepdims=True)
    )
    grad_hidden_ref[...] = grad_hidden
    branch = grad_hidden.astype(BF)
    grad_att_ref[...] = mm_nt(branch, out_weight[...]).astype(BF)
    grad_out = mm_tn(att[...], branch).astype(BF)
    middle = grad_out.shape[1] // 2
    left = jnp.concatenate([grad_out[:, :middle], summed.astype(BF)], axis=1)
    right = jnp.concatenate([grad_out[:, middle:], jnp.zeros(summed.shape, BF)], axis=1)
    first = where[groups + 1] == 0
    grad_away[...] = jnp.where(first, right, left)
    grad_kept[...] = jnp.where(first, left, right)


def project_back_kernel(where, tok, normed, dq, dk, dv, weight, away, kept, rows_back, own_back, total, gain_total, *, slots, gain_at):
    step = pl.program_id(0)
    rank = where[step]
    own = where[slots]
    width = tok.shape[1]

    @pl.when(step == 0)
    def _():
        total[...] = jnp.zeros_like(total)
        gain_total[...] = jnp.zeros_like(gain_total)

    @pl.when(rank > own)
    def _():
        rows_back[...] = jnp.zeros_like(rows_back)

    @pl.when(rank <= own)
    def _():
        low = normed[...]
        x = tok[...].astype(F32)
        unit = x * rms_scale(x)
        grad_k, grad_v = dk[...], dv[...]
        total[:, width : 2 * width] += mm_tn(low, grad_k)
        total[:, 2 * width :] += mm_tn(low, grad_v)
        back = mm_nt(grad_k, weight[:, width : 2 * width]) + mm_nt(grad_v, weight[:, 2 * width :])
        rows_back[...] = back.astype(BF)
        gain_total[...] += jnp.sum((back * unit).reshape(-1, 8, width), axis=0)

        @pl.when(rank == own)
        def _():
            grad_q = dq[...]
            total[:, :width] += mm_tn(low, grad_q)
            mine = mm_nt(grad_q, weight[:, :width])
            own_back[...] = mine
            gain_total[...] += jnp.sum((mine * unit).reshape(-1, 8, width), axis=0)

    @pl.when(step == slots - 1)
    def _():
        half = kept.shape[1]
        ones = (lanes((8, SMALL)) == gain_at).astype(BF)
        high, rest = split_low(gain_total[...])
        extra = mm_tn(high, ones) + mm_tn(rest, ones)
        left = total[:, :half].astype(BF)
        right = jnp.concatenate(
            [
                total[:, half:].astype(BF),
                extra.astype(BF),
                jnp.zeros((width, 2 * half - 3 * width - SMALL), BF),
            ],
            axis=1,
        )
        first = where[slots + 1] == 0
        away[...] = jnp.where(first, right, left)
        kept[...] = jnp.where(first, left, right)


def finish_kernel(where, tok, small_t, grad_hidden, own_back, rows_back, out, *, gain_at):
    x = tok[...].astype(F32)
    scale = rms_scale(x)
    normed = x * scale
    grad = (own_back[...] + rows_back[...]) * small_t[gain_at : gain_at + 1, :]
    out[...] = (
        grad_hidden[...]
        + scale * (grad - normed * jnp.mean(grad * normed, axis=-1, keepdims=True))
    ).astype(BF)


def shared_kernel(where, total, other, qkv, out, router, gate, value, gain_one, gain_two, stream, *, columns, half, width, entries):
    kinds, mix_at, value_at, gain_one_at, gain_two_at, square_at = columns
    first = where[0] == 0
    a, b = total[...].astype(F32), other[...].astype(F32)
    left, right = jnp.where(first, a, b), jnp.where(first, b, a)
    rest = 3 * width - half
    qkv[:, :half] = left[:, :half]
    qkv[:, half:] = right[:, :rest]
    out[:, : width // 2] = left[:, half : half + width // 2]
    out[:, width // 2 :] = right[:, half : half + width // 2]
    rows = left.shape[0]

    def as_columns(block):
        spare = jnp.zeros((SMALL - rows, SMALL), F32)
        return jnp.concatenate([block, spare], axis=0).T[:, :rows]

    small = left[:, half + width // 2 : half + width // 2 + SMALL]
    turned_small = as_columns(small)
    turned_one = as_columns(right[:, rest : rest + SMALL])
    router[...] = turned_small[:kinds]
    gate[...] = turned_small[mix_at : mix_at + 2 * NCONST]
    value[...] = turned_small[value_at : value_at + NCONST]
    gain_two[...] = turned_small[gain_two_at : gain_two_at + 1]
    gain_one[...] = turned_one[gain_one_at : gain_one_at + 1]
    squares = small[:1, square_at : square_at + 4]
    hidden = squares[:, 0:1] + squares[:, 1:2]
    outputs = squares[:, 2:3] + squares[:, 3:4]
    stream[...] = jnp.sqrt(jnp.where(lanes((1, 2)) == 0, hidden, outputs) / entries)


def on_device(
    tokens,
    gain_one,
    qkv_weight,
    out_weight,
    gain_two,
    router_weight,
    const_gate,
    const_value,
    expert_gate_up,
    expert_down,
    gate_residual,
    routes,
    cotangent,
):
    parts = lax.axis_size("fsdp")
    groups = lax.axis_size("expert")
    me_fsdp = lax.axis_index("fsdp").astype(jnp.int32)
    me_expert = lax.axis_index("expert").astype(jnp.int32)
    minor, major, core = me_fsdp % 2, me_fsdp // 2, me_expert % 2
    packed = parts == 8 and groups == 4
    major_count = parts // 2
    tok = tokens[0]
    count, width = tok.shape
    length = groups * count
    pairs = width // PAIR
    kinds = router_weight.shape[1]
    mix_at, value_at = kinds, kinds + 2 * NCONST
    gain_one_at = value_at + NCONST
    gain_two_at = gain_one_at + 1
    square_at = gain_two_at + 1
    shard_rows = width // parts
    unit = FF // parts
    units = FF // 2
    fixed = lambda j, w: (0, 0)
    at_slot = lambda j, w: (j, 0)
    at_rank = lambda j, w: (w[j], 0)
    just_minor = jnp.stack([minor])

    small_rows = jnp.concatenate(
        [router_weight.T, const_gate.T, const_value.T, gain_one[None], gain_two[None]], axis=0
    )
    small_rows = jnp.pad(
        small_rows, ((0, 32 - small_rows.shape[0]), (0, SMALL - small_rows.shape[1]))
    )
    weight_args, order, across = (), [], None
    if packed:
        shared = shared_pack(qkv_weight, out_weight, small_rows)
        across = swap(tok, "expert", 2)
        away = call(
            blocks_kernel,
            shaped((8 * shard_rows, 256), BF),
            (just_minor, expert_gate_up[0]),
            name="blocks",
            micros=1,
        )
        arrived = swap(away, "fsdp", 1)
        part = call(
            pack_kernel,
            shaped((16 * shard_rows + 3 * 256, 256), BF),
            (just_minor, expert_gate_up[0], arrived, expert_down[0]),
            name="pack_expert",
            micros=1,
        )
        own_half, other_half, order, stage = shared_gather(
            shared, ((), (arrived, across), (part,))
        )
        weight_args = (own_half, other_half)
        part = after(part, *stage)
        far, near = along(part, FAR), along(part, NEAR)
    else:
        qkv_full = lax.all_gather(qkv_weight, "fsdp", axis=0, tiled=True)
        out_full = lax.all_gather(out_weight, "fsdp", axis=0, tiled=True)
        small = lax.all_gather(small_rows[:, :shard_rows], "fsdp", axis=1, tiled=True).T
        small = jnp.pad(small, ((0, 0), (0, SMALL - 32)))
        small_t = small.astype(F32).T[:32]
        weight_args = (qkv_full, small_t)
        halves = expert_gate_up[0].reshape(shard_rows, 2, major_count, 2, unit)
        away = lax.dynamic_index_in_dim(halves, 1 - minor, 3, False).reshape(shard_rows, FF)
        kept = lax.dynamic_index_in_dim(halves, minor, 3, False).reshape(shard_rows, FF)
        arrived = swap(away, "fsdp", 1)
        part = jnp.concatenate(
            [jnp.where(minor == 0, kept, arrived), jnp.where(minor == 0, arrived, kept)], axis=0
        )
        gather = functools.partial(
            lax.all_gather,
            axis_name="fsdp",
            axis=0,
            tiled=True,
            axis_index_groups=minor_groups(major_count),
        )
        gate_up_half, down_half = gather(part), gather(expert_down[0])
    tok_all, ranks = sequence_gather(tok, across)
    where = jnp.stack(
        [jnp.asarray(r, jnp.int32) for r in ranks] + [me_expert] + order + [core]
    )

    frequency = 10000.0 ** (-jnp.arange(HEAD // 2, dtype=F32) / (HEAD // 2))
    angles = jnp.arange(length, dtype=F32)[:, None] * frequency[None, :]
    cosine, sine = jnp.cos(angles), jnp.sin(angles)
    cosine = jnp.concatenate([cosine, cosine, cosine, cosine], axis=1)
    sine = jnp.concatenate([-sine, sine, -sine, sine], axis=1)

    half_columns = 2 * width + SMALL
    outs = [
        shaped((count, width), BF),
        shaped((length, width), BF),
        shaped((length, width), BF),
        shaped((length, width), BF),
    ]
    out_specs = [pl.BlockSpec((count, width), fixed)] + [pl.BlockSpec((count, width), at_rank)] * 3
    if packed:
        weight_specs = [pl.BlockSpec((width, half_columns), fixed)] * 2
        outs += [
            shaped((width, 3 * width), BF),
            shaped((width, width), BF),
            shaped((width, SMALL), BF),
            shaped((32, width), F32),
        ]
        out_specs += [pl.BlockSpec(o.shape, fixed) for o in outs[4:]]
    else:
        weight_specs = [pl.BlockSpec((width, 3 * width), fixed), pl.BlockSpec((32, width), fixed)]
    projected = call(
        functools.partial(project_kernel, slots=groups, gain_at=gain_one_at, placed=not packed),
        outs,
        (where, tok_all, cosine, sine) + weight_args,
        grid=(groups,),
        in_specs=[
            pl.BlockSpec((count, width), at_slot),
            pl.BlockSpec((count, PAIR), at_rank),
            pl.BlockSpec((count, PAIR), at_rank),
        ]
        + weight_specs,
        out_specs=out_specs,
        name="project",
        micros=10,
    )
    q, k_all, v_all, normed_all = projected[:4]
    if packed:
        qkv_full, out_full, small, small_t = projected[4:]
    head_rows = pl.BlockSpec((count, PAIR), lambda h, w: (0, h))
    head_keys = pl.BlockSpec((length, PAIR), lambda h, w: (0, h))
    head_log = pl.BlockSpec((1, 8, 2 * count), lambda h, w: (h, 0, 0))
    attended, log_total = call(
        functools.partial(attend_kernel, slots=groups),
        [shaped((count, width), BF), shaped((pairs, 8, 2 * count), F32)],
        (where, q, k_all, v_all),
        grid=(pairs,),
        in_specs=[head_rows, head_keys, head_keys],
        out_specs=[head_rows, head_log],
        name="attend",
        micros=12,
    )

    residual, route, cot = gate_residual[0], routes[0], cotangent[0]
    slots = jnp.stack([me_expert ^ j for j in range(groups)] + [me_fsdp, core])
    block = shaped((2 * MOST, width), BF)
    hidden, low_two, *sends = call(
        functools.partial(route_kernel, groups=groups, gain_at=gain_two_at),
        [shaped((count, width), F32), shaped((count, width), BF)] + [block] * groups,
        (slots, attended, out_full, tok, small, small_t, residual, route, cot),
        scratch=[pltpu.VMEM((groups * MOST, width), BF)] * 2,
        name="route",
        micros=5,
    )
    lower, upper = range(groups // 2), range(groups // 2, groups)
    received = [sends[0]] + [swap(sends[j], "expert", j) for j in range(1, groups)]
    other_low = swap(jnp.concatenate([received[j] for j in lower], axis=0), "fsdp", 1)
    high = jnp.concatenate([received[j] for j in upper], axis=0)
    other_high = swap(after(high, other_low), "fsdp", 1)
    if packed:
        far_held, near_held = lax.optimization_barrier((far, near, other_low))[:2]
        onward = along(far_held, OUTWARD)
        middle = along(after(part, far_held), MIDDLE)
        inner = jnp.logical_or(major == 1, major == 2).astype(jnp.int32)
        places = jnp.stack([major, major ^ 1, major ^ 2, major ^ 3, inner])
        weights = (part, near_held, far_held, middle, onward)
        grads = [shaped(part.shape, BF)] * 4
        room = [pltpu.VMEM((width, 2 * units), BF), pltpu.VMEM((units, width), BF)]
    else:
        places = just_minor
        weights = (gate_up_half, down_half)
        grads = [shaped((width, 2 * units), BF), shaped((units, width), BF)]
        room = []
    rows_total = 2 * groups * MOST
    results = call(
        functools.partial(expert_kernel, groups=groups, hidden_units=units, packed=packed),
        [shaped((groups * MOST, width), F32)] * 2 + [shaped((groups * MOST, width), BF)] * 2 + grads,
        (places,) + tuple(received) + (other_low, other_high) + weights,
        scratch=[pltpu.VMEM((rows_total, width), BF)] * 2
        + [pltpu.VMEM((rows_total, width), F32)] * 2
        + [pltpu.VMEM((rows_total, units), BF), pltpu.VMEM((rows_total, 2 * units), BF)]
        + room,
        name="expert",
        micros=18,
    )
    own_low, own_high, part_low, part_high = results[:4]
    grads = results[4:]
    high = (own_high + swap(part_high, "fsdp", 1).astype(F32)).astype(BF)
    low = (own_low + swap(part_low, "fsdp", 1).astype(F32)).astype(BF)
    backs = []
    for j in range(groups):
        whole = low if j in lower else high
        base = (j % (groups // 2)) * 2 * MOST
        piece = whole[base : base + 2 * MOST]
        backs.append(swap(piece, "expert", j) if j else piece)

    if packed:
        first = along(grads[3], INWARD)
        middle = along(grads[3], MIDDLE)
        near = along(after(grads[1], first), NEAR)
        sent = added(grads[2], first)
        split = sent.shape[0] // 2
        far_early = along(sent[:split], FAR)
        far_late = along(sent[split:], FAR)
        backs[0] = after(backs[0], sent, middle)
        away, kept, shard_down = call(
            sum_parts_kernel,
            [
                shaped((8 * shard_rows, 256), BF),
                shaped((8 * shard_rows, 256), F32),
                shaped((256, width), F32),
            ],
            (just_minor, grads[0], near, middle, far_early, far_late),
            name="sum_parts",
            micros=3,
        )
        shard_gate_up = call(
            unpack_kernel,
            shaped((shard_rows, 2 * FF), F32),
            (just_minor, kept, swap(away, "fsdp", 1)),
            name="unpack_expert",
            micros=2,
        )
    else:
        scatter = lambda v: lax.psum_scatter(
            v,
            "fsdp",
            scatter_dimension=0,
            tiled=True,
            axis_index_groups=minor_groups(major_count),
        ).astype(F32)
        shard_down = scatter(grads[1])
        part = scatter(grads[0]).reshape(2, shard_rows, FF)
        away = lax.dynamic_index_in_dim(part, 1 - minor, 0, False).astype(BF)
        kept = lax.dynamic_index_in_dim(part, minor, 0, False)
        arrived = swap(away, "fsdp", 1).astype(F32)
        first = jnp.where(minor == 0, kept, arrived).reshape(shard_rows, 2, major_count, 1, unit)
        second = jnp.where(minor == 0, arrived, kept).reshape(shard_rows, 2, major_count, 1, unit)
        shard_gate_up = jnp.concatenate([first, second], axis=3).reshape(shard_rows, 2 * FF)

    columns = (kinds, mix_at, value_at, gain_one_at, gain_two_at, square_at)
    out_half = width // 2 + SMALL
    outputs, grad_hidden, grad_att, out_away, out_kept, grad_residual = call(
        functools.partial(combine_kernel, groups=groups, columns=columns, shard_rows=shard_rows),
        [
            shaped((count, width), BF),
            shaped((count, width), F32),
            shaped((count, width), BF),
            shaped((width, out_half), BF),
            shaped((width, out_half), BF),
            shaped((count, kinds), BF),
        ],
        (slots,) + tuple(backs)
        + (hidden, low_two, cot, route, residual, small, small_t, out_full, attended),
        scratch=[pltpu.VMEM((groups * MOST, width), BF)] * 2,
        name="combine",
        micros=10,
    )
    if packed:
        out_both = across_cores(out_away, out_kept)
    own_rows = pl.BlockSpec((count, PAIR), lambda h, w: (w[groups], 0))
    all_rows = pl.BlockSpec((length, PAIR), lambda h, w: (0, 0))
    dq, dk, dv = call(
        functools.partial(attend_back_kernel, slots=groups),
        [shaped((count, width), BF), shaped((length, width), BF), shaped((length, width), BF)],
        (where, q, k_all, v_all, grad_att, log_total, cosine, sine, cosine, sine),
        grid=(pairs,),
        in_specs=[head_rows, head_keys, head_keys, head_rows, head_log, all_rows, all_rows, own_rows, own_rows],
        out_specs=[head_rows, head_keys, head_keys],
        name="attend_back",
        micros=15,
    )
    half = (3 * width // 2 + SMALL // 2 + 127) // 128 * 128
    if packed:
        dq = after(dq, out_both, near, far_early)
        out_away, out_kept = minor_halves(out_both, shard_rows)
        out_arrived = swap(out_away, "fsdp", 1)
    back_where = jnp.stack(
        [jnp.asarray(r, jnp.int32) for r in ranks] + [me_expert, core]
    )
    qkv_away, qkv_kept, rows_back, own_back = call(
        functools.partial(project_back_kernel, slots=groups, gain_at=gain_one_at),
        [
            shaped((width, half), BF),
            shaped((width, half), BF),
            shaped((length, width), BF),
            shaped((count, width), F32),
        ],
        (back_where, tok_all, normed_all, dq, dk, dv, qkv_full),
        grid=(groups,),
        in_specs=[
            pl.BlockSpec((count, width), at_slot),
            pl.BlockSpec((count, width), at_rank),
            pl.BlockSpec((count, width), fixed),
            pl.BlockSpec((count, width), at_rank),
            pl.BlockSpec((count, width), at_rank),
            pl.BlockSpec((width, 3 * width), fixed),
        ],
        out_specs=[
            pl.BlockSpec((width, half), fixed),
            pl.BlockSpec((width, half), fixed),
            pl.BlockSpec((count, width), at_rank),
            pl.BlockSpec((count, width), fixed),
        ],
        scratch=[pltpu.VMEM((width, 3 * width), F32), pltpu.VMEM((8, width), F32)],
        name="project_back",
        micros=11,
    )
    if packed:
        qkv_both = across_cores(after(qkv_away, out_arrived), qkv_kept)
        qkv_away, qkv_kept = minor_halves(qkv_both, shard_rows)
        parts_all = jnp.concatenate(
            [added(qkv_kept, swap(qkv_away, "fsdp", 1)), added(out_kept, out_arrived)], axis=2
        )
        total, other = across_rest(after(parts_all, far_late))
    else:
        first = core == 0
        mine = jnp.concatenate([qkv_kept, out_kept], axis=1)
        theirs = jnp.concatenate([qkv_away, out_away], axis=1)
        both = jnp.concatenate(
            [jnp.where(first, mine, theirs), jnp.where(first, theirs, mine)], axis=1
        )
        both = lax.psum_scatter(both, "fsdp", scatter_dimension=0, tiled=True)
        both = lax.psum(both, "expert")
        left, right = both[:, : half + out_half], both[:, half + out_half :]
        total, other = jnp.where(first, left, right), jnp.where(first, right, left)
    rows_sum = sequence_scatter_sum(rows_back, count)
    grad_tokens = call(
        functools.partial(finish_kernel, gain_at=gain_one_at),
        shaped((count, width), BF),
        (just_minor, tok, small_t, grad_hidden, own_back, rows_sum),
        name="finish",
        micros=3,
    )

    shared_grads = call(
        functools.partial(
            shared_kernel, columns=columns, half=half, width=width, entries=length * width
        ),
        [
            shaped((shard_rows, 3 * width), F32),
            shaped((shard_rows, width), F32),
            shaped((kinds, shard_rows), F32),
            shaped((2 * NCONST, shard_rows), F32),
            shaped((NCONST, shard_rows), F32),
            shaped((1, shard_rows), F32),
            shaped((1, shard_rows), F32),
            shaped((1, 2), F32),
        ],
        (jnp.stack([core]), total, other),
        name="shared_grads",
        micros=3,
    )
    grad_qkv, grad_out, grad_router, grad_gate, grad_value, grad_one, grad_two, stream = shared_grads
    return (
        outputs[None],
        grad_tokens[None],
        grad_one[0],
        grad_qkv,
        grad_out,
        grad_two[0],
        grad_router.T,
        grad_gate.T,
        grad_value.T,
        shard_gate_up[None],
        shard_down[None],
        grad_residual[None],
        stream,
    )


def solution(mesh):
    return jax.shard_map(
        on_device,
        mesh=mesh,
        in_specs=(
            P("fsdp", "expert", None),
            P("fsdp"),
            P("fsdp", None),
            P("fsdp", None),
            P("fsdp"),
            P("fsdp", None),
            P("fsdp", None),
            P("fsdp", None),
            P("expert", "fsdp", None),
            P("expert", "fsdp", None),
            P("fsdp", "expert", None),
            P("fsdp", "expert", None),
            P("fsdp", "expert", None),
        ),
        out_specs=(
            P("fsdp", "expert", None),
            P("fsdp", "expert", None),
            P("fsdp"),
            P("fsdp", None),
            P("fsdp", None),
            P("fsdp"),
            P("fsdp", None),
            P("fsdp", None),
            P("fsdp", None),
            P("expert", "fsdp", None),
            P("expert", "fsdp", None),
            P("fsdp", "expert", None),
            P("fsdp", None),
        ),
        check_vma=False,
    )
```

```python
import functools

import jax
import jax.numpy as jnp
from jax import lax
from jax.experimental import pallas as pl
from jax.experimental.pallas import tpu as pltpu
from jax.sharding import PartitionSpec as P

HEAD = 64
FF = 2048
NCONST = 2
MOST = 80
PAIR = 2 * HEAD
SMALL = 128

epsilon = 1e-06
masked_score = -1e30
BF = jnp.bfloat16
F32 = jnp.float32


def mm(a, b):
    return jnp.dot(a, b, preferred_element_type=F32)


def mm_nt(a, b):
    return lax.dot_general(a, b, (((1,), (1,)), ((), ())), preferred_element_type=F32)


def mm_tn(a, b):
    return lax.dot_general(a, b, (((0,), (0,)), ((), ())), preferred_element_type=F32)


def split_low(values):
    high = values.astype(BF)
    return high, (values - high.astype(F32)).astype(BF)


def lanes(shape):
    return lax.broadcasted_iota(jnp.int32, shape, len(shape) - 1)


def rows_of(shape):
    return lax.broadcasted_iota(jnp.int32, shape, 0)


def rms_scale(values):
    return lax.rsqrt(jnp.mean(values * values, axis=-1, keepdims=True) + epsilon)


def turned(values, cosine, sine):
    lane = lanes(values.shape) % HEAD
    swapped = jnp.where(
        lane < HEAD // 2,
        pltpu.roll(values, PAIR - HEAD // 2, 1),
        pltpu.roll(values, HEAD // 2, 1),
    )
    return values * cosine + swapped * sine


def call(kernel, outs, args, grid=(), in_specs=None, out_specs=None, scratch=(), scalars=1, name=None, micros=2):
    whole = pl.BlockSpec(memory_space=pltpu.VMEM)
    multi = isinstance(outs, (tuple, list))
    if in_specs is None:
        in_specs = [whole] * (len(args) - scalars)
    if out_specs is None:
        out_specs = [whole] * len(outs) if multi else whole
    return pl.pallas_call(
        kernel,
        out_shape=outs,
        grid_spec=pltpu.PrefetchScalarGridSpec(
            num_scalar_prefetch=scalars,
            grid=grid,
            in_specs=in_specs,
            out_specs=out_specs,
            scratch_shapes=list(scratch),
        ),
        compiler_params=pltpu.CompilerParams(vmem_limit_bytes=56 * 1024 * 1024),
        cost_estimate=pl.CostEstimate(
            flops=micros * 90_000_000, transcendentals=0, bytes_accessed=micros * 300_000
        ),
        name=name,
    )(*args)


def shaped(shape, dtype):
    return jax.ShapeDtypeStruct(shape, dtype)


def swap(values, axis, bits):
    size = lax.axis_size(axis)
    return lax.ppermute(values, axis, [(i, i ^ bits) for i in range(size)])


def along(values, pairs):
    return lax.ppermute(
        values, "fsdp", [(2 * i + b, 2 * j + b) for i, j in pairs for b in (0, 1)]
    )


def after(values, *others):
    return lax.optimization_barrier((values,) + tuple(others))[0]


FAR = ((0, 2), (2, 0), (1, 3), (3, 1))
NEAR = ((0, 1), (1, 0), (2, 3), (3, 2))
MIDDLE = ((1, 2), (2, 1))
OUTWARD = ((2, 3), (1, 0))
INWARD = ((0, 1), (3, 2))


def minor_groups(major):
    return [[2 * i + b for i in range(major)] for b in (0, 1)]


def blocks_kernel(where, gate_up, out):
    rows = gate_up.shape[0]
    for block in range(8):
        at = (2 * block + 1 - where[0]) * 256
        out[block * rows : (block + 1) * rows, :] = gate_up[:, pl.ds(pl.multiple_of(at, 256), 256)]


def pack_kernel(where, gate_up, arrived, out):
    rows = gate_up.shape[0]
    mine = where[0]
    for block in range(8):
        at = (2 * block + mine) * 256
        own = pl.ds(pl.multiple_of(2 * block * rows + mine * rows, rows), rows)
        other = pl.ds(pl.multiple_of(2 * block * rows + (1 - mine) * rows, rows), rows)
        out[own, :] = gate_up[:, pl.ds(pl.multiple_of(at, 256), 256)]
        out[other, :] = arrived[block * rows : (block + 1) * rows, :]


def sum_parts_kernel(where, a, b, c, early, late, away, kept, down):
    rows = away.shape[0] // 8
    mine = where[0]
    split = early.shape[0]

    def total(start, size, block):
        d, base = (early, 0) if block * 2 * rows < split else (late, split)
        source, shifted = pl.ds(start, size), pl.ds(start - base, size)
        return (
            a[source, :].astype(F32)
            + b[source, :].astype(F32)
            + c[source, :].astype(F32)
            + d[shifted, :].astype(F32)
        )

    for block in range(8):
        here = slice(block * rows, (block + 1) * rows)
        base = 2 * block * rows
        own = pl.multiple_of(base + mine * rows, rows)
        other = pl.multiple_of(base + (1 - mine) * rows, rows)
        away[here, :] = total(other, rows, block).astype(BF)
        kept[here, :] = total(own, rows, block)
    base = 16 * rows
    for block in range(3):
        down[:, block * 256 : (block + 1) * 256] = total(base + block * 256, 256, 8)


def unpack_kernel(where, kept, arrived, out):
    rows = out.shape[0]
    mine = where[0]
    for block in range(8):
        here = slice(block * rows, (block + 1) * rows)
        own = pl.ds(pl.multiple_of((2 * block + mine) * 256, 256), 256)
        other = pl.ds(pl.multiple_of((2 * block + 1 - mine) * 256, 256), 256)
        out[:, own] = kept[here, :]
        out[:, other] = arrived[here, :].astype(F32)


def shared_pack(qkv, out, small_rows):
    core = lax.axis_index("expert") % 2
    half_qkv, half_out = qkv.shape[1] // 2, out.shape[1] // 2
    rows = qkv.shape[0]

    def kernel(where, qkv_ref, out_ref, small_ref, packed):
        packed[:, :half_qkv] = qkv_ref[:, pl.ds(pl.multiple_of(where[0] * half_qkv, 128), half_qkv)]
        packed[:, half_qkv : half_qkv + half_out] = out_ref[
            :, pl.ds(pl.multiple_of(where[0] * half_out, 128), half_out)
        ]
        packed[:32, half_qkv + half_out :] = small_ref[...]
        packed[32:, half_qkv + half_out :] = jnp.zeros((rows - 32, SMALL), BF)

    return call(
        kernel,
        shaped((rows, half_qkv + half_out + SMALL), BF),
        (jnp.stack([core]).astype(jnp.int32), qkv, out, small_rows),
        name="pack_shared",
        micros=1,
    )


def shared_gather(major, early, late):
    me = lax.axis_index("fsdp")
    minor = [swap(major[0], "fsdp", 1)]
    for j in (1, 2, 3):
        minor.append(swap(after(major[j], *early[j - 1]), "fsdp", 1))
    slots = [2 * j for j in range(4)] + [2 * j + 1 for j in range(4)]
    own = after(jnp.concatenate(major + minor, axis=0), *late)
    return own, swap(own, "expert", 1), [me ^ s for s in slots]


def added(kept, arrived):
    return (kept.astype(F32) + arrived.astype(F32)).astype(BF)


def across_rest(parts, rows):
    total = parts[:rows].astype(F32)
    for j in (1, 2, 3):
        total += swap(parts[j * rows : (j + 1) * rows], "fsdp", 2 * j).astype(F32)
    total = total.astype(BF)
    total = added(total, swap(total, "expert", 2))
    return total, swap(total, "expert", 1)


def sequence_gather(values, across):
    size = lax.axis_size("expert")
    me = lax.axis_index("expert")
    if size != 4:
        every = lax.all_gather(values, "expert", axis=0, tiled=True)
        middle = every.shape[0] // 2
        return every[:middle], every[middle:], list(range(size))
    pair = jnp.concatenate([values, across], axis=0)
    return pair, swap(pair, "expert", 1), [me, me ^ 2, me ^ 1, me ^ 3]


def exchange(sends):
    half = len(sends) // 2
    received = [swap(v, "expert", j) if j else v for j, v in enumerate(sends)]
    low = swap(jnp.concatenate(received[:half], axis=0), "fsdp", 1)
    high = swap(after(jnp.concatenate(received[half:], axis=0), low), "fsdp", 1)
    return received, low, high


def exchange_back(low, high, size):
    rows = 2 * low.shape[0] // size
    if size == 4:
        upper = swap(high, "expert", 2)
        joined = swap(jnp.concatenate([low[rows:], upper[rows:]], axis=0), "expert", 1)
        return [low[:rows], joined[:rows], upper[:rows], joined[rows:]]
    pieces = [w[i : i + rows] for w in (low, high) for i in range(0, w.shape[0], rows)]
    return [swap(piece, "expert", j) if j else piece for j, piece in enumerate(pieces)]


def sequence_scatter_sum(full, rows):
    size = lax.axis_size("expert")
    me = lax.axis_index("expert")
    if size != 4:
        return lax.psum_scatter(full, "expert", scatter_dimension=0, tiled=True).astype(F32)

    def block(bits):
        return lax.dynamic_slice_in_dim(full, (me ^ bits) * rows, rows, 0)

    away = jnp.concatenate([block(1), block(3)], axis=0)
    kept = jnp.concatenate([block(0), block(2)], axis=0)
    both = kept.astype(F32) + swap(away, "expert", 1).astype(F32)
    return both[:rows] + swap(both[rows:].astype(BF), "expert", 2).astype(F32)


def project_kernel(where, *refs, slots, gain_at, placed):
    if placed:
        tok_a, tok_b, cosine, sine, weight, small_t, q, k, v, normed = refs
    else:
        tok_a, tok_b, cosine, sine, own_ref, other_ref = refs[:6]
        q, k, v, normed, weight, out_ref, small_ref, small_t = refs[6:]
    step = pl.program_id(0)
    rank = where[step]
    own = where[slots]
    width = tok_a.shape[1]

    if not placed:

        @pl.when(step == 0)
        def _():
            first = where[slots + 9] == 0
            rows = width // 8
            half_qkv, half_out = 3 * width // 2, width // 2
            for index in range(8):
                source = pl.ds(index * rows, rows)
                target = pl.ds(pl.multiple_of(where[slots + 1 + index] * rows, rows), rows)
                a, b = own_ref[source, :], other_ref[source, :]
                left = jnp.where(first, a, b)
                right = jnp.where(first, b, a)
                weight[target, :half_qkv] = left[:, :half_qkv]
                weight[target, half_qkv:] = right[:, :half_qkv]
                out_ref[target, :half_out] = left[:, half_qkv : half_qkv + half_out]
                out_ref[target, half_out:] = right[:, half_qkv : half_qkv + half_out]
                of_rows = jnp.zeros((SMALL, SMALL), F32)
                of_rows = jnp.concatenate(
                    [a[:32, half_qkv + half_out :].astype(F32), of_rows[32:]], axis=0
                ).T
                small_ref[target, :] = of_rows[:rows].astype(BF)
            small_t[...] = small_ref[...].astype(F32).T[:32]

    @pl.when(rank > own)
    def _():
        k[...] = jnp.zeros_like(k)
        v[...] = jnp.zeros_like(v)
        normed[...] = jnp.zeros_like(normed)

    @pl.when(rank <= own)
    def _():
        x = jnp.where(step < slots // 2, tok_a[...], tok_b[...]).astype(F32)
        wide = (x * rms_scale(x)) * small_t[gain_at : gain_at + 1, :]
        low = wide.astype(BF)
        normed[...] = low.T
        cos, sin = cosine[...], sine[...]
        keys = mm(low, weight[:, width : 2 * width])
        for at in range(0, width, PAIR):
            k[:, at : at + PAIR] = turned(keys[:, at : at + PAIR], cos, sin).astype(BF)
        v[...] = mm(low, weight[:, 2 * width :]).astype(BF)

        @pl.when(rank == own)
        def _():
            queries = mm(low, weight[:, :width])
            for at in range(0, width, PAIR):
                q[:, at : at + PAIR] = turned(queries[:, at : at + PAIR], cos, sin).astype(BF)


def stacked_heads(values, scale=None):
    lane = lanes(values.shape)
    if scale is not None:
        values = values * jnp.asarray(scale, values.dtype)
    zero = jnp.zeros_like(values)
    return jnp.concatenate(
        [jnp.where(lane < HEAD, values, zero), jnp.where(lane < HEAD, zero, values)], axis=0
    )


def visible_keys(own, keys, count):
    key = lax.broadcasted_iota(jnp.int32, (keys, 2 * count), 0)
    query = lax.broadcasted_iota(jnp.int32, (keys, 2 * count), 1) % count
    return key <= query + own * count


def attend_kernel(where, q, k, v, attended, log_total, *, slots):
    own = where[slots]
    count, keys = q.shape[0], k.shape[0]
    query = stacked_heads(q[...], HEAD ** (-0.5))
    scores = mm_nt(k[...], query)
    scores = jnp.where(visible_keys(own, keys, count), scores, masked_score)
    top = jnp.max(scores, axis=0, keepdims=True)
    weights = jnp.exp(scores - top)
    total = jnp.sum(weights, axis=0, keepdims=True)
    log_total[...] = jnp.broadcast_to(top + jnp.log(total), (8, 2 * count))[None]
    weights = (weights * (1.0 / total)).astype(BF)
    both = mm_tn(weights, v[...])
    lane = lanes((count, PAIR))
    attended[...] = jnp.where(lane < HEAD, both[:count], both[count:]).astype(BF)


def attend_back_kernel(where, q, k, v, grad_att, log_total, cosine, sine, normed, normed_own, dq, dk, dv, away, kept, sums, *, slots, packed):
    step = pl.program_id(0)
    own = where[slots]
    count, keys = q.shape[0], k.shape[0]
    query = stacked_heads(q[...], HEAD ** (-0.5))
    grad_rows = stacked_heads(grad_att[...])
    key_rows = k[...]
    scores = mm_nt(key_rows, query)
    weights = jnp.where(
        visible_keys(own, keys, count), jnp.exp(scores - log_total[0, :1, :]), 0.0
    )
    grad_weights = mm_nt(v[...], grad_rows)
    delta = jnp.sum(weights * grad_weights, axis=0, keepdims=True)
    grad_scores = (weights * (grad_weights - delta)).astype(BF)
    grad_v = mm(weights.astype(BF), grad_rows).astype(BF)
    dv[...] = grad_v
    grad_k = turned(mm(grad_scores, query), cosine[...], -sine[...]).astype(BF)
    dk[...] = grad_k
    both = mm_tn(grad_scores, key_rows)
    lane = lanes((count, PAIR))
    grad_q = jnp.where(lane < HEAD, both[:count], both[count:]) * HEAD ** (-0.5)
    mine = pl.ds(pl.multiple_of(own * count, count), count)
    grad_q = turned(grad_q, cosine[mine, :], -sine[mine, :]).astype(BF)
    dq[...] = grad_q
    of_keys = mm(normed[...], jnp.concatenate([grad_k, grad_v], axis=1))
    of_queries = mm(normed_own[...], grad_q)
    steps = kept.shape[1] // (3 * PAIR)
    for index in range(steps):

        @pl.when(step == index)
        def _():
            for part, values in enumerate((of_queries, of_keys[:, :PAIR], of_keys[:, PAIR:])):
                at = (part * steps + index) * PAIR
                sums[:, at : at + PAIR] = values.astype(BF)

    @pl.when(step == steps - 1)
    def _():
        if packed:
            split_rows(where, slots + 1, sums, away, kept)
        else:
            kept[...] = sums[...]
            away[...] = jnp.zeros_like(away)


def split_rows(where, at, values, away, kept):
    core = where[at + 8]
    rows = values.shape[0] // 16
    for index in range(8):
        target = slice(index * rows, (index + 1) * rows)
        base = where[at + index] * 2
        kept[target, :] = values[pl.ds(pl.multiple_of((base + core) * rows, rows), rows), :]
        away[target, :] = values[pl.ds(pl.multiple_of((base + 1 - core) * rows, rows), rows), :]


def routing(routes, resid, logits, groups):
    count = routes.shape[0]
    lane = lanes((count, SMALL))
    kind = lanes(resid.shape)
    hot, picked = [], []
    for choice in range(2):
        route = routes[:, choice : choice + 1]
        hot.append(lane == route)
        picked.append(
            jnp.sum(jnp.where(hot[choice], logits, 0.0), axis=-1, keepdims=True)
            + jnp.sum(jnp.where(kind == route, resid, 0.0), axis=-1, keepdims=True)
        )
    top = jnp.maximum(picked[0], picked[1])
    first, second = jnp.exp(picked[0] - top), jnp.exp(picked[1] - top)
    gates = [first / (first + second), second / (first + second)]
    named = jnp.logical_or(hot[0], hot[1]).astype(BF)
    earlier = (lanes((count, count)) < rows_of((count, count))).astype(BF)
    place = mm(earlier, named)
    dispatch = []
    column = lanes((count, groups * MOST))
    for choice in range(2):
        route = routes[:, choice : choice + 1]
        slot = jnp.sum(jnp.where(hot[choice], place, 0.0), axis=-1, keepdims=True)
        target = jnp.where(route < groups, route * MOST + slot.astype(jnp.int32), -1)
        dispatch.append((column == target).astype(BF))
    return gates, hot, dispatch


def route_kernel(where, att, out_weight, tok, small, small_t, resid, routes, cot, hidden_ref, low_ref, *rest, groups, gain_at):
    sends = rest[:groups]
    rows_x, rows_g = rest[groups], rest[groups + 1]
    hidden = tok[...].astype(F32) + mm(att[...], out_weight[...])
    hidden_ref[...] = hidden
    low = ((hidden * rms_scale(hidden)) * small_t[gain_at : gain_at + 1, :]).astype(BF)
    low_ref[...] = low
    logits = mm(low, small[...])
    gates, _, dispatch = routing(routes[...], resid[...].astype(F32), logits, groups)
    grad = cot[...].astype(F32)
    rows_x[...] = mm_tn(dispatch[0] + dispatch[1], low).astype(BF)
    rows_g[...] = (
        mm_tn(dispatch[0], (gates[0] * grad).astype(BF))
        + mm_tn(dispatch[1], (gates[1] * grad).astype(BF))
    ).astype(BF)
    for slot in range(groups):
        source = pl.ds(pl.multiple_of(where[slot] * MOST, MOST), MOST)
        sends[slot][:MOST, :] = rows_x[source, :]
        sends[slot][MOST:, :] = rows_g[source, :]


def expert_kernel(where, *refs, groups, hidden_units, packed):
    refs = list(refs)

    def take(amount):
        taken = refs[:amount]
        del refs[:amount]
        return taken

    received = take(groups) + take(2)
    if packed:
        unit_parts, down_parts = take(5), take(5)
    else:
        gate_up, down = take(2)
    own_out, other_out = take(2), take(2)
    if packed:
        messages = take(4)
    else:
        grad_gate_up, grad_down = take(2)
    rows, grads, out_rows, back_rows, acts, grad_units = take(6)
    if packed:
        gate_up, down = take(2)
    width = rows.shape[1]
    total = 2 * groups * MOST
    index = 0
    for ref in received:
        for base in range(0, ref.shape[0], 2 * MOST):
            target = slice(index * MOST, (index + 1) * MOST)
            rows[target, :] = ref[base : base + MOST, :]
            grads[target, :] = ref[base + MOST : base + 2 * MOST, :]
            index += 1
    if packed:
        part = width // 4

        def place(slot, ref, down_ref):
            target = pl.ds(pl.multiple_of(where[slot] * part, part), part)
            for block in range(8):
                gate_up[target, block * 256 : (block + 1) * 256] = ref[
                    block * part : (block + 1) * part, :
                ]
            down[pl.ds(pl.multiple_of(where[slot] * 256, 256), 256), :] = down_ref[...]

        for slot in range(3):
            place(slot, unit_parts[slot], down_parts[slot])

        @pl.when(where[4] == 1)
        def _():
            place(3, unit_parts[3], down_parts[3])

        @pl.when(where[4] == 0)
        def _():
            place(3, unit_parts[4], down_parts[4])

    x, g = rows[...], grads[...]
    chunk = 256
    for at in range(0, hidden_units, chunk):
        gate_w = gate_up[:, at : at + chunk]
        up_w = gate_up[:, hidden_units + at : hidden_units + at + chunk]
        down_w = down[at : at + chunk, :]
        gate, up = mm(x, gate_w), mm(x, up_w)
        sig = 1.0 / (1.0 + jnp.exp(-gate))
        silu = gate * sig
        act = (silu * up).astype(BF)
        acts[:, at : at + chunk] = act
        grad_act = mm_nt(g, down_w)
        grad_gate = (grad_act * up * sig * (1.0 + gate * (1.0 - sig))).astype(BF)
        grad_up = (grad_act * silu).astype(BF)
        grad_units[:, at : at + chunk] = grad_gate
        grad_units[:, hidden_units + at : hidden_units + at + chunk] = grad_up
        part_out = mm(act, down_w)
        part_back = mm_nt(grad_gate, gate_w) + mm_nt(grad_up, up_w)
        if at == 0:
            out_rows[...] = part_out
            back_rows[...] = part_back
        else:
            out_rows[...] += part_out
            back_rows[...] += part_back
    index = 0
    for ref in own_out + other_out:
        for base in range(0, ref.shape[0], 2 * MOST):
            source = slice(index * MOST, (index + 1) * MOST)
            ref[base : base + MOST, :] = out_rows[source, :].astype(ref.dtype)
            ref[base + MOST : base + 2 * MOST, :] = back_rows[source, :].astype(ref.dtype)
            index += 1
    if not packed:
        grad_gate_up[...] = mm_tn(x, grad_units[...]).astype(BF)
        grad_down[...] = mm_tn(acts[...], g).astype(BF)
        return
    part = width // 4
    for block in range(8):
        of_block = mm_tn(x, grad_units[:, block * 256 : (block + 1) * 256])
        gate_up[:, block * 256 : (block + 1) * 256] = of_block.astype(BF)
    for slot, ref in enumerate(messages):
        source = pl.ds(pl.multiple_of(where[slot] * part, part), part)
        for block in range(8):
            ref[block * part : (block + 1) * part, :] = gate_up[
                source, block * 256 : (block + 1) * 256
            ]
        mine = acts[:, pl.ds(pl.multiple_of(where[slot] * 256, 256), 256)]
        of_down = mm_tn(mine, g).astype(BF)
        for block in range(3):
            base = 8 * part + block * 256
            ref[base : base + 256, :] = of_down[:, block * 256 : (block + 1) * 256]


def combine_kernel(where, *refs, groups, columns, shard_rows, packed):
    backs = refs[:groups]
    (hidden_ref, low_ref, cot, routes, resid, small, small_t, out_weight, att,
     out_ref, grad_hidden_ref, grad_att_ref, grad_away, grad_kept, grad_resid,
     rows_y, rows_d, sums) = refs[groups:]
    kinds, mix_at, value_at, gain_two_at, square_at = columns
    for slot in range(groups):
        target = pl.ds(pl.multiple_of(where[slot] * MOST, MOST), MOST)
        rows_y[target, :] = backs[slot][:MOST, :]
        rows_d[target, :] = backs[slot][MOST:, :]
    hidden, low = hidden_ref[...], low_ref[...]
    count = low.shape[0]
    normed_input = low.astype(F32)
    grad_low_type = cot[...]
    grad = grad_low_type.astype(F32)
    logits = mm(low, small[...])
    grad_small_dot = mm(grad_low_type, small[...])
    route = routes[...]
    gates, hot, dispatch = routing(route, resid[...].astype(F32), logits, groups)
    returned = [mm(dispatch[c], rows_y[...]) for c in range(2)]
    grad_back = mm(dispatch[0] + dispatch[1], rows_d[...])
    grad_dot = jnp.sum(grad * normed_input, axis=-1, keepdims=True)
    is_copy = [(route[:, c : c + 1] == groups + 1).astype(F32) for c in range(2)]
    grad_gates = [
        jnp.sum(grad * returned[c], axis=-1, keepdims=True) + is_copy[c] * grad_dot
        for c in range(2)
    ]
    direct = gates[0] * is_copy[0] + gates[1] * is_copy[1]
    mixture = gates[0] * returned[0] + gates[1] * returned[1]
    lane = lanes((count, SMALL))
    grad_logits = jnp.zeros((count, SMALL), F32)
    value_weights = jnp.zeros((count, SMALL), F32)
    for const in range(NCONST):
        first = logits[:, mix_at + 2 * const : mix_at + 2 * const + 1]
        second = logits[:, mix_at + 2 * const + 1 : mix_at + 2 * const + 2]
        top = jnp.maximum(first, second)
        first, second = jnp.exp(first - top), jnp.exp(second - top)
        mix = [first / (first + second), second / (first + second)]
        value_dot = grad_small_dot[:, value_at + const : value_at + const + 1]
        named = [(route[:, c : c + 1] == groups + 2 + const).astype(F32) for c in range(2)]
        for c in range(2):
            grad_gates[c] += named[c] * (mix[0] * grad_dot + mix[1] * value_dot)
        weight = gates[0] * named[0] + gates[1] * named[1]
        direct += weight * mix[0]
        of_value = weight * mix[1]
        mixture += of_value * small_t[value_at + const : value_at + const + 1, :]
        value_weights = jnp.where(lane == value_at + const, of_value, value_weights)
        grad_mix = [weight * grad_dot, weight * value_dot]
        common = mix[0] * grad_mix[0] + mix[1] * grad_mix[1]
        for c in range(2):
            grad_logits = jnp.where(
                lane == mix_at + 2 * const + c, mix[c] * (grad_mix[c] - common), grad_logits
            )
    outputs = hidden + mixture + direct * normed_input
    out_ref[...] = outputs.astype(BF)
    common = gates[0] * grad_gates[0] + gates[1] * grad_gates[1]
    for c in range(2):
        grad_logits = jnp.where(hot[c], gates[c] * (grad_gates[c] - common), grad_logits)
    grad_resid[...] = grad_logits[:, :kinds].astype(BF)
    high, rest = split_low(grad_logits)
    weights = small[...]
    grad_low = grad_back + direct * grad + mm_nt(high, weights) + mm_nt(rest, weights)
    scale = rms_scale(hidden)
    normed = hidden * scale
    of_gain = split_low(grad_low * normed)
    ones = (lane == gain_two_at).astype(BF)
    value_high, value_rest = split_low(value_weights)
    summed = (
        mm_tn(low, high)
        + mm_tn(low, rest)
        + mm_tn(grad_low_type, value_high)
        + mm_tn(grad_low_type, value_rest)
        + mm_tn(of_gain[0], ones)
        + mm_tn(of_gain[1], ones)
    )
    column, row = lanes(summed.shape), rows_of(summed.shape)
    mine = row // shard_rows == where[groups]
    for index, total in enumerate((jnp.sum(hidden * hidden), jnp.sum(outputs * outputs))):
        for part, value in enumerate(split_low(jnp.full((1, 1), total, F32))):
            spot = jnp.logical_and(mine, column == square_at + 2 * index + part)
            summed = jnp.where(spot, value.astype(F32), summed)
    grad_normed = grad_low * small_t[gain_two_at : gain_two_at + 1, :]
    grad_hidden = grad + scale * (
        grad_normed - normed * jnp.mean(grad_normed * normed, axis=-1, keepdims=True)
    )
    grad_hidden_ref[...] = grad_hidden
    branch = grad_hidden.astype(BF)
    grad_att_ref[...] = mm_nt(branch, out_weight[...]).astype(BF)
    width = branch.shape[1]
    sums[:, :width] = mm_tn(att[...], branch).astype(BF)
    sums[:, width:] = summed.astype(BF)
    if packed:
        split_rows(where, groups + 1, sums, grad_away, grad_kept)
    else:
        grad_kept[...] = sums[...]
        grad_away[...] = jnp.zeros_like(grad_away)


def project_back_kernel(where, *refs, slots):
    queries, keys, values = refs[0:2], refs[2:4], refs[4:6]
    weight, rows_back, own_back = refs[6:]
    rank = where[pl.program_id(0)]
    own = where[slots]
    half = keys[0].shape[1]
    width = 2 * half

    def through(parts, base):
        result = mm_nt(parts[0][...], weight[:, base : base + half])
        return result + mm_nt(parts[1][...], weight[:, base + half : base + width])

    @pl.when(rank > own)
    def _():
        rows_back[...] = jnp.zeros_like(rows_back)

    @pl.when(rank <= own)
    def _():
        rows_back[...] = (through(keys, width) + through(values, 2 * width)).astype(BF)

        @pl.when(rank == own)
        def _():
            own_back[...] = through(queries, 0)


def finish_kernel(where, tok, small_t, grad_hidden, own_back, rows_back, out, *, gain_at):
    x = tok[...].astype(F32)
    scale = rms_scale(x)
    normed = x * scale
    grad = (own_back[...] + rows_back[...]) * small_t[gain_at : gain_at + 1, :]
    out[...] = (
        grad_hidden[...]
        + scale * (grad - normed * jnp.mean(grad * normed, axis=-1, keepdims=True))
    ).astype(BF)


def shared_kernel(where, total, other, weight, gain, qkv, out, router, gate, value, gain_one, gain_two, stream, *, columns, width, entries, packed):
    kinds, mix_at, value_at, gain_two_at, square_at = columns
    first = where[0] == 0
    a, b = total[...].astype(F32), other[...].astype(F32)
    values = a
    if packed:
        values = jnp.concatenate([jnp.where(first, a, b), jnp.where(first, b, a)], axis=0)
    half = width // 2
    for part in range(3):
        for side in range(2):
            at = (3 * side + part) * half
            to = part * width + side * half
            qkv[:, to : to + half] = values[:, at : at + half]
    out[...] = values[:, 3 * width : 4 * width]
    rows = values.shape[0]

    def as_columns(block):
        spare = jnp.zeros((SMALL - rows, SMALL), F32)
        return jnp.concatenate([block, spare], axis=0).T[:, :rows]

    small = values[:, 4 * width :]
    turned_small = as_columns(small)
    router[...] = turned_small[:kinds]
    gate[...] = turned_small[mix_at : mix_at + 2 * NCONST]
    value[...] = turned_small[value_at : value_at + NCONST]
    gain_two[...] = turned_small[gain_two_at : gain_two_at + 1]
    of_gain = jnp.sum(qkv[...] * weight[...].astype(F32), axis=-1, keepdims=True)
    gain_one[...] = as_columns(jnp.broadcast_to(of_gain, (rows, SMALL)))[:1] / gain[...].astype(F32)
    squares = small[:1, square_at : square_at + 4]
    hidden = squares[:, 0:1] + squares[:, 1:2]
    outputs = squares[:, 2:3] + squares[:, 3:4]
    stream[...] = jnp.sqrt(jnp.where(lanes((1, 2)) == 0, hidden, outputs) / entries)


def on_device(
    tokens,
    gain_one,
    qkv_weight,
    out_weight,
    gain_two,
    router_weight,
    const_gate,
    const_value,
    expert_gate_up,
    expert_down,
    gate_residual,
    routes,
    cotangent,
):
    parts = lax.axis_size("fsdp")
    groups = lax.axis_size("expert")
    me_fsdp = lax.axis_index("fsdp").astype(jnp.int32)
    me_expert = lax.axis_index("expert").astype(jnp.int32)
    minor, major, core = me_fsdp % 2, me_fsdp // 2, me_expert % 2
    packed = parts == 8 and groups == 4
    major_count = parts // 2
    tok = tokens[0]
    count, width = tok.shape
    length = groups * count
    pairs = width // PAIR
    kinds = router_weight.shape[1]
    mix_at, value_at = kinds, kinds + 2 * NCONST
    gain_one_at = value_at + NCONST
    gain_two_at = gain_one_at + 1
    square_at = gain_two_at + 1
    shard_rows = width // parts
    unit = FF // parts
    units = FF // 2
    fixed = lambda j, w: (0, 0)
    at_slot = lambda j, w: (j, 0)
    at_rank = lambda j, w: (w[j], 0)
    just_minor = jnp.stack([minor])

    small_rows = jnp.concatenate(
        [router_weight.T, const_gate.T, const_value.T, gain_one[None], gain_two[None]], axis=0
    )
    small_rows = jnp.pad(
        small_rows, ((0, 32 - small_rows.shape[0]), (0, SMALL - small_rows.shape[1]))
    )
    frequency = 10000.0 ** (-jnp.arange(HEAD // 2, dtype=F32) / (HEAD // 2))
    angles = jnp.arange(length, dtype=F32)[:, None] * frequency[None, :]
    cosine, sine = jnp.cos(angles), jnp.sin(angles)
    cosine = jnp.concatenate([cosine, cosine, cosine, cosine], axis=1)
    sine = jnp.concatenate([-sine, sine, -sine, sine], axis=1)

    weight_args, order, across = (), [], None
    if packed:
        shared = shared_pack(qkv_weight, out_weight, small_rows)
        across = swap(tok, "expert", 2)
        away = call(
            blocks_kernel,
            shaped((8 * shard_rows, 256), BF),
            (just_minor, expert_gate_up[0]),
            name="blocks",
            micros=1,
        )
        arrived = swap(away, "fsdp", 1)
        part = call(
            pack_kernel,
            shaped((16 * shard_rows, 256), BF),
            (just_minor, expert_gate_up[0], arrived),
            name="pack_expert",
            micros=1,
        )
        down = expert_down[0]
        tok_a, tok_b, ranks = sequence_gather(tok, across)
        stage = [shared] + [swap(shared, "fsdp", 2 * j) for j in (1, 2, 3)]
        down_near = along(after(down, stage[1]), NEAR)
        down_far = along(after(down, stage[1]), FAR)
        own_half, other_half, order = shared_gather(
            stage, ((), (arrived, across), (part, cosine, sine, tok_b)), (down_near, down_far)
        )
        down_onward = along(down_far, OUTWARD)
        down_middle = along(after(down, down_far), MIDDLE)
        weight_args = (own_half, other_half)
        part = after(part, *stage[1:])
        far, near = along(part, FAR), along(part, NEAR)
    else:
        qkv_full = lax.all_gather(qkv_weight, "fsdp", axis=0, tiled=True)
        out_full = lax.all_gather(out_weight, "fsdp", axis=0, tiled=True)
        small = lax.all_gather(small_rows[:, :shard_rows], "fsdp", axis=1, tiled=True).T
        small = jnp.pad(small, ((0, 0), (0, SMALL - 32)))
        small_t = small.astype(F32).T[:32]
        weight_args = (qkv_full, small_t)
        halves = expert_gate_up[0].reshape(shard_rows, 2, major_count, 2, unit)
        away = lax.dynamic_index_in_dim(halves, 1 - minor, 3, False).reshape(shard_rows, FF)
        kept = lax.dynamic_index_in_dim(halves, minor, 3, False).reshape(shard_rows, FF)
        arrived = swap(away, "fsdp", 1)
        part = jnp.concatenate(
            [jnp.where(minor == 0, kept, arrived), jnp.where(minor == 0, arrived, kept)], axis=0
        )
        gather = functools.partial(
            lax.all_gather,
            axis_name="fsdp",
            axis=0,
            tiled=True,
            axis_index_groups=minor_groups(major_count),
        )
        gate_up_half, down_half = gather(part), gather(expert_down[0])
        tok_a, tok_b, ranks = sequence_gather(tok, across)
    where = jnp.stack(
        [jnp.asarray(r, jnp.int32) for r in ranks] + [me_expert] + order + [core]
    )

    half_columns = 2 * width + SMALL
    outs = [
        shaped((count, width), BF),
        shaped((length, width), BF),
        shaped((length, width), BF),
        shaped((width, length), BF),
    ]
    out_specs = [
        pl.BlockSpec((count, width), fixed),
        pl.BlockSpec((count, width), at_rank),
        pl.BlockSpec((count, width), at_rank),
        pl.BlockSpec((width, count), lambda j, w: (0, w[j])),
    ]
    if packed:
        weight_specs = [pl.BlockSpec((width, half_columns), fixed)] * 2
        outs += [
            shaped((width, 3 * width), BF),
            shaped((width, width), BF),
            shaped((width, SMALL), BF),
            shaped((32, width), F32),
        ]
        out_specs += [pl.BlockSpec(o.shape, fixed) for o in outs[4:]]
    else:
        weight_specs = [pl.BlockSpec((width, 3 * width), fixed), pl.BlockSpec((32, width), fixed)]
    projected = call(
        functools.partial(project_kernel, slots=groups, gain_at=gain_one_at, placed=not packed),
        outs,
        (where, tok_a, tok_b, cosine, sine) + weight_args,
        grid=(groups,),
        in_specs=[
            pl.BlockSpec((count, width), lambda j, w: (jnp.minimum(j, groups // 2 - 1), 0)),
            pl.BlockSpec((count, width), lambda j, w: (jnp.maximum(j - groups // 2, 0), 0)),
            pl.BlockSpec((count, PAIR), at_rank),
            pl.BlockSpec((count, PAIR), at_rank),
        ]
        + weight_specs,
        out_specs=out_specs,
        name="project",
        micros=10,
    )
    q, k_all, v_all, normed = projected[:4]
    if packed:
        qkv_full, out_full, small, small_t = projected[4:]
    head_rows = pl.BlockSpec((count, PAIR), lambda h, w: (0, h))
    head_keys = pl.BlockSpec((length, PAIR), lambda h, w: (0, h))
    head_log = pl.BlockSpec((1, 8, 2 * count), lambda h, w: (h, 0, 0))
    attended, log_total = call(
        functools.partial(attend_kernel, slots=groups),
        [shaped((count, width), BF), shaped((pairs, 8, 2 * count), F32)],
        (where, q, k_all, v_all),
        grid=(pairs,),
        in_specs=[head_rows, head_keys, head_keys],
        out_specs=[head_rows, head_log],
        name="attend",
        micros=12,
    )

    residual, route, cot = gate_residual[0], routes[0], cotangent[0]
    owners = [me_fsdp ^ (2 * j + i) for i in (0, 1) for j in range(4)] + [core]
    slots = jnp.stack([me_expert ^ j for j in range(groups)] + [me_fsdp] + owners)
    block = shaped((2 * MOST, width), BF)
    hidden, low_two, *sends = call(
        functools.partial(route_kernel, groups=groups, gain_at=gain_two_at),
        [shaped((count, width), F32), shaped((count, width), BF)] + [block] * groups,
        (slots, attended, out_full, tok, small, small_t, residual, route, cot),
        scratch=[pltpu.VMEM((groups * MOST, width), BF)] * 2,
        name="route",
        micros=5,
    )
    received, other_low, other_high = exchange(sends)
    if packed:
        far, near = lax.optimization_barrier(
            (far, near, low_two, down_onward, down_middle)
        )[:2]
        onward = along(far, OUTWARD)
        middle = along(after(part, far), MIDDLE)
        inner = jnp.logical_or(major == 1, major == 2).astype(jnp.int32)
        places = jnp.stack([major, major ^ 1, major ^ 2, major ^ 3, inner])
        weights = (part, near, far, middle, onward)
        weights += (down, down_near, down_far, down_middle, down_onward)
        grads = [shaped((part.shape[0] + 3 * 256, 256), BF)] * 4
        room = [pltpu.VMEM((width, 2 * units), BF), pltpu.VMEM((units, width), BF)]
    else:
        places = just_minor
        weights = (gate_up_half, down_half)
        grads = [shaped((width, 2 * units), BF), shaped((units, width), BF)]
        room = []
    rows_total = 2 * groups * MOST
    results = call(
        functools.partial(expert_kernel, groups=groups, hidden_units=units, packed=packed),
        [shaped((groups * MOST, width), F32)] * 2 + [shaped((groups * MOST, width), BF)] * 2 + grads,
        (places,) + tuple(received) + (other_low, other_high) + weights,
        scratch=[pltpu.VMEM((rows_total, width), BF)] * 2
        + [pltpu.VMEM((rows_total, width), F32)] * 2
        + [pltpu.VMEM((rows_total, units), BF), pltpu.VMEM((rows_total, 2 * units), BF)]
        + room,
        name="expert",
        micros=18,
    )
    own_low, own_high, part_low, part_high = results[:4]
    grads = results[4:]
    high = (own_high + swap(part_high, "fsdp", 1).astype(F32)).astype(BF)
    low = (own_low + swap(part_low, "fsdp", 1).astype(F32)).astype(BF)
    backs = exchange_back(low, high, groups)

    if packed:
        first = along(grads[3], INWARD)
        middle = along(grads[3], MIDDLE)
        sent = added(grads[2], first)
        near = along(after(grads[1], first), NEAR)
        split = 12 * shard_rows
        far = [along(sent[:split], FAR), along(sent[split:], FAR)]
        backs[0] = after(backs[0], sent, middle)
        away, kept, shard_down = call(
            sum_parts_kernel,
            [
                shaped((8 * shard_rows, 256), BF),
                shaped((8 * shard_rows, 256), F32),
                shaped((256, width), F32),
            ],
            (just_minor, grads[0], near, middle) + tuple(far),
            name="sum_parts",
            micros=3,
        )
        shard_gate_up = call(
            unpack_kernel,
            shaped((shard_rows, 2 * FF), F32),
            (just_minor, kept, swap(away, "fsdp", 1)),
            name="unpack_expert",
            micros=2,
        )
    else:
        scatter = lambda v: lax.psum_scatter(
            v,
            "fsdp",
            scatter_dimension=0,
            tiled=True,
            axis_index_groups=minor_groups(major_count),
        ).astype(F32)
        shard_down = scatter(grads[1])
        part = scatter(grads[0]).reshape(2, shard_rows, FF)
        away = lax.dynamic_index_in_dim(part, 1 - minor, 0, False).astype(BF)
        kept = lax.dynamic_index_in_dim(part, minor, 0, False)
        arrived = swap(away, "fsdp", 1).astype(F32)
        first = jnp.where(minor == 0, kept, arrived).reshape(shard_rows, 2, major_count, 1, unit)
        second = jnp.where(minor == 0, arrived, kept).reshape(shard_rows, 2, major_count, 1, unit)
        shard_gate_up = jnp.concatenate([first, second], axis=3).reshape(shard_rows, 2 * FF)

    columns = (kinds, mix_at, value_at, gain_two_at, square_at)
    part_rows = width // 2 if packed else width
    out_part = shaped((part_rows, width + SMALL), BF)
    outputs, grad_hidden, grad_att, out_away, out_kept, grad_residual = call(
        functools.partial(
            combine_kernel, groups=groups, columns=columns, shard_rows=shard_rows, packed=packed
        ),
        [
            shaped((count, width), BF),
            shaped((count, width), F32),
            shaped((count, width), BF),
            out_part,
            out_part,
            shaped((count, kinds), BF),
        ],
        (slots,) + tuple(backs)
        + (hidden, low_two, cot, route, residual, small, small_t, out_full, attended),
        scratch=[pltpu.VMEM((groups * MOST, width), BF)] * 2
        + [pltpu.VMEM((width, width + SMALL), BF)],
        name="combine",
        micros=10,
    )
    head_half = pairs // 2
    back_where = jnp.stack([jnp.asarray(r, jnp.int32) for r in ranks] + [me_expert] + owners)

    def attend_back(part, grad_rows):
        base = part * head_half
        from_rows = pl.BlockSpec((count, PAIR), lambda h, w: (0, base + h))
        from_keys = pl.BlockSpec((length, PAIR), lambda h, w: (0, base + h))
        to_rows = pl.BlockSpec((count, PAIR), lambda h, w: (0, h))
        to_keys = pl.BlockSpec((length, PAIR), lambda h, w: (0, h))
        grads_part = shaped((part_rows, 3 * width // 2), BF)
        return call(
            functools.partial(attend_back_kernel, slots=groups, packed=packed),
            [
                shaped((count, width // 2), BF),
                shaped((length, width // 2), BF),
                shaped((length, width // 2), BF),
                grads_part,
                grads_part,
            ],
            (back_where, q, k_all, v_all, grad_rows, log_total, cosine, sine, normed, normed),
            grid=(head_half,),
            in_specs=[
                from_rows,
                from_keys,
                from_keys,
                from_rows,
                pl.BlockSpec((1, 8, 2 * count), lambda h, w: (base + h, 0, 0)),
                pl.BlockSpec((length, PAIR), fixed),
                pl.BlockSpec((length, PAIR), fixed),
                pl.BlockSpec((width, length), fixed),
                pl.BlockSpec((width, count), lambda h, w: (0, w[groups])),
            ],
            out_specs=[
                to_rows,
                to_keys,
                to_keys,
                pl.BlockSpec(grads_part.shape, fixed),
                pl.BlockSpec(grads_part.shape, fixed),
            ],
            scratch=[pltpu.VMEM((width, 3 * width // 2), BF)],
            name="attend_back",
            micros=11,
        )

    dq_a, dk_a, dv_a, a_away, a_kept = attend_back(0, grad_att)
    if packed:
        quarter = width // 4
        a_away, a_kept, out_kept, _ = lax.optimization_barrier((a_away, a_kept, out_kept, far[0]))
        out_both = added(out_kept, swap(out_away, "expert", 1))
        grad_att = after(grad_att, a_kept, out_both)
    dq_b, dk_b, dv_b, b_away, b_kept = attend_back(1, grad_att)
    half_rows = pl.BlockSpec((count, width // 2), fixed)
    half_keys = pl.BlockSpec((count, width // 2), at_rank)
    rows_back, own_back = call(
        functools.partial(project_back_kernel, slots=groups),
        [shaped((length, width), BF), shaped((count, width), F32)],
        (back_where, dq_a, dq_b, dk_a, dk_b, dv_a, dv_b, qkv_full),
        grid=(groups,),
        in_specs=[half_rows] * 2 + [half_keys] * 4 + [pl.BlockSpec((width, 3 * width), fixed)],
        out_specs=[pl.BlockSpec((count, width), at_rank), pl.BlockSpec((count, width), fixed)],
        name="project_back",
        micros=6,
    )
    if packed:
        a_both = added(a_kept, swap(a_away, "expert", 1))
        out_sum = added(out_both[:quarter], swap(out_both[quarter:], "fsdp", 1))
        a_sum = added(a_both[:quarter], swap(a_both[quarter:], "fsdp", 1))
        b_away, out_sum, a_sum = lax.optimization_barrier(
            (b_away, out_sum, a_sum, near)
        )[:3]
        b_both = added(b_kept, swap(b_away, "expert", 1))
        b_sum = added(b_both[:quarter], swap(b_both[quarter:], "fsdp", 1))
        parts_all = jnp.concatenate([a_sum, b_sum, out_sum], axis=1)
        total, other = across_rest(
            after(parts_all, away, rows_back), shard_rows // 2
        )
    else:
        both = jnp.concatenate([a_kept, b_kept, out_kept], axis=1)
        both = lax.psum_scatter(both, "fsdp", scatter_dimension=0, tiled=True)
        total = lax.psum(both, "expert")
        other = total
    rows_sum = sequence_scatter_sum(rows_back, count)
    grad_tokens = call(
        functools.partial(finish_kernel, gain_at=gain_one_at),
        shaped((count, width), BF),
        (just_minor, tok, small_t, grad_hidden, own_back, rows_sum),
        name="finish",
        micros=3,
    )

    shared_grads = call(
        functools.partial(
            shared_kernel, columns=columns, width=width, entries=length * width, packed=packed
        ),
        [
            shaped((shard_rows, 3 * width), F32),
            shaped((shard_rows, width), F32),
            shaped((kinds, shard_rows), F32),
            shaped((2 * NCONST, shard_rows), F32),
            shaped((NCONST, shard_rows), F32),
            shaped((1, shard_rows), F32),
            shaped((1, shard_rows), F32),
            shaped((1, 2), F32),
        ],
        (jnp.stack([core]), total, other, qkv_weight, gain_one[None]),
        name="shared_grads",
        micros=3,
    )
    grad_qkv, grad_out, grad_router, grad_gate, grad_value, grad_one, grad_two, stream = shared_grads
    return (
        outputs[None],
        grad_tokens[None],
        grad_one[0],
        grad_qkv,
        grad_out,
        grad_two[0],
        grad_router.T,
        grad_gate.T,
        grad_value.T,
        shard_gate_up[None],
        shard_down[None],
        grad_residual[None],
        stream,
    )


def solution(mesh):
    return jax.shard_map(
        on_device,
        mesh=mesh,
        in_specs=(
            P("fsdp", "expert", None),
            P("fsdp"),
            P("fsdp", None),
            P("fsdp", None),
            P("fsdp"),
            P("fsdp", None),
            P("fsdp", None),
            P("fsdp", None),
            P("expert", "fsdp", None),
            P("expert", "fsdp", None),
            P("fsdp", "expert", None),
            P("fsdp", "expert", None),
            P("fsdp", "expert", None),
        ),
        out_specs=(
            P("fsdp", "expert", None),
            P("fsdp", "expert", None),
            P("fsdp"),
            P("fsdp", None),
            P("fsdp", None),
            P("fsdp"),
            P("fsdp", None),
            P("fsdp", None),
            P("fsdp", None),
            P("expert", "fsdp", None),
            P("expert", "fsdp", None),
            P("fsdp", "expert", None),
            P("fsdp", None),
        ),
        check_vma=False,
    )
```

```python
import functools

import jax
import jax.numpy as jnp
from jax import lax
from jax.experimental import pallas as pl
from jax.experimental.pallas import tpu as pltpu
from jax.sharding import PartitionSpec as P

HEAD = 64
FF = 2048
NCONST = 2
MOST = 80
PAIR = 2 * HEAD
SMALL = 128

epsilon = 1e-06
masked_score = -1e30
BF = jnp.bfloat16
F32 = jnp.float32


def mm(a, b):
    return jnp.dot(a, b, preferred_element_type=F32)


def mm_nt(a, b):
    return lax.dot_general(a, b, (((1,), (1,)), ((), ())), preferred_element_type=F32)


def mm_tn(a, b):
    return lax.dot_general(a, b, (((0,), (0,)), ((), ())), preferred_element_type=F32)


def split_low(values):
    high = values.astype(BF)
    return high, (values - high.astype(F32)).astype(BF)


def lanes(shape):
    return lax.broadcasted_iota(jnp.int32, shape, len(shape) - 1)


def rows_of(shape):
    return lax.broadcasted_iota(jnp.int32, shape, 0)


def rms_scale(values):
    return lax.rsqrt(jnp.mean(values * values, axis=-1, keepdims=True) + epsilon)


def turned(values, cosine, sine):
    lane = lanes(values.shape) % HEAD
    swapped = jnp.where(
        lane < HEAD // 2,
        pltpu.roll(values, PAIR - HEAD // 2, 1),
        pltpu.roll(values, HEAD // 2, 1),
    )
    return values * cosine + swapped * sine


def call(kernel, outs, args, grid=(), in_specs=None, out_specs=None, scratch=(), scalars=1, name=None, micros=2):
    whole = pl.BlockSpec(memory_space=pltpu.VMEM)
    multi = isinstance(outs, (tuple, list))
    if in_specs is None:
        in_specs = [whole] * (len(args) - scalars)
    if out_specs is None:
        out_specs = [whole] * len(outs) if multi else whole
    return pl.pallas_call(
        kernel,
        out_shape=outs,
        grid_spec=pltpu.PrefetchScalarGridSpec(
            num_scalar_prefetch=scalars,
            grid=grid,
            in_specs=in_specs,
            out_specs=out_specs,
            scratch_shapes=list(scratch),
        ),
        compiler_params=pltpu.CompilerParams(vmem_limit_bytes=56 * 1024 * 1024),
        cost_estimate=pl.CostEstimate(
            flops=micros * 90_000_000, transcendentals=0, bytes_accessed=micros * 300_000
        ),
        name=name,
    )(*args)


def shaped(shape, dtype):
    return jax.ShapeDtypeStruct(shape, dtype)


def swap(values, axis, bits):
    size = lax.axis_size(axis)
    return lax.ppermute(values, axis, [(i, i ^ bits) for i in range(size)])


def along(values, pairs):
    return lax.ppermute(
        values, "fsdp", [(2 * i + b, 2 * j + b) for i, j in pairs for b in (0, 1)]
    )


def after(values, *others):
    return lax.optimization_barrier((values,) + tuple(others))[0]


FAR = ((0, 2), (2, 0), (1, 3), (3, 1))
NEAR = ((0, 1), (1, 0), (2, 3), (3, 2))
MIDDLE = ((1, 2), (2, 1))
OUTWARD = ((2, 3), (1, 0))
INWARD = ((0, 1), (3, 2))


def minor_groups(major):
    return [[2 * i + b for i in range(major)] for b in (0, 1)]


def blocks_kernel(where, gate_up, out):
    rows = gate_up.shape[0]
    for block in range(8):
        at = (2 * block + 1 - where[0]) * 256
        out[block * rows : (block + 1) * rows, :] = gate_up[:, pl.ds(pl.multiple_of(at, 256), 256)]


def pack_kernel(where, gate_up, arrived, out):
    rows = gate_up.shape[0]
    mine = where[0]
    for block in range(8):
        at = (2 * block + mine) * 256
        own = pl.ds(pl.multiple_of(2 * block * rows + mine * rows, rows), rows)
        other = pl.ds(pl.multiple_of(2 * block * rows + (1 - mine) * rows, rows), rows)
        out[own, :] = gate_up[:, pl.ds(pl.multiple_of(at, 256), 256)]
        out[other, :] = arrived[block * rows : (block + 1) * rows, :]


def sum_parts_kernel(where, a, b, c, d0, d1, d2, away, kept, down):
    rows = away.shape[0] // 8
    mine = where[0]

    def total(start, size, d, base):
        source, shifted = pl.ds(start, size), pl.ds(start - base, size)
        return (
            a[source, :].astype(F32)
            + b[source, :].astype(F32)
            + c[source, :].astype(F32)
            + d[shifted, :].astype(F32)
        )

    for block in range(8):
        here = slice(block * rows, (block + 1) * rows)
        base = 2 * block * rows
        d, cut = ((d0, 0), (d1, 8 * rows), (d2, 14 * rows))[(block > 3) + (block > 6)]
        own = pl.multiple_of(base + mine * rows, rows)
        other = pl.multiple_of(base + (1 - mine) * rows, rows)
        away[here, :] = total(other, rows, d, cut).astype(BF)
        kept[here, :] = total(own, rows, d, cut)
    for block in range(3):
        base = 16 * rows + block * 256
        down[:, block * 256 : (block + 1) * 256] = total(base, 256, d2, 14 * rows)


def unpack_kernel(where, kept, arrived, out):
    rows = out.shape[0]
    mine = where[0]
    for block in range(8):
        here = slice(block * rows, (block + 1) * rows)
        own = pl.ds(pl.multiple_of((2 * block + mine) * 256, 256), 256)
        other = pl.ds(pl.multiple_of((2 * block + 1 - mine) * 256, 256), 256)
        out[:, own] = kept[here, :]
        out[:, other] = arrived[here, :].astype(F32)


def shared_pack(qkv, out, small_rows):
    core = lax.axis_index("expert") % 2
    half_qkv, half_out = qkv.shape[1] // 2, out.shape[1] // 2
    rows = qkv.shape[0]

    def kernel(where, qkv_ref, out_ref, small_ref, packed):
        packed[:, :half_qkv] = qkv_ref[:, pl.ds(pl.multiple_of(where[0] * half_qkv, 128), half_qkv)]
        packed[:, half_qkv : half_qkv + half_out] = out_ref[
            :, pl.ds(pl.multiple_of(where[0] * half_out, 128), half_out)
        ]
        packed[:32, half_qkv + half_out :] = small_ref[...]
        packed[32:, half_qkv + half_out :] = jnp.zeros((rows - 32, SMALL), BF)

    return call(
        kernel,
        shaped((rows, half_qkv + half_out + SMALL), BF),
        (jnp.stack([core]).astype(jnp.int32), qkv, out, small_rows),
        name="pack_shared",
        micros=1,
    )


def shared_gather(mine, down, early, late):
    me = lax.axis_index("fsdp")
    major = [mine, swap(mine, "fsdp", 2), swap(mine, "fsdp", 4)]
    minor = [swap(mine, "fsdp", 1)]
    major.append(swap(after(mine, minor[0]), "fsdp", 6))
    minor.append(swap(after(major[1], minor[0]), "fsdp", 1))
    minor.append(swap(after(major[2], *early), "fsdp", 1))
    minor.append(swap(after(major[3], minor[1], *late), "fsdp", 1))
    down_near = along(after(down, major[3]), NEAR)
    down_far = along(after(down, major[3]), FAR)
    slots = [2 * j for j in range(4)] + [2 * j + 1 for j in range(4)]
    own = after(jnp.concatenate(major + minor, axis=0), down_near, down_far)
    return own, swap(own, "expert", 1), [me ^ s for s in slots], down_near, down_far


def added(kept, arrived):
    return (kept.astype(F32) + arrived.astype(F32)).astype(BF)


def along_chips(both, gate):
    for axis, bits in (("expert", 2), ("fsdp", 1)):
        half = both.shape[0] // 2
        both = added(after(both[:half], *gate), swap(both[half:], axis, bits))
        gate = ()
    return both


def across_major(parts, rows):
    pieces = [swap(parts[j * rows : (j + 1) * rows], "fsdp", 2 * j) for j in (1, 2, 3)]
    total = parts[:rows].astype(F32)
    for piece in pieces:
        total += piece.astype(F32)
    return total.astype(BF), pieces[0]


def sequence_gather(values, across):
    size = lax.axis_size("expert")
    me = lax.axis_index("expert")
    if size != 4:
        every = lax.all_gather(values, "expert", axis=0, tiled=True)
        middle = every.shape[0] // 2
        return every[:middle], every[middle:], list(range(size))
    pair = jnp.concatenate([values, across], axis=0)
    return pair, swap(pair, "expert", 1), [me, me ^ 2, me ^ 1, me ^ 3]


def exchange(sends):
    half = len(sends) // 2
    received = [swap(v, "expert", j) if j else v for j, v in enumerate(sends)]
    low = swap(jnp.concatenate(received[:half], axis=0), "fsdp", 1)
    high = swap(after(jnp.concatenate(received[half:], axis=0), low), "fsdp", 1)
    return received, low, high


def exchange_back(low, high, size):
    rows = 2 * low.shape[0] // size
    if size == 4:
        upper = swap(high, "expert", 2)
        joined = swap(jnp.concatenate([low[rows:], upper[rows:]], axis=0), "expert", 1)
        return [low[:rows], joined[:rows], upper[:rows], joined[rows:]]
    pieces = [w[i : i + rows] for w in (low, high) for i in range(0, w.shape[0], rows)]
    return [swap(piece, "expert", j) if j else piece for j, piece in enumerate(pieces)]


def sequence_scatter_sum(full, rows):
    size = lax.axis_size("expert")
    me = lax.axis_index("expert")
    if size != 4:
        return lax.psum_scatter(full, "expert", scatter_dimension=0, tiled=True).astype(F32)

    def block(bits):
        return lax.dynamic_slice_in_dim(full, (me ^ bits) * rows, rows, 0)

    away = jnp.concatenate([block(1), block(3)], axis=0)
    kept = jnp.concatenate([block(0), block(2)], axis=0)
    both = kept.astype(F32) + swap(away, "expert", 1).astype(F32)
    return both[:rows] + swap(both[rows:].astype(BF), "expert", 2).astype(F32)


def project_kernel(where, *refs, slots, gain_at, placed):
    if placed:
        tok_a, tok_b, cosine, sine, weight, small_t, q, k, v, normed = refs
    else:
        tok_a, tok_b, cosine, sine, own_ref, other_ref = refs[:6]
        q, k, v, normed, weight, out_ref, small_ref, small_t = refs[6:]
    step = pl.program_id(0)
    rank = where[step]
    own = where[slots]
    width = tok_a.shape[1]

    if not placed:

        @pl.when(step == 0)
        def _():
            first = where[slots + 9] == 0
            rows = width // 8
            half_qkv, half_out = 3 * width // 2, width // 2
            for index in range(8):
                source = pl.ds(index * rows, rows)
                target = pl.ds(pl.multiple_of(where[slots + 1 + index] * rows, rows), rows)
                a, b = own_ref[source, :], other_ref[source, :]
                left = jnp.where(first, a, b)
                right = jnp.where(first, b, a)
                weight[target, :half_qkv] = left[:, :half_qkv]
                weight[target, half_qkv:] = right[:, :half_qkv]
                out_ref[target, :half_out] = left[:, half_qkv : half_qkv + half_out]
                out_ref[target, half_out:] = right[:, half_qkv : half_qkv + half_out]
                of_rows = jnp.zeros((SMALL, SMALL), F32)
                of_rows = jnp.concatenate(
                    [a[:32, half_qkv + half_out :].astype(F32), of_rows[32:]], axis=0
                ).T
                small_ref[target, :] = of_rows[:rows].astype(BF)
            small_t[...] = small_ref[...].astype(F32).T[:32]

    @pl.when(rank > own)
    def _():
        k[...] = jnp.zeros_like(k)
        v[...] = jnp.zeros_like(v)
        normed[...] = jnp.zeros_like(normed)

    @pl.when(rank <= own)
    def _():
        x = jnp.where(step < slots // 2, tok_a[...], tok_b[...]).astype(F32)
        wide = (x * rms_scale(x)) * small_t[gain_at : gain_at + 1, :]
        low = wide.astype(BF)
        normed[...] = low.T
        cos, sin = cosine[...], sine[...]
        keys = mm(low, weight[:, width : 2 * width])
        for at in range(0, width, PAIR):
            k[:, at : at + PAIR] = turned(keys[:, at : at + PAIR], cos, sin).astype(BF)
        v[...] = mm(low, weight[:, 2 * width :]).astype(BF)

        @pl.when(rank == own)
        def _():
            queries = mm(low, weight[:, :width])
            for at in range(0, width, PAIR):
                q[:, at : at + PAIR] = turned(queries[:, at : at + PAIR], cos, sin).astype(BF)


def stacked_heads(values, scale=None):
    lane = lanes(values.shape)
    if scale is not None:
        values = values * jnp.asarray(scale, values.dtype)
    zero = jnp.zeros_like(values)
    return jnp.concatenate(
        [jnp.where(lane < HEAD, values, zero), jnp.where(lane < HEAD, zero, values)], axis=0
    )


def visible_keys(own, keys, count):
    key = lax.broadcasted_iota(jnp.int32, (keys, 2 * count), 0)
    query = lax.broadcasted_iota(jnp.int32, (keys, 2 * count), 1) % count
    return key <= query + own * count


def attend_kernel(where, q, k, v, attended, log_total, *, slots):
    own = where[slots]
    count, keys = q.shape[0], k.shape[0]
    query = stacked_heads(q[...], HEAD ** (-0.5))
    scores = mm_nt(k[...], query)
    scores = jnp.where(visible_keys(own, keys, count), scores, masked_score)
    top = jnp.max(scores, axis=0, keepdims=True)
    weights = jnp.exp(scores - top)
    total = jnp.sum(weights, axis=0, keepdims=True)
    log_total[...] = jnp.broadcast_to(top + jnp.log(total), (8, 2 * count))[None]
    weights = (weights * (1.0 / total)).astype(BF)
    both = mm_tn(weights, v[...])
    lane = lanes((count, PAIR))
    attended[...] = jnp.where(lane < HEAD, both[:count], both[count:]).astype(BF)


def attend_back_kernel(where, q, k, v, grad_att, log_total, cosine, sine, normed, normed_own, dq, dk, dv, away, kept, sums, *, slots, packed):
    step = pl.program_id(0)
    own = where[slots]
    count, keys = q.shape[0], k.shape[0]
    query = stacked_heads(q[...], HEAD ** (-0.5))
    grad_rows = stacked_heads(grad_att[...])
    key_rows = k[...]
    scores = mm_nt(key_rows, query)
    weights = jnp.where(
        visible_keys(own, keys, count), jnp.exp(scores - log_total[0, :1, :]), 0.0
    )
    grad_weights = mm_nt(v[...], grad_rows)
    delta = jnp.sum(weights * grad_weights, axis=0, keepdims=True)
    grad_scores = (weights * (grad_weights - delta)).astype(BF)
    grad_v = mm(weights.astype(BF), grad_rows).astype(BF)
    dv[...] = grad_v
    grad_k = turned(mm(grad_scores, query), cosine[...], -sine[...]).astype(BF)
    dk[...] = grad_k
    both = mm_tn(grad_scores, key_rows)
    lane = lanes((count, PAIR))
    grad_q = jnp.where(lane < HEAD, both[:count], both[count:]) * HEAD ** (-0.5)
    mine = pl.ds(pl.multiple_of(own * count, count), count)
    grad_q = turned(grad_q, cosine[mine, :], -sine[mine, :]).astype(BF)
    dq[...] = grad_q
    of_keys = mm(normed[...], jnp.concatenate([grad_k, grad_v], axis=1))
    of_queries = mm(normed_own[...], grad_q)
    steps = kept.shape[1] // (3 * PAIR)
    for index in range(steps):

        @pl.when(step == index)
        def _():
            for part, values in enumerate((of_queries, of_keys[:, :PAIR], of_keys[:, PAIR:])):
                at = (part * steps + index) * PAIR
                sums[:, at : at + PAIR] = values

    @pl.when(step == steps - 1)
    def _():
        if packed:
            split_rows(where, slots + 1, sums, away, kept)
        else:
            kept[...] = sums[...].astype(BF)
            away[...] = jnp.zeros_like(away)


def split_rows(where, at, values, away, kept):
    core, chip = where[at + 8], where[at + 9]
    rows = values.shape[0] // 32
    for index in range(0, 16, 2):
        target = slice(index * rows, (index + 2) * rows)
        for ref, side in ((kept, core), (away, 1 - core)):
            pieces = []
            for step in (index, index + 1):
                rank = 2 * (chip ^ (step // 8)) + side
                base = (where[at + step % 8] * 4 + rank) * rows
                pieces.append(values[pl.ds(pl.multiple_of(base, 8), rows), :])
            ref[target, :] = jnp.concatenate(pieces, axis=0).astype(BF)


def routing(routes, resid, logits, groups):
    count = routes.shape[0]
    lane = lanes((count, SMALL))
    kind = lanes(resid.shape)
    hot, picked = [], []
    for choice in range(2):
        route = routes[:, choice : choice + 1]
        hot.append(lane == route)
        picked.append(
            jnp.sum(jnp.where(hot[choice], logits, 0.0), axis=-1, keepdims=True)
            + jnp.sum(jnp.where(kind == route, resid, 0.0), axis=-1, keepdims=True)
        )
    top = jnp.maximum(picked[0], picked[1])
    first, second = jnp.exp(picked[0] - top), jnp.exp(picked[1] - top)
    gates = [first / (first + second), second / (first + second)]
    named = jnp.logical_or(hot[0], hot[1]).astype(BF)
    earlier = (lanes((count, count)) < rows_of((count, count))).astype(BF)
    place = mm(earlier, named)
    dispatch = []
    column = lanes((count, groups * MOST))
    for choice in range(2):
        route = routes[:, choice : choice + 1]
        slot = jnp.sum(jnp.where(hot[choice], place, 0.0), axis=-1, keepdims=True)
        target = jnp.where(route < groups, route * MOST + slot.astype(jnp.int32), -1)
        dispatch.append((column == target).astype(BF))
    return gates, hot, dispatch


def route_kernel(where, att, out_weight, tok, small, small_t, resid, routes, cot, hidden_ref, low_ref, *rest, groups, gain_at):
    sends = rest[:groups]
    rows_x, rows_g = rest[groups], rest[groups + 1]
    hidden = tok[...].astype(F32) + mm(att[...], out_weight[...])
    hidden_ref[...] = hidden
    low = ((hidden * rms_scale(hidden)) * small_t[gain_at : gain_at + 1, :]).astype(BF)
    low_ref[...] = low
    logits = mm(low, small[...])
    gates, _, dispatch = routing(routes[...], resid[...].astype(F32), logits, groups)
    grad = cot[...].astype(F32)
    rows_x[...] = mm_tn(dispatch[0] + dispatch[1], low).astype(BF)
    rows_g[...] = (
        mm_tn(dispatch[0], (gates[0] * grad).astype(BF))
        + mm_tn(dispatch[1], (gates[1] * grad).astype(BF))
    ).astype(BF)
    for slot in range(groups):
        source = pl.ds(pl.multiple_of(where[slot] * MOST, MOST), MOST)
        sends[slot][:MOST, :] = rows_x[source, :]
        sends[slot][MOST:, :] = rows_g[source, :]


def expert_kernel(where, *refs, groups, hidden_units, packed):
    refs = list(refs)

    def take(amount):
        taken = refs[:amount]
        del refs[:amount]
        return taken

    received = take(groups) + take(2)
    if packed:
        unit_parts, down_parts = take(5), take(5)
    else:
        gate_up, down = take(2)
    own_out, other_out = take(2), take(2)
    if packed:
        messages = take(4)
    else:
        grad_gate_up, grad_down = take(2)
    rows, grads, out_rows, back_rows, acts, grad_units = take(6)
    if packed:
        gate_up, down = take(2)
    width = rows.shape[1]
    total = 2 * groups * MOST
    index = 0
    for ref in received:
        for base in range(0, ref.shape[0], 2 * MOST):
            target = slice(index * MOST, (index + 1) * MOST)
            rows[target, :] = ref[base : base + MOST, :]
            grads[target, :] = ref[base + MOST : base + 2 * MOST, :]
            index += 1
    if packed:
        part = width // 4

        def place(slot, ref, down_ref):
            target = pl.ds(pl.multiple_of(where[slot] * part, part), part)
            for block in range(8):
                gate_up[target, block * 256 : (block + 1) * 256] = ref[
                    block * part : (block + 1) * part, :
                ]
            down[pl.ds(pl.multiple_of(where[slot] * 256, 256), 256), :] = down_ref[...]

        for slot in range(3):
            place(slot, unit_parts[slot], down_parts[slot])

        @pl.when(where[4] == 1)
        def _():
            place(3, unit_parts[3], down_parts[3])

        @pl.when(where[4] == 0)
        def _():
            place(3, unit_parts[4], down_parts[4])

    x, g = rows[...], grads[...]
    chunk = 256
    out_rows[...] = jnp.zeros_like(out_rows)
    back_rows[...] = jnp.zeros_like(back_rows)

    def forward_back(step, carry):
        first = pl.ds(pl.multiple_of(step * chunk, chunk), chunk)
        second = pl.ds(pl.multiple_of(hidden_units + step * chunk, chunk), chunk)
        gate_w, up_w, down_w = gate_up[:, first], gate_up[:, second], down[first, :]
        gate, up = mm(x, gate_w), mm(x, up_w)
        sig = 1.0 / (1.0 + jnp.exp(-gate))
        silu = gate * sig
        act = (silu * up).astype(BF)
        acts[:, first] = act
        grad_act = mm_nt(g, down_w)
        grad_gate = (grad_act * up * sig * (1.0 + gate * (1.0 - sig))).astype(BF)
        grad_up = (grad_act * silu).astype(BF)
        grad_units[:, first] = grad_gate
        grad_units[:, second] = grad_up
        out_rows[...] += mm(act, down_w)
        back_rows[...] += mm_nt(grad_gate, gate_w) + mm_nt(grad_up, up_w)
        return carry

    lax.fori_loop(0, hidden_units // chunk, forward_back, 0)
    index = 0
    for ref in own_out + other_out:
        for base in range(0, ref.shape[0], 2 * MOST):
            source = slice(index * MOST, (index + 1) * MOST)
            ref[base : base + MOST, :] = out_rows[source, :].astype(ref.dtype)
            ref[base + MOST : base + 2 * MOST, :] = back_rows[source, :].astype(ref.dtype)
            index += 1
    if not packed:
        grad_gate_up[...] = mm_tn(x, grad_units[...]).astype(BF)
        grad_down[...] = mm_tn(acts[...], g).astype(BF)
        return
    part = width // 4

    def weight_grad(step, carry):
        block = pl.ds(pl.multiple_of(step * 512, 512), 512)
        gate_up[:, block] = mm_tn(x, grad_units[:, block]).astype(BF)
        return carry

    lax.fori_loop(0, 4, weight_grad, 0)
    for slot, ref in enumerate(messages):
        source = pl.ds(pl.multiple_of(where[slot] * part, part), part)
        for block in range(8):
            ref[block * part : (block + 1) * part, :] = gate_up[
                source, block * 256 : (block + 1) * 256
            ]
        mine = acts[:, pl.ds(pl.multiple_of(where[slot] * 256, 256), 256)]
        of_down = mm_tn(mine, g).astype(BF)
        for block in range(3):
            base = 8 * part + block * 256
            ref[base : base + 256, :] = of_down[:, block * 256 : (block + 1) * 256]


def combine_kernel(where, *refs, groups, columns, shard_rows, packed):
    backs = refs[:groups]
    (hidden_ref, low_ref, cot, routes, resid, small, small_t, out_weight, att,
     out_ref, grad_hidden_ref, grad_att_ref, grad_away, grad_kept, grad_resid,
     rows_y, rows_d, sums) = refs[groups:]
    kinds, mix_at, value_at, gain_two_at, square_at = columns
    for slot in range(groups):
        target = pl.ds(pl.multiple_of(where[slot] * MOST, MOST), MOST)
        rows_y[target, :] = backs[slot][:MOST, :]
        rows_d[target, :] = backs[slot][MOST:, :]
    hidden, low = hidden_ref[...], low_ref[...]
    count = low.shape[0]
    normed_input = low.astype(F32)
    grad_low_type = cot[...]
    grad = grad_low_type.astype(F32)
    logits = mm(low, small[...])
    grad_small_dot = mm(grad_low_type, small[...])
    route = routes[...]
    gates, hot, dispatch = routing(route, resid[...].astype(F32), logits, groups)
    returned = [mm(dispatch[c], rows_y[...]) for c in range(2)]
    grad_back = mm(dispatch[0] + dispatch[1], rows_d[...])
    grad_dot = jnp.sum(grad * normed_input, axis=-1, keepdims=True)
    is_copy = [(route[:, c : c + 1] == groups + 1).astype(F32) for c in range(2)]
    grad_gates = [
        jnp.sum(grad * returned[c], axis=-1, keepdims=True) + is_copy[c] * grad_dot
        for c in range(2)
    ]
    direct = gates[0] * is_copy[0] + gates[1] * is_copy[1]
    mixture = gates[0] * returned[0] + gates[1] * returned[1]
    lane = lanes((count, SMALL))
    grad_logits = jnp.zeros((count, SMALL), F32)
    value_weights = jnp.zeros((count, SMALL), F32)
    for const in range(NCONST):
        first = logits[:, mix_at + 2 * const : mix_at + 2 * const + 1]
        second = logits[:, mix_at + 2 * const + 1 : mix_at + 2 * const + 2]
        top = jnp.maximum(first, second)
        first, second = jnp.exp(first - top), jnp.exp(second - top)
        mix = [first / (first + second), second / (first + second)]
        value_dot = grad_small_dot[:, value_at + const : value_at + const + 1]
        named = [(route[:, c : c + 1] == groups + 2 + const).astype(F32) for c in range(2)]
        for c in range(2):
            grad_gates[c] += named[c] * (mix[0] * grad_dot + mix[1] * value_dot)
        weight = gates[0] * named[0] + gates[1] * named[1]
        direct += weight * mix[0]
        of_value = weight * mix[1]
        mixture += of_value * small_t[value_at + const : value_at + const + 1, :]
        value_weights = jnp.where(lane == value_at + const, of_value, value_weights)
        grad_mix = [weight * grad_dot, weight * value_dot]
        common = mix[0] * grad_mix[0] + mix[1] * grad_mix[1]
        for c in range(2):
            grad_logits = jnp.where(
                lane == mix_at + 2 * const + c, mix[c] * (grad_mix[c] - common), grad_logits
            )
    outputs = hidden + mixture + direct * normed_input
    out_ref[...] = outputs.astype(BF)
    common = gates[0] * grad_gates[0] + gates[1] * grad_gates[1]
    for c in range(2):
        grad_logits = jnp.where(hot[c], gates[c] * (grad_gates[c] - common), grad_logits)
    grad_resid[...] = grad_logits[:, :kinds].astype(BF)
    high, rest = split_low(grad_logits)
    weights = small[...]
    grad_low = grad_back + direct * grad + mm_nt(high, weights) + mm_nt(rest, weights)
    scale = rms_scale(hidden)
    normed = hidden * scale
    of_gain = split_low(grad_low * normed)
    ones = (lane == gain_two_at).astype(BF)
    value_high, value_rest = split_low(value_weights)
    summed = (
        mm_tn(low, high)
        + mm_tn(low, rest)
        + mm_tn(grad_low_type, value_high)
        + mm_tn(grad_low_type, value_rest)
        + mm_tn(of_gain[0], ones)
        + mm_tn(of_gain[1], ones)
    )
    column, row = lanes(summed.shape), rows_of(summed.shape)
    mine = row // shard_rows == where[groups]
    for index, total in enumerate((jnp.sum(hidden * hidden), jnp.sum(outputs * outputs))):
        for part, value in enumerate(split_low(jnp.full((1, 1), total, F32))):
            spot = jnp.logical_and(mine, column == square_at + 2 * index + part)
            summed = jnp.where(spot, value.astype(F32), summed)
    grad_normed = grad_low * small_t[gain_two_at : gain_two_at + 1, :]
    grad_hidden = grad + scale * (
        grad_normed - normed * jnp.mean(grad_normed * normed, axis=-1, keepdims=True)
    )
    grad_hidden_ref[...] = grad_hidden
    branch = grad_hidden.astype(BF)
    grad_att_ref[...] = mm_nt(branch, out_weight[...]).astype(BF)
    width = branch.shape[1]
    sums[:, :width] = mm_tn(att[...], branch)
    sums[:, width:] = summed
    if packed:
        split_rows(where, groups + 1, sums, grad_away, grad_kept)
    else:
        grad_kept[...] = sums[...].astype(BF)
        grad_away[...] = jnp.zeros_like(grad_away)


def project_back_kernel(where, *refs, slots):
    queries, keys, values = refs[0:2], refs[2:4], refs[4:6]
    weight, rows_back, own_back = refs[6:]
    rank = where[pl.program_id(0)]
    own = where[slots]
    half = keys[0].shape[1]
    width = 2 * half

    def through(parts, base):
        result = mm_nt(parts[0][...], weight[:, base : base + half])
        return result + mm_nt(parts[1][...], weight[:, base + half : base + width])

    @pl.when(rank > own)
    def _():
        rows_back[...] = jnp.zeros_like(rows_back)

    @pl.when(rank <= own)
    def _():
        rows_back[...] = (through(keys, width) + through(values, 2 * width)).astype(BF)

        @pl.when(rank == own)
        def _():
            own_back[...] = through(queries, 0)


def finish_kernel(where, tok, small_t, grad_hidden, own_back, rows_back, out, *, gain_at):
    x = tok[...].astype(F32)
    scale = rms_scale(x)
    normed = x * scale
    grad = (own_back[...] + rows_back[...]) * small_t[gain_at : gain_at + 1, :]
    out[...] = (
        grad_hidden[...]
        + scale * (grad - normed * jnp.mean(grad * normed, axis=-1, keepdims=True))
    ).astype(BF)


def shared_kernel(where, total, other, weight, gain, qkv, out, router, gate, value, gain_one, gain_two, stream, room, *, columns, width, entries, packed):
    kinds, mix_at, value_at, gain_two_at, square_at = columns
    if packed:
        rows = room.shape[0] // 4
        for parts, rank in ((total, where[0]), (other, where[0] ^ 1)):
            both = parts[...].astype(F32)
            room[pl.ds(pl.multiple_of(rank * rows, 8), rows), :] = both[:rows]
            room[pl.ds(pl.multiple_of((rank ^ 2) * rows, 8), rows), :] = both[rows:]
    else:
        room[...] = total[...].astype(F32)
    values = room[...]
    half = width // 2
    for part in range(3):
        for side in range(2):
            at = (3 * side + part) * half
            to = part * width + side * half
            qkv[:, to : to + half] = values[:, at : at + half]
    out[...] = values[:, 3 * width : 4 * width]
    rows = values.shape[0]

    def as_columns(block):
        spare = jnp.zeros((SMALL - rows, SMALL), F32)
        return jnp.concatenate([block, spare], axis=0).T[:, :rows]

    small = values[:, 4 * width :]
    turned_small = as_columns(small)
    router[...] = turned_small[:kinds]
    gate[...] = turned_small[mix_at : mix_at + 2 * NCONST]
    value[...] = turned_small[value_at : value_at + NCONST]
    gain_two[...] = turned_small[gain_two_at : gain_two_at + 1]
    of_gain = jnp.sum(qkv[...] * weight[...].astype(F32), axis=-1, keepdims=True)
    gain_one[...] = as_columns(jnp.broadcast_to(of_gain, (rows, SMALL)))[:1] / gain[...].astype(F32)
    squares = small[:1, square_at : square_at + 4]
    hidden = squares[:, 0:1] + squares[:, 1:2]
    outputs = squares[:, 2:3] + squares[:, 3:4]
    stream[...] = jnp.sqrt(jnp.where(lanes((1, 2)) == 0, hidden, outputs) / entries)


def on_device(
    tokens,
    gain_one,
    qkv_weight,
    out_weight,
    gain_two,
    router_weight,
    const_gate,
    const_value,
    expert_gate_up,
    expert_down,
    gate_residual,
    routes,
    cotangent,
):
    parts = lax.axis_size("fsdp")
    groups = lax.axis_size("expert")
    me_fsdp = lax.axis_index("fsdp").astype(jnp.int32)
    me_expert = lax.axis_index("expert").astype(jnp.int32)
    minor, major, core = me_fsdp % 2, me_fsdp // 2, me_expert % 2
    packed = parts == 8 and groups == 4
    major_count = parts // 2
    tok = tokens[0]
    count, width = tok.shape
    length = groups * count
    pairs = width // PAIR
    kinds = router_weight.shape[1]
    mix_at, value_at = kinds, kinds + 2 * NCONST
    gain_one_at = value_at + NCONST
    gain_two_at = gain_one_at + 1
    square_at = gain_two_at + 1
    shard_rows = width // parts
    unit = FF // parts
    units = FF // 2
    fixed = lambda j, w: (0, 0)
    at_slot = lambda j, w: (j, 0)
    at_rank = lambda j, w: (w[j], 0)
    just_minor = jnp.stack([minor])

    small_rows = jnp.concatenate(
        [router_weight.T, const_gate.T, const_value.T, gain_one[None], gain_two[None]], axis=0
    )
    small_rows = jnp.pad(
        small_rows, ((0, 32 - small_rows.shape[0]), (0, SMALL - small_rows.shape[1]))
    )
    frequency = 10000.0 ** (-jnp.arange(HEAD // 2, dtype=F32) / (HEAD // 2))
    angles = jnp.arange(length, dtype=F32)[:, None] * frequency[None, :]
    cosine, sine = jnp.cos(angles), jnp.sin(angles)
    cosine = jnp.concatenate([cosine, cosine, cosine, cosine], axis=1)
    sine = jnp.concatenate([-sine, sine, -sine, sine], axis=1)

    weight_args, order, across = (), [], None
    if packed:
        shared = shared_pack(qkv_weight, out_weight, small_rows)
        across = swap(tok, "expert", 2)
        tok_a, tok_b, ranks = sequence_gather(tok, across)
        away = call(
            blocks_kernel,
            shaped((8 * shard_rows, 256), BF),
            (just_minor, expert_gate_up[0]),
            name="blocks",
            micros=1,
        )
        arrived = swap(away, "fsdp", 1)
        part = call(
            pack_kernel,
            shaped((16 * shard_rows, 256), BF),
            (just_minor, expert_gate_up[0], arrived),
            name="pack_expert",
            micros=1,
        )
        down = expert_down[0]
        own_half, other_half, order, down_near, down_far = shared_gather(
            shared, down, (across, arrived), (part, tok_b, cosine, sine)
        )
        down_onward = along(down_far, OUTWARD)
        down_middle = along(after(down, down_far), MIDDLE)
        weight_args = (own_half, other_half)
        far, near = along(part, FAR), along(part, NEAR)
    else:
        qkv_full = lax.all_gather(qkv_weight, "fsdp", axis=0, tiled=True)
        out_full = lax.all_gather(out_weight, "fsdp", axis=0, tiled=True)
        small = lax.all_gather(small_rows[:, :shard_rows], "fsdp", axis=1, tiled=True).T
        small = jnp.pad(small, ((0, 0), (0, SMALL - 32)))
        small_t = small.astype(F32).T[:32]
        weight_args = (qkv_full, small_t)
        halves = expert_gate_up[0].reshape(shard_rows, 2, major_count, 2, unit)
        away = lax.dynamic_index_in_dim(halves, 1 - minor, 3, False).reshape(shard_rows, FF)
        kept = lax.dynamic_index_in_dim(halves, minor, 3, False).reshape(shard_rows, FF)
        arrived = swap(away, "fsdp", 1)
        part = jnp.concatenate(
            [jnp.where(minor == 0, kept, arrived), jnp.where(minor == 0, arrived, kept)], axis=0
        )
        gather = functools.partial(
            lax.all_gather,
            axis_name="fsdp",
            axis=0,
            tiled=True,
            axis_index_groups=minor_groups(major_count),
        )
        gate_up_half, down_half = gather(part), gather(expert_down[0])
        tok_a, tok_b, ranks = sequence_gather(tok, across)
    where = jnp.stack(
        [jnp.asarray(r, jnp.int32) for r in ranks] + [me_expert] + order + [core]
    )

    half_columns = 2 * width + SMALL
    outs = [
        shaped((count, width), BF),
        shaped((length, width), BF),
        shaped((length, width), BF),
        shaped((width, length), BF),
    ]
    out_specs = [
        pl.BlockSpec((count, width), fixed),
        pl.BlockSpec((count, width), at_rank),
        pl.BlockSpec((count, width), at_rank),
        pl.BlockSpec((width, count), lambda j, w: (0, w[j])),
    ]
    if packed:
        weight_specs = [pl.BlockSpec((width, half_columns), fixed)] * 2
        outs += [
            shaped((width, 3 * width), BF),
            shaped((width, width), BF),
            shaped((width, SMALL), BF),
            shaped((32, width), F32),
        ]
        out_specs += [pl.BlockSpec(o.shape, fixed) for o in outs[4:]]
    else:
        weight_specs = [pl.BlockSpec((width, 3 * width), fixed), pl.BlockSpec((32, width), fixed)]
    projected = call(
        functools.partial(project_kernel, slots=groups, gain_at=gain_one_at, placed=not packed),
        outs,
        (where, tok_a, tok_b, cosine, sine) + weight_args,
        grid=(groups,),
        in_specs=[
            pl.BlockSpec((count, width), lambda j, w: (jnp.minimum(j, groups // 2 - 1), 0)),
            pl.BlockSpec((count, width), lambda j, w: (jnp.maximum(j - groups // 2, 0), 0)),
            pl.BlockSpec((count, PAIR), at_rank),
            pl.BlockSpec((count, PAIR), at_rank),
        ]
        + weight_specs,
        out_specs=out_specs,
        name="project",
        micros=10,
    )
    q, k_all, v_all, normed = projected[:4]
    if packed:
        qkv_full, out_full, small, small_t = projected[4:]
    head_rows = pl.BlockSpec((count, PAIR), lambda h, w: (0, h))
    head_keys = pl.BlockSpec((length, PAIR), lambda h, w: (0, h))
    head_log = pl.BlockSpec((1, 8, 2 * count), lambda h, w: (h, 0, 0))
    attended, log_total = call(
        functools.partial(attend_kernel, slots=groups),
        [shaped((count, width), BF), shaped((pairs, 8, 2 * count), F32)],
        (where, q, k_all, v_all),
        grid=(pairs,),
        in_specs=[head_rows, head_keys, head_keys],
        out_specs=[head_rows, head_log],
        name="attend",
        micros=12,
    )

    residual, route, cot = gate_residual[0], routes[0], cotangent[0]
    if packed:
        attended = after(attended, down_onward, down_middle)
    owners = [me_fsdp ^ (2 * j + i) for i in (0, 1) for j in range(4)]
    owners += [core, me_expert // 2]
    slots = jnp.stack([me_expert ^ j for j in range(groups)] + [me_fsdp] + owners)
    block = shaped((2 * MOST, width), BF)
    hidden, low_two, *sends = call(
        functools.partial(route_kernel, groups=groups, gain_at=gain_two_at),
        [shaped((count, width), F32), shaped((count, width), BF)] + [block] * groups,
        (slots, attended, out_full, tok, small, small_t, residual, route, cot),
        scratch=[pltpu.VMEM((groups * MOST, width), BF)] * 2,
        name="route",
        micros=5,
    )
    received, other_low, other_high = exchange(sends)
    if packed:
        far, near = lax.optimization_barrier((far, near, low_two))[:2]
        onward = along(far, OUTWARD)
        middle = along(after(part, far), MIDDLE)
        inner = jnp.logical_or(major == 1, major == 2).astype(jnp.int32)
        places = jnp.stack([major, major ^ 1, major ^ 2, major ^ 3, inner])
        weights = (part, near, far, middle, onward)
        weights += (down, down_near, down_far, down_middle, down_onward)
        grads = [shaped((part.shape[0] + 3 * 256, 256), BF)] * 4
        room = [pltpu.VMEM((width, 2 * units), BF), pltpu.VMEM((units, width), BF)]
    else:
        places = just_minor
        weights = (gate_up_half, down_half)
        grads = [shaped((width, 2 * units), BF), shaped((units, width), BF)]
        room = []
    rows_total = 2 * groups * MOST
    results = call(
        functools.partial(expert_kernel, groups=groups, hidden_units=units, packed=packed),
        [shaped((groups * MOST, width), F32)] * 2 + [shaped((groups * MOST, width), BF)] * 2 + grads,
        (places,) + tuple(received) + (other_low, other_high) + weights,
        scratch=[pltpu.VMEM((rows_total, width), BF)] * 2
        + [pltpu.VMEM((rows_total, width), F32)] * 2
        + [pltpu.VMEM((rows_total, units), BF), pltpu.VMEM((rows_total, 2 * units), BF)]
        + room,
        name="expert",
        micros=18,
    )
    own_low, own_high, part_low, part_high = results[:4]
    grads = results[4:]
    high = (own_high + swap(part_high, "fsdp", 1).astype(F32)).astype(BF)
    low = (own_low + swap(part_low, "fsdp", 1).astype(F32)).astype(BF)
    backs = exchange_back(low, high, groups)

    if packed:
        first = along(grads[3], INWARD)
        middle = along(grads[3], MIDDLE)
        sent = added(grads[2], first)
        near = along(after(grads[1], first), NEAR)
        cuts = (0, 8 * shard_rows, 14 * shard_rows, sent.shape[0])
        far = [along(sent[a:b], FAR) for a, b in zip(cuts, cuts[1:])]
        backs[0] = after(backs[0], sent, middle)
    else:
        scatter = lambda v: lax.psum_scatter(
            v,
            "fsdp",
            scatter_dimension=0,
            tiled=True,
            axis_index_groups=minor_groups(major_count),
        ).astype(F32)
        shard_down = scatter(grads[1])
        part = scatter(grads[0]).reshape(2, shard_rows, FF)
        away = lax.dynamic_index_in_dim(part, 1 - minor, 0, False).astype(BF)
        kept = lax.dynamic_index_in_dim(part, minor, 0, False)
        arrived = swap(away, "fsdp", 1).astype(F32)
        first = jnp.where(minor == 0, kept, arrived).reshape(shard_rows, 2, major_count, 1, unit)
        second = jnp.where(minor == 0, arrived, kept).reshape(shard_rows, 2, major_count, 1, unit)
        shard_gate_up = jnp.concatenate([first, second], axis=3).reshape(shard_rows, 2 * FF)

    columns = (kinds, mix_at, value_at, gain_two_at, square_at)
    part_rows = width // 2 if packed else width
    out_part = shaped((part_rows, width + SMALL), BF)
    outputs, grad_hidden, grad_att, out_away, out_kept, grad_residual = call(
        functools.partial(
            combine_kernel, groups=groups, columns=columns, shard_rows=shard_rows, packed=packed
        ),
        [
            shaped((count, width), BF),
            shaped((count, width), F32),
            shaped((count, width), BF),
            out_part,
            out_part,
            shaped((count, kinds), BF),
        ],
        (slots,) + tuple(backs)
        + (hidden, low_two, cot, route, residual, small, small_t, out_full, attended),
        scratch=[pltpu.VMEM((groups * MOST, width), BF)] * 2
        + [pltpu.VMEM((width, width + SMALL), F32)],
        name="combine",
        micros=10,
    )
    head_half = pairs // 2
    back_where = jnp.stack([jnp.asarray(r, jnp.int32) for r in ranks] + [me_expert] + owners)

    def attend_back(part, grad_rows):
        base = part * head_half
        from_rows = pl.BlockSpec((count, PAIR), lambda h, w: (0, base + h))
        from_keys = pl.BlockSpec((length, PAIR), lambda h, w: (0, base + h))
        to_rows = pl.BlockSpec((count, PAIR), lambda h, w: (0, h))
        to_keys = pl.BlockSpec((length, PAIR), lambda h, w: (0, h))
        grads_part = shaped((part_rows, 3 * width // 2), BF)
        return call(
            functools.partial(attend_back_kernel, slots=groups, packed=packed),
            [
                shaped((count, width // 2), BF),
                shaped((length, width // 2), BF),
                shaped((length, width // 2), BF),
                grads_part,
                grads_part,
            ],
            (back_where, q, k_all, v_all, grad_rows, log_total, cosine, sine, normed, normed),
            grid=(head_half,),
            in_specs=[
                from_rows,
                from_keys,
                from_keys,
                from_rows,
                pl.BlockSpec((1, 8, 2 * count), lambda h, w: (base + h, 0, 0)),
                pl.BlockSpec((length, PAIR), fixed),
                pl.BlockSpec((length, PAIR), fixed),
                pl.BlockSpec((width, length), fixed),
                pl.BlockSpec((width, count), lambda h, w: (0, w[groups])),
            ],
            out_specs=[
                to_rows,
                to_keys,
                to_keys,
                pl.BlockSpec(grads_part.shape, fixed),
                pl.BlockSpec(grads_part.shape, fixed),
            ],
            scratch=[pltpu.VMEM((width, 3 * width // 2), F32)],
            name="attend_back",
            micros=11,
        )

    dq_a, dk_a, dv_a, a_away, a_kept = attend_back(0, grad_att)
    if packed:
        a_away, a_kept, out_kept = lax.optimization_barrier(
            (a_away, a_kept, out_kept, far[0], near)
        )[:3]
        out_both = added(out_kept, swap(out_away, "expert", 1))
        a_both = added(a_kept, swap(a_away, "expert", 1))
        grad_att = after(grad_att, a_both, out_both)
    dq_b, dk_b, dv_b, b_away, b_kept = attend_back(1, grad_att)
    def project_back(dq_late):
        half_rows = pl.BlockSpec((count, width // 2), fixed)
        half_keys = pl.BlockSpec((count, width // 2), at_rank)
        return call(
            functools.partial(project_back_kernel, slots=groups),
            [shaped((length, width), BF), shaped((count, width), F32)],
            (back_where, dq_a, dq_late, dk_a, dk_b, dv_a, dv_b, qkv_full),
            grid=(groups,),
            in_specs=[half_rows] * 2 + [half_keys] * 4 + [pl.BlockSpec((width, 3 * width), fixed)],
            out_specs=[pl.BlockSpec((count, width), at_rank), pl.BlockSpec((count, width), fixed)],
            name="project_back",
            micros=6,
        )

    if packed:
        b_away = after(b_away, far[1])
        out_sum, a_sum = along_chips(out_both, (b_kept,)), along_chips(a_both, (b_kept,))
        b_both = added(b_kept, swap(b_away, "expert", 1))
        dq_b = after(dq_b, b_both)
        b_sum = along_chips(b_both, ())
        parts_all = jnp.concatenate([a_sum, b_sum, out_sum], axis=1)
        rows_back, own_back = project_back(dq_b)
        total, piece = across_major(after(parts_all, rows_back), shard_rows // 4)
        own_grads = after(grads[0], piece)
        away, kept, shard_down = call(
            sum_parts_kernel,
            [
                shaped((8 * shard_rows, 256), BF),
                shaped((8 * shard_rows, 256), F32),
                shaped((256, width), F32),
            ],
            (just_minor, own_grads, near, middle) + tuple(far),
            name="sum_parts",
            micros=3,
        )
        shard_gate_up = call(
            unpack_kernel,
            shaped((shard_rows, 2 * FF), F32),
            (just_minor, kept, swap(away, "fsdp", 1)),
            name="unpack_expert",
            micros=2,
        )
    else:
        both = jnp.concatenate([a_kept, b_kept, out_kept], axis=1)
        both = lax.psum_scatter(both, "fsdp", scatter_dimension=0, tiled=True)
        total = lax.psum(both, "expert")
        other = total
        rows_back, own_back = project_back(dq_b)
    rows_sum = sequence_scatter_sum(rows_back, count)
    grad_tokens = call(
        functools.partial(finish_kernel, gain_at=gain_one_at),
        shaped((count, width), BF),
        (just_minor, tok, small_t, grad_hidden, own_back, rows_sum),
        name="finish",
        micros=3,
    )

    if packed:
        total = after(total, grad_tokens, shard_gate_up)
        total = jnp.concatenate([total, swap(total, "expert", 2)], axis=0)
        other = swap(total, "expert", 1)
    shared_grads = call(
        functools.partial(
            shared_kernel, columns=columns, width=width, entries=length * width, packed=packed
        ),
        [
            shaped((shard_rows, 3 * width), F32),
            shaped((shard_rows, width), F32),
            shaped((kinds, shard_rows), F32),
            shaped((2 * NCONST, shard_rows), F32),
            shaped((NCONST, shard_rows), F32),
            shaped((1, shard_rows), F32),
            shaped((1, shard_rows), F32),
            shaped((1, 2), F32),
        ],
        (jnp.stack([me_expert]), total, other, qkv_weight, gain_one[None]),
        scratch=[pltpu.VMEM((shard_rows, 4 * width + SMALL), F32)],
        name="shared_grads",
        micros=3,
    )
    grad_qkv, grad_out, grad_router, grad_gate, grad_value, grad_one, grad_two, stream = shared_grads
    return (
        outputs[None],
        grad_tokens[None],
        grad_one[0],
        grad_qkv,
        grad_out,
        grad_two[0],
        grad_router.T,
        grad_gate.T,
        grad_value.T,
        shard_gate_up[None],
        shard_down[None],
        grad_residual[None],
        stream,
    )


def solution(mesh):
    return jax.shard_map(
        on_device,
        mesh=mesh,
        in_specs=(
            P("fsdp", "expert", None),
            P("fsdp"),
            P("fsdp", None),
            P("fsdp", None),
            P("fsdp"),
            P("fsdp", None),
            P("fsdp", None),
            P("fsdp", None),
            P("expert", "fsdp", None),
            P("expert", "fsdp", None),
            P("fsdp", "expert", None),
            P("fsdp", "expert", None),
            P("fsdp", "expert", None),
        ),
        out_specs=(
            P("fsdp", "expert", None),
            P("fsdp", "expert", None),
            P("fsdp"),
            P("fsdp", None),
            P("fsdp", None),
            P("fsdp"),
            P("fsdp", None),
            P("fsdp", None),
            P("fsdp", None),
            P("expert", "fsdp", None),
            P("expert", "fsdp", None),
            P("fsdp", "expert", None),
            P("fsdp", None),
        ),
        check_vma=False,
    )
```

```python
import functools

import jax
import jax.numpy as jnp
from jax import lax
from jax.experimental import pallas as pl
from jax.experimental.pallas import tpu as pltpu
from jax.sharding import PartitionSpec as P

HEAD = 64
FF = 2048
NCONST = 2
MOST = 80
PAIR = 2 * HEAD
SMALL = 128

epsilon = 1e-06
masked_score = -1e30
BF = jnp.bfloat16
F32 = jnp.float32


def mm(a, b):
    return jnp.dot(a, b, preferred_element_type=F32)


def mm_nt(a, b):
    return lax.dot_general(a, b, (((1,), (1,)), ((), ())), preferred_element_type=F32)


def mm_tn(a, b):
    return lax.dot_general(a, b, (((0,), (0,)), ((), ())), preferred_element_type=F32)


def split_low(values):
    high = values.astype(BF)
    return high, (values - high.astype(F32)).astype(BF)


def lanes(shape):
    return lax.broadcasted_iota(jnp.int32, shape, len(shape) - 1)


def rows_of(shape):
    return lax.broadcasted_iota(jnp.int32, shape, 0)


def rms_scale(values):
    return lax.rsqrt(jnp.mean(values * values, axis=-1, keepdims=True) + epsilon)


def turned(values, cosine, sine):
    lane = lanes(values.shape) % HEAD
    swapped = jnp.where(
        lane < HEAD // 2,
        pltpu.roll(values, PAIR - HEAD // 2, 1),
        pltpu.roll(values, HEAD // 2, 1),
    )
    return values * cosine + swapped * sine


def call(kernel, outs, args, grid=(), in_specs=None, out_specs=None, scratch=(), scalars=1, name=None, micros=2):
    whole = pl.BlockSpec(memory_space=pltpu.VMEM)
    multi = isinstance(outs, (tuple, list))
    if in_specs is None:
        in_specs = [whole] * (len(args) - scalars)
    if out_specs is None:
        out_specs = [whole] * len(outs) if multi else whole
    return pl.pallas_call(
        kernel,
        out_shape=outs,
        grid_spec=pltpu.PrefetchScalarGridSpec(
            num_scalar_prefetch=scalars,
            grid=grid,
            in_specs=in_specs,
            out_specs=out_specs,
            scratch_shapes=list(scratch),
        ),
        compiler_params=pltpu.CompilerParams(vmem_limit_bytes=56 * 1024 * 1024),
        cost_estimate=pl.CostEstimate(
            flops=micros * 90_000_000, transcendentals=0, bytes_accessed=micros * 300_000
        ),
        name=name,
    )(*args)


def shaped(shape, dtype):
    return jax.ShapeDtypeStruct(shape, dtype)


def swap(values, axis, bits):
    size = lax.axis_size(axis)
    return lax.ppermute(values, axis, [(i, i ^ bits) for i in range(size)])


def along(values, pairs):
    return lax.ppermute(
        values, "fsdp", [(2 * i + b, 2 * j + b) for i, j in pairs for b in (0, 1)]
    )


def after(values, *others):
    return lax.optimization_barrier((values,) + tuple(others))[0]


FAR = ((0, 2), (2, 0), (1, 3), (3, 1))
NEAR = ((0, 1), (1, 0), (2, 3), (3, 2))
MIDDLE = ((1, 2), (2, 1))
OUTWARD = ((2, 3), (1, 0))
INWARD = ((0, 1), (3, 2))
UP = ((0, 1), (1, 2), (2, 3))
DOWN = ((3, 2), (2, 1), (1, 0))


def minor_groups(major):
    return [[2 * i + b for i in range(major)] for b in (0, 1)]


def blocks_kernel(where, gate_up, out):
    rows = gate_up.shape[0]
    for block in range(8):
        at = (2 * block + 1 - where[0]) * 256
        out[block * rows : (block + 1) * rows, :] = gate_up[:, pl.ds(pl.multiple_of(at, 256), 256)]


def pack_kernel(where, gate_up, arrived, out):
    rows = gate_up.shape[0]
    mine = where[0]
    for block in range(8):
        at = (2 * block + mine) * 256
        own = pl.ds(pl.multiple_of(2 * block * rows + mine * rows, rows), rows)
        other = pl.ds(pl.multiple_of(2 * block * rows + (1 - mine) * rows, rows), rows)
        out[own, :] = gate_up[:, pl.ds(pl.multiple_of(at, 256), 256)]
        out[other, :] = arrived[block * rows : (block + 1) * rows, :]


def sum_parts_kernel(where, a, b, c, away, kept, down):
    rows = away.shape[0] // 8
    mine = where[0]

    def total(source):
        return a[source, :].astype(F32) + b[source, :].astype(F32) + c[source, :].astype(F32)

    for block in range(8):
        here = slice(block * rows, (block + 1) * rows)
        base = 2 * block * rows
        own = pl.ds(pl.multiple_of(base + mine * rows, rows), rows)
        other = pl.ds(pl.multiple_of(base + (1 - mine) * rows, rows), rows)
        away[here, :] = total(other).astype(BF)
        kept[here, :] = total(own)
    for block in range(3):
        base = 16 * rows + block * 256
        down[:, block * 256 : (block + 1) * 256] = total(slice(base, base + 256))


def unpack_kernel(where, kept, arrived, out):
    rows = out.shape[0]
    mine = where[0]
    for block in range(8):
        here = slice(block * rows, (block + 1) * rows)
        own = pl.ds(pl.multiple_of((2 * block + mine) * 256, 256), 256)
        other = pl.ds(pl.multiple_of((2 * block + 1 - mine) * 256, 256), 256)
        out[:, own] = kept[here, :]
        out[:, other] = arrived[here, :].astype(F32)


def shared_pack(qkv, out, small):
    core = lax.axis_index("expert") % 2
    half_qkv, half_out = qkv.shape[1] // 2, out.shape[1] // 2
    rows = qkv.shape[0]

    def kernel(where, qkv_ref, out_ref, *refs):
        small_refs, (packed, room) = refs[:-2], refs[-2:]
        packed[:, :half_qkv] = qkv_ref[:, pl.ds(pl.multiple_of(where[0] * half_qkv, 128), half_qkv)]
        packed[:, half_qkv : half_qkv + half_out] = out_ref[
            :, pl.ds(pl.multiple_of(where[0] * half_out, 128), half_out)
        ]
        room[...] = jnp.zeros_like(room)
        at = 0
        for ref in small_refs:
            room[at : at + ref.shape[0], : ref.shape[1]] = ref[...].astype(F32)
            at += ref.shape[0]
        packed[:, half_qkv + half_out :] = room[...].astype(BF)

    return call(
        kernel,
        shaped((rows, half_qkv + half_out + SMALL), BF),
        (jnp.stack([core]).astype(jnp.int32), qkv, out) + small,
        scratch=[pltpu.VMEM((rows, SMALL), F32)],
        name="pack_shared",
        micros=1,
    )


def shared_gather(mine, down, early, late):
    me = lax.axis_index("fsdp")
    major = [mine, swap(mine, "fsdp", 2), swap(mine, "fsdp", 4)]
    minor = [swap(mine, "fsdp", 1)]
    major.append(swap(after(mine, minor[0]), "fsdp", 6))
    minor.append(swap(after(major[1], minor[0]), "fsdp", 1))
    minor.append(swap(after(major[2], *early), "fsdp", 1))
    minor.append(swap(after(major[3], minor[1], *late), "fsdp", 1))
    down_near = along(after(down, major[3]), NEAR)
    down_far = along(after(down, major[3]), FAR)
    slots = [2 * j for j in range(4)] + [2 * j + 1 for j in range(4)]
    own = after(jnp.concatenate(major + minor, axis=0), down_near, down_far)
    return own, swap(own, "expert", 1), [me ^ s for s in slots], down_near, down_far


def added(kept, arrived):
    return (kept.astype(F32) + arrived.astype(F32)).astype(BF)


def along_chips(both, gate):
    for axis, bits in (("expert", 2), ("fsdp", 1)):
        half = both.shape[0] // 2
        both = added(after(both[:half], *gate), swap(both[half:], axis, bits))
        gate = ()
    return both


def across_major(parts, rows):
    pieces = [swap(parts[j * rows : (j + 1) * rows], "fsdp", 2 * j) for j in (1, 2, 3)]
    return [parts[:rows]] + pieces


def summed_up(pieces):
    total = pieces[0].astype(F32)
    for piece in pieces[1:]:
        total += piece.astype(F32)
    return total.astype(BF)


def sequence_gather(values, across):
    size = lax.axis_size("expert")
    me = lax.axis_index("expert")
    if size != 4:
        every = lax.all_gather(values, "expert", axis=0, tiled=True)
        middle = every.shape[0] // 2
        return every[:middle], every[middle:], list(range(size))
    pair = jnp.concatenate([values, across], axis=0)
    return pair, swap(pair, "expert", 1), [me, me ^ 2, me ^ 1, me ^ 3]


def exchange(sends):
    half = len(sends) // 2
    received = [swap(v, "expert", j) if j else v for j, v in enumerate(sends)]
    low = swap(jnp.concatenate(received[:half], axis=0), "fsdp", 1)
    high = swap(after(jnp.concatenate(received[half:], axis=0), low), "fsdp", 1)
    return received, low, high


def exchange_back(low, high, size):
    rows = 2 * low.shape[0] // size
    if size == 4:
        upper = swap(high, "expert", 2)
        joined = swap(jnp.concatenate([low[rows:], upper[rows:]], axis=0), "expert", 1)
        return [low[:rows], joined[:rows], upper[:rows], joined[rows:]]
    pieces = [w[i : i + rows] for w in (low, high) for i in range(0, w.shape[0], rows)]
    return [swap(piece, "expert", j) if j else piece for j, piece in enumerate(pieces)]


def sequence_scatter_sum(full, rows):
    size = lax.axis_size("expert")
    me = lax.axis_index("expert")
    if size != 4:
        return lax.psum_scatter(full, "expert", scatter_dimension=0, tiled=True).astype(F32)

    def block(bits):
        return lax.dynamic_slice_in_dim(full, (me ^ bits) * rows, rows, 0)

    away = jnp.concatenate([block(1), block(3)], axis=0)
    kept = jnp.concatenate([block(0), block(2)], axis=0)
    both = kept.astype(F32) + swap(away, "expert", 1).astype(F32)
    return both[:rows] + swap(both[rows:].astype(BF), "expert", 2).astype(F32)


def project_kernel(where, *refs, slots, gain_at, placed):
    if placed:
        tok_a, tok_b, cosine, sine, weight, small_t, q, k, v, normed = refs
    else:
        tok_a, tok_b, cosine, sine, own_ref, other_ref = refs[:6]
        q, k, v, normed, weight, out_ref, small_ref, small_t = refs[6:]
    step = pl.program_id(0)
    rank = where[step]
    own = where[slots]
    width = tok_a.shape[1]

    if not placed:

        @pl.when(step == 0)
        def _():
            first = where[slots + 9] == 0
            rows = width // 8
            half_qkv, half_out = 3 * width // 2, width // 2
            for index in range(8):
                source = pl.ds(index * rows, rows)
                target = pl.ds(pl.multiple_of(where[slots + 1 + index] * rows, rows), rows)
                a, b = own_ref[source, :], other_ref[source, :]
                left = jnp.where(first, a, b)
                right = jnp.where(first, b, a)
                weight[target, :half_qkv] = left[:, :half_qkv]
                weight[target, half_qkv:] = right[:, :half_qkv]
                out_ref[target, :half_out] = left[:, half_qkv : half_qkv + half_out]
                out_ref[target, half_out:] = right[:, half_qkv : half_qkv + half_out]
                of_rows = jnp.zeros((SMALL, SMALL), F32)
                of_rows = jnp.concatenate(
                    [a[:32, half_qkv + half_out :].astype(F32), of_rows[32:]], axis=0
                ).T
                small_ref[target, :] = of_rows[:rows].astype(BF)
            small_t[...] = small_ref[...].astype(F32).T[:32]

    @pl.when(rank > own)
    def _():
        k[...] = jnp.zeros_like(k)
        v[...] = jnp.zeros_like(v)
        normed[...] = jnp.zeros_like(normed)

    @pl.when(rank <= own)
    def _():
        x = jnp.where(step < slots // 2, tok_a[...], tok_b[...]).astype(F32)
        wide = (x * rms_scale(x)) * small_t[gain_at : gain_at + 1, :]
        low = wide.astype(BF)
        normed[...] = low.T
        cos, sin = cosine[...], sine[...]
        keys = mm(low, weight[:, width : 2 * width])
        for at in range(0, width, PAIR):
            k[:, at : at + PAIR] = turned(keys[:, at : at + PAIR], cos, sin).astype(BF)
        v[...] = mm(low, weight[:, 2 * width :]).astype(BF)

        @pl.when(rank == own)
        def _():
            queries = mm(low, weight[:, :width])
            for at in range(0, width, PAIR):
                q[:, at : at + PAIR] = turned(queries[:, at : at + PAIR], cos, sin).astype(BF)


def stacked_heads(values, scale=None):
    lane = lanes(values.shape)
    if scale is not None:
        values = values * jnp.asarray(scale, values.dtype)
    zero = jnp.zeros_like(values)
    return jnp.concatenate(
        [jnp.where(lane < HEAD, values, zero), jnp.where(lane < HEAD, zero, values)], axis=0
    )


def visible_keys(own, keys, count):
    key = lax.broadcasted_iota(jnp.int32, (keys, 2 * count), 0)
    query = lax.broadcasted_iota(jnp.int32, (keys, 2 * count), 1) % count
    return key <= query + own * count


def attend_kernel(where, q, k, v, attended, kept, *, slots):
    own = where[slots]
    count, keys = q.shape[0], k.shape[0]
    query = stacked_heads(q[...], HEAD ** (-0.5))
    scores = mm_nt(k[...], query)
    scores = jnp.where(visible_keys(own, keys, count), scores, masked_score)
    top = jnp.max(scores, axis=0, keepdims=True)
    weights = jnp.exp(scores - top)
    total = jnp.sum(weights, axis=0, keepdims=True)
    weights = (weights * (1.0 / total)).astype(BF)
    kept[0] = weights
    both = mm_tn(weights, v[...])
    lane = lanes((count, PAIR))
    attended[...] = jnp.where(lane < HEAD, both[:count], both[count:]).astype(BF)


def attend_back_kernel(where, q, k, v, grad_att, kept_weights, cosine, sine, normed, normed_own, dq, dk, dv, away, kept, sums, *, slots, packed):
    step = pl.program_id(0)
    own = where[slots]
    count = q.shape[0]
    query = stacked_heads(q[...], HEAD ** (-0.5))
    grad_rows = stacked_heads(grad_att[...])
    key_rows = k[...]
    low_weights = kept_weights[0]
    weights = low_weights.astype(F32)
    grad_weights = mm_nt(v[...], grad_rows)
    delta = jnp.sum(weights * grad_weights, axis=0, keepdims=True)
    grad_scores = (weights * (grad_weights - delta)).astype(BF)
    grad_v = mm(low_weights, grad_rows).astype(BF)
    dv[...] = grad_v
    grad_k = turned(mm(grad_scores, query), cosine[...], -sine[...]).astype(BF)
    dk[...] = grad_k
    both = mm_tn(grad_scores, key_rows)
    lane = lanes((count, PAIR))
    grad_q = jnp.where(lane < HEAD, both[:count], both[count:]) * HEAD ** (-0.5)
    mine = pl.ds(pl.multiple_of(own * count, count), count)
    grad_q = turned(grad_q, cosine[mine, :], -sine[mine, :]).astype(BF)
    dq[...] = grad_q
    of_keys = mm(normed[...], jnp.concatenate([grad_k, grad_v], axis=1))
    of_queries = mm(normed_own[...], grad_q)
    steps = kept.shape[1] // (3 * PAIR)
    for index in range(steps):

        @pl.when(step == index)
        def _():
            for part, values in enumerate((of_queries, of_keys[:, :PAIR], of_keys[:, PAIR:])):
                at = (part * steps + index) * PAIR
                sums[:, at : at + PAIR] = values

    @pl.when(step == steps - 1)
    def _():
        if packed:
            split_rows(where, slots + 1, sums, away, kept)
        else:
            kept[...] = sums[...].astype(BF)
            away[...] = jnp.zeros_like(away)


def split_rows(where, at, values, away, kept):
    core, chip = where[at + 8], where[at + 9]
    rows = values.shape[0] // 32
    for index in range(0, 16, 2):
        target = slice(index * rows, (index + 2) * rows)
        for ref, side in ((kept, core), (away, 1 - core)):
            pieces = []
            for step in (index, index + 1):
                rank = 2 * (chip ^ (step // 8)) + side
                base = (where[at + step % 8] * 4 + rank) * rows
                pieces.append(values[pl.ds(pl.multiple_of(base, 8), rows), :])
            ref[target, :] = jnp.concatenate(pieces, axis=0).astype(BF)


def as_lanes(rows):
    rows = rows.astype(F32)
    spare = jnp.zeros((SMALL - rows.shape[0], rows.shape[1]), F32)
    return jnp.concatenate([rows, spare], axis=0).T


def routing(routes, resid, logits, groups):
    count = routes.shape[0]
    lane = lanes((count, SMALL))
    logits = logits + resid
    hot, picked = [], []
    for choice in range(2):
        route = routes[:, choice : choice + 1]
        hot.append(lane == route)
        picked.append(jnp.sum(jnp.where(hot[choice], logits, 0.0), axis=-1, keepdims=True))
    top = jnp.maximum(picked[0], picked[1])
    first, second = jnp.exp(picked[0] - top), jnp.exp(picked[1] - top)
    gates = [first / (first + second), second / (first + second)]
    named = jnp.logical_or(hot[0], hot[1]).astype(BF)
    earlier = (lanes((count, count)) < rows_of((count, count))).astype(BF)
    place = mm(earlier, named)
    dispatch = []
    column = lanes((count, groups * MOST))
    for choice in range(2):
        route = routes[:, choice : choice + 1]
        slot = jnp.sum(jnp.where(hot[choice], place, 0.0), axis=-1, keepdims=True)
        target = jnp.where(route < groups, route * MOST + slot.astype(jnp.int32), -1)
        dispatch.append((column == target).astype(BF))
    return gates, hot, dispatch


def route_kernel(where, att, out_weight, tok, small, small_t, resid, routes, cot, hidden_ref, low_ref, *rest, groups, gain_at):
    sends = rest[:groups]
    rows_x, rows_g = rest[groups], rest[groups + 1]
    hidden = tok[...].astype(F32) + mm(att[...], out_weight[...])
    hidden_ref[...] = hidden
    low = ((hidden * rms_scale(hidden)) * small_t[gain_at : gain_at + 1, :]).astype(BF)
    low_ref[...] = low
    logits = mm(low, small[...])
    route = as_lanes(routes[...])[:, :2].astype(jnp.int32)
    gates, _, dispatch = routing(route, as_lanes(resid[...]), logits, groups)
    grad = cot[...].astype(F32)
    rows_x[...] = mm_tn(dispatch[0] + dispatch[1], low).astype(BF)
    rows_g[...] = (
        mm_tn(dispatch[0], (gates[0] * grad).astype(BF))
        + mm_tn(dispatch[1], (gates[1] * grad).astype(BF))
    ).astype(BF)
    for slot in range(groups):
        source = pl.ds(pl.multiple_of(where[slot] * MOST, MOST), MOST)
        sends[slot][:MOST, :] = rows_x[source, :]
        sends[slot][MOST:, :] = rows_g[source, :]


def expert_kernel(where, *refs, groups, hidden_units, packed):
    refs = list(refs)

    def take(amount):
        taken = refs[:amount]
        del refs[:amount]
        return taken

    received = take(groups) + take(2)
    if packed:
        unit_parts, down_parts = take(5), take(5)
    else:
        gate_up, down = take(2)
    own_out, other_out = take(2), take(2)
    if packed:
        messages = take(4)
    else:
        grad_gate_up, grad_down = take(2)
    rows, grads, out_rows, back_rows, acts, grad_units = take(6)
    if packed:
        gate_up, down = take(2)
    width = rows.shape[1]
    total = 2 * groups * MOST
    index = 0
    for ref in received:
        for base in range(0, ref.shape[0], 2 * MOST):
            target = slice(index * MOST, (index + 1) * MOST)
            rows[target, :] = ref[base : base + MOST, :]
            grads[target, :] = ref[base + MOST : base + 2 * MOST, :]
            index += 1
    if packed:
        part = width // 4

        def place(slot, ref, down_ref):
            target = pl.ds(pl.multiple_of(where[slot] * part, part), part)
            for block in range(8):
                gate_up[target, block * 256 : (block + 1) * 256] = ref[
                    block * part : (block + 1) * part, :
                ]
            down[pl.ds(pl.multiple_of(where[slot] * 256, 256), 256), :] = down_ref[...]

        for slot in range(3):
            place(slot, unit_parts[slot], down_parts[slot])

        @pl.when(where[4] == 1)
        def _():
            place(3, unit_parts[3], down_parts[3])

        @pl.when(where[4] == 0)
        def _():
            place(3, unit_parts[4], down_parts[4])

    x, g = rows[...], grads[...]
    chunk = 256
    out_rows[...] = jnp.zeros_like(out_rows)
    back_rows[...] = jnp.zeros_like(back_rows)

    def forward_back(step, carry):
        first = pl.ds(pl.multiple_of(step * chunk, chunk), chunk)
        second = pl.ds(pl.multiple_of(hidden_units + step * chunk, chunk), chunk)
        gate_w, up_w, down_w = gate_up[:, first], gate_up[:, second], down[first, :]
        gate, up = mm(x, gate_w), mm(x, up_w)
        sig = 1.0 / (1.0 + jnp.exp(-gate))
        silu = gate * sig
        act = (silu * up).astype(BF)
        acts[:, first] = act
        grad_act = mm_nt(g, down_w)
        grad_gate = (grad_act * up * sig * (1.0 + gate * (1.0 - sig))).astype(BF)
        grad_up = (grad_act * silu).astype(BF)
        grad_units[:, first] = grad_gate
        grad_units[:, second] = grad_up
        out_rows[...] += mm(act, down_w)
        back_rows[...] += mm_nt(grad_gate, gate_w) + mm_nt(grad_up, up_w)
        return carry

    lax.fori_loop(0, hidden_units // chunk, forward_back, 0)
    index = 0
    for ref in own_out + other_out:
        for base in range(0, ref.shape[0], 2 * MOST):
            source = slice(index * MOST, (index + 1) * MOST)
            ref[base : base + MOST, :] = out_rows[source, :].astype(ref.dtype)
            ref[base + MOST : base + 2 * MOST, :] = back_rows[source, :].astype(ref.dtype)
            index += 1
    if not packed:
        grad_gate_up[...] = mm_tn(x, grad_units[...]).astype(BF)
        grad_down[...] = mm_tn(acts[...], g).astype(BF)
        return
    part = width // 4

    def weight_grad(step, carry):
        block = pl.ds(pl.multiple_of(step * 512, 512), 512)
        gate_up[:, block] = mm_tn(x, grad_units[:, block]).astype(BF)
        return carry

    lax.fori_loop(0, 4, weight_grad, 0)
    for slot, ref in enumerate(messages):
        source = pl.ds(pl.multiple_of(where[slot] * part, part), part)
        for block in range(8):
            ref[block * part : (block + 1) * part, :] = gate_up[
                source, block * 256 : (block + 1) * 256
            ]
        mine = acts[:, pl.ds(pl.multiple_of(where[slot] * 256, 256), 256)]
        of_down = mm_tn(mine, g).astype(BF)
        for block in range(3):
            base = 8 * part + block * 256
            ref[base : base + 256, :] = of_down[:, block * 256 : (block + 1) * 256]


def combine_kernel(where, *refs, groups, columns, shard_rows, packed):
    backs = refs[:groups]
    (hidden_ref, low_ref, cot, routes, resid, small, small_t, out_weight, att,
     out_ref, grad_hidden_ref, grad_att_ref, grad_away, grad_kept, grad_resid,
     rows_y, rows_d, sums) = refs[groups:]
    kinds, mix_at, value_at, gain_two_at, square_at = columns
    for slot in range(groups):
        target = pl.ds(pl.multiple_of(where[slot] * MOST, MOST), MOST)
        rows_y[target, :] = backs[slot][:MOST, :]
        rows_d[target, :] = backs[slot][MOST:, :]
    hidden, low = hidden_ref[...], low_ref[...]
    count = low.shape[0]
    normed_input = low.astype(F32)
    grad_low_type = cot[...]
    grad = grad_low_type.astype(F32)
    logits = mm(low, small[...])
    grad_small_dot = mm(grad_low_type, small[...])
    route = as_lanes(routes[...])[:, :2].astype(jnp.int32)
    gates, hot, dispatch = routing(route, as_lanes(resid[...]), logits, groups)
    returned = [mm(dispatch[c], rows_y[...]) for c in range(2)]
    grad_back = mm(dispatch[0] + dispatch[1], rows_d[...])
    grad_dot = jnp.sum(grad * normed_input, axis=-1, keepdims=True)
    is_copy = [(route[:, c : c + 1] == groups + 1).astype(F32) for c in range(2)]
    grad_gates = [
        jnp.sum(grad * returned[c], axis=-1, keepdims=True) + is_copy[c] * grad_dot
        for c in range(2)
    ]
    direct = gates[0] * is_copy[0] + gates[1] * is_copy[1]
    mixture = gates[0] * returned[0] + gates[1] * returned[1]
    lane = lanes((count, SMALL))
    grad_logits = jnp.zeros((count, SMALL), F32)
    value_weights = jnp.zeros((count, SMALL), F32)
    for const in range(NCONST):
        first = logits[:, mix_at + 2 * const : mix_at + 2 * const + 1]
        second = logits[:, mix_at + 2 * const + 1 : mix_at + 2 * const + 2]
        top = jnp.maximum(first, second)
        first, second = jnp.exp(first - top), jnp.exp(second - top)
        mix = [first / (first + second), second / (first + second)]
        value_dot = grad_small_dot[:, value_at + const : value_at + const + 1]
        named = [(route[:, c : c + 1] == groups + 2 + const).astype(F32) for c in range(2)]
        for c in range(2):
            grad_gates[c] += named[c] * (mix[0] * grad_dot + mix[1] * value_dot)
        weight = gates[0] * named[0] + gates[1] * named[1]
        direct += weight * mix[0]
        of_value = weight * mix[1]
        mixture += of_value * small_t[value_at + const : value_at + const + 1, :]
        value_weights = jnp.where(lane == value_at + const, of_value, value_weights)
        grad_mix = [weight * grad_dot, weight * value_dot]
        common = mix[0] * grad_mix[0] + mix[1] * grad_mix[1]
        for c in range(2):
            grad_logits = jnp.where(
                lane == mix_at + 2 * const + c, mix[c] * (grad_mix[c] - common), grad_logits
            )
    outputs = hidden + mixture + direct * normed_input
    out_ref[...] = outputs.astype(BF)
    common = gates[0] * grad_gates[0] + gates[1] * grad_gates[1]
    for c in range(2):
        grad_logits = jnp.where(hot[c], gates[c] * (grad_gates[c] - common), grad_logits)
    grad_resid[...] = grad_logits.T[:kinds].astype(BF)
    high, rest = split_low(grad_logits)
    weights = small[...]
    grad_low = grad_back + direct * grad + mm_nt(high, weights) + mm_nt(rest, weights)
    scale = rms_scale(hidden)
    normed = hidden * scale
    of_gain = split_low(grad_low * normed)
    ones = (lane == gain_two_at).astype(BF)
    value_high, value_rest = split_low(value_weights)
    summed = (
        mm_tn(low, high)
        + mm_tn(low, rest)
        + mm_tn(grad_low_type, value_high)
        + mm_tn(grad_low_type, value_rest)
        + mm_tn(of_gain[0], ones)
        + mm_tn(of_gain[1], ones)
    )
    column, row = lanes(summed.shape), rows_of(summed.shape)
    mine = row // shard_rows == where[groups]
    for index, total in enumerate((jnp.sum(hidden * hidden), jnp.sum(outputs * outputs))):
        for part, value in enumerate(split_low(jnp.full((1, 1), total, F32))):
            spot = jnp.logical_and(mine, column == square_at + 2 * index + part)
            summed = jnp.where(spot, value.astype(F32), summed)
    grad_normed = grad_low * small_t[gain_two_at : gain_two_at + 1, :]
    grad_hidden = grad + scale * (
        grad_normed - normed * jnp.mean(grad_normed * normed, axis=-1, keepdims=True)
    )
    grad_hidden_ref[...] = grad_hidden
    branch = grad_hidden.astype(BF)
    grad_att_ref[...] = mm_nt(branch, out_weight[...]).astype(BF)
    width = branch.shape[1]
    sums[:, :width] = mm_tn(att[...], branch)
    sums[:, width:] = summed
    if packed:
        split_rows(where, groups + 1, sums, grad_away, grad_kept)
    else:
        grad_kept[...] = sums[...].astype(BF)
        grad_away[...] = jnp.zeros_like(grad_away)


def project_back_kernel(where, *refs, slots):
    queries, keys, values = refs[0:2], refs[2:4], refs[4:6]
    weight, rows_back, own_back = refs[6:]
    rank = where[pl.program_id(0)]
    own = where[slots]
    half = keys[0].shape[1]
    width = 2 * half

    def through(parts, base):
        result = mm_nt(parts[0][...], weight[:, base : base + half])
        return result + mm_nt(parts[1][...], weight[:, base + half : base + width])

    @pl.when(rank > own)
    def _():
        rows_back[...] = jnp.zeros_like(rows_back)

    @pl.when(rank <= own)
    def _():
        rows_back[...] = (through(keys, width) + through(values, 2 * width)).astype(BF)

        @pl.when(rank == own)
        def _():
            own_back[...] = through(queries, 0)


def finish_kernel(where, tok, small_t, grad_hidden, own_back, rows_back, out, *, gain_at):
    x = tok[...].astype(F32)
    scale = rms_scale(x)
    normed = x * scale
    grad = (own_back[...] + rows_back[...]) * small_t[gain_at : gain_at + 1, :]
    out[...] = (
        grad_hidden[...]
        + scale * (grad - normed * jnp.mean(grad * normed, axis=-1, keepdims=True))
    ).astype(BF)


def shared_kernel(where, total, other, weight, gain, qkv, out, router, gate, value, gain_one, gain_two, stream, room, *, columns, width, entries, packed):
    kinds, mix_at, value_at, gain_two_at, square_at = columns
    if packed:
        rows = room.shape[0] // 4
        for parts, rank in ((total, where[0]), (other, where[0] ^ 1)):
            both = parts[...].astype(F32)
            room[pl.ds(pl.multiple_of(rank * rows, 8), rows), :] = both[:rows]
            room[pl.ds(pl.multiple_of((rank ^ 2) * rows, 8), rows), :] = both[rows:]
    else:
        room[...] = total[...].astype(F32)
    values = room[...]
    half = width // 2
    for part in range(3):
        for side in range(2):
            at = (3 * side + part) * half
            to = part * width + side * half
            qkv[:, to : to + half] = values[:, at : at + half]
    out[...] = values[:, 3 * width : 4 * width]
    rows = values.shape[0]

    def as_columns(block):
        spare = jnp.zeros((SMALL - rows, SMALL), F32)
        return jnp.concatenate([block, spare], axis=0).T[:, :rows]

    small = values[:, 4 * width :]
    turned_small = as_columns(small)
    router[...] = turned_small[:kinds]
    gate[...] = turned_small[mix_at : mix_at + 2 * NCONST]
    value[...] = turned_small[value_at : value_at + NCONST]
    gain_two[...] = turned_small[gain_two_at : gain_two_at + 1]
    of_gain = jnp.sum(qkv[...] * weight[...].astype(F32), axis=-1, keepdims=True)
    gain_one[...] = as_columns(jnp.broadcast_to(of_gain, (rows, SMALL)))[:1] / gain[...].astype(F32)
    squares = small[:1, square_at : square_at + 4]
    hidden = squares[:, 0:1] + squares[:, 1:2]
    outputs = squares[:, 2:3] + squares[:, 3:4]
    stream[...] = jnp.sqrt(jnp.where(lanes((1, 2)) == 0, hidden, outputs) / entries)


def on_device(
    tokens,
    gain_one,
    qkv_weight,
    out_weight,
    gain_two,
    router_weight,
    const_gate,
    const_value,
    expert_gate_up,
    expert_down,
    gate_residual,
    routes,
    cotangent,
):
    parts = lax.axis_size("fsdp")
    groups = lax.axis_size("expert")
    me_fsdp = lax.axis_index("fsdp").astype(jnp.int32)
    me_expert = lax.axis_index("expert").astype(jnp.int32)
    minor, major, core = me_fsdp % 2, me_fsdp // 2, me_expert % 2
    packed = parts == 8 and groups == 4
    major_count = parts // 2
    tok = tokens[0]
    count, width = tok.shape
    length = groups * count
    pairs = width // PAIR
    kinds = router_weight.shape[1]
    mix_at, value_at = kinds, kinds + 2 * NCONST
    gain_one_at = value_at + NCONST
    gain_two_at = gain_one_at + 1
    square_at = gain_two_at + 1
    shard_rows = width // parts
    unit = FF // parts
    units = FF // 2
    fixed = lambda j, w: (0, 0)
    at_slot = lambda j, w: (j, 0)
    at_rank = lambda j, w: (w[j], 0)
    just_minor = jnp.stack([minor])

    small_parts = (router_weight.T, const_gate.T, const_value.T, gain_one[None], gain_two[None])
    frequency = 10000.0 ** (-jnp.arange(HEAD // 2, dtype=F32) / (HEAD // 2))
    angles = jnp.arange(length, dtype=F32)[:, None] * frequency[None, :]
    cosine, sine = jnp.cos(angles), jnp.sin(angles)
    cosine = jnp.concatenate([cosine, cosine, cosine, cosine], axis=1)
    sine = jnp.concatenate([-sine, sine, -sine, sine], axis=1)

    weight_args, order, across = (), [], None
    if packed:
        shared = shared_pack(qkv_weight, out_weight, small_parts)
        across = swap(tok, "expert", 2)
        tok_a, tok_b, ranks = sequence_gather(tok, across)
        away = call(
            blocks_kernel,
            shaped((8 * shard_rows, 256), BF),
            (just_minor, expert_gate_up[0]),
            name="blocks",
            micros=1,
        )
        arrived = swap(away, "fsdp", 1)
        part = call(
            pack_kernel,
            shaped((16 * shard_rows, 256), BF),
            (just_minor, expert_gate_up[0], arrived),
            name="pack_expert",
            micros=1,
        )
        down = expert_down[0]
        own_half, other_half, order, down_near, down_far = shared_gather(
            shared, down, (across, arrived), (part, tok_b, cosine, sine)
        )
        down_onward = along(down_far, OUTWARD)
        down_middle = along(after(down, down_far), MIDDLE)
        weight_args = (own_half, other_half)
        far, near = along(part, FAR), along(part, NEAR)
    else:
        qkv_full = lax.all_gather(qkv_weight, "fsdp", axis=0, tiled=True)
        out_full = lax.all_gather(out_weight, "fsdp", axis=0, tiled=True)
        small_rows = jnp.concatenate(small_parts, axis=0)
        small = lax.all_gather(small_rows, "fsdp", axis=1, tiled=True).T
        small = jnp.pad(small, ((0, 0), (0, SMALL - small.shape[1])))
        small_t = small.astype(F32).T[:32]
        weight_args = (qkv_full, small_t)
        halves = expert_gate_up[0].reshape(shard_rows, 2, major_count, 2, unit)
        away = lax.dynamic_index_in_dim(halves, 1 - minor, 3, False).reshape(shard_rows, FF)
        kept = lax.dynamic_index_in_dim(halves, minor, 3, False).reshape(shard_rows, FF)
        arrived = swap(away, "fsdp", 1)
        part = jnp.concatenate(
            [jnp.where(minor == 0, kept, arrived), jnp.where(minor == 0, arrived, kept)], axis=0
        )
        gather = functools.partial(
            lax.all_gather,
            axis_name="fsdp",
            axis=0,
            tiled=True,
            axis_index_groups=minor_groups(major_count),
        )
        gate_up_half, down_half = gather(part), gather(expert_down[0])
        tok_a, tok_b, ranks = sequence_gather(tok, across)
    where = jnp.stack(
        [jnp.asarray(r, jnp.int32) for r in ranks] + [me_expert] + order + [core]
    )

    half_columns = 2 * width + SMALL
    outs = [
        shaped((count, width), BF),
        shaped((length, width), BF),
        shaped((length, width), BF),
        shaped((width, length), BF),
    ]
    out_specs = [
        pl.BlockSpec((count, width), fixed),
        pl.BlockSpec((count, width), at_rank),
        pl.BlockSpec((count, width), at_rank),
        pl.BlockSpec((width, count), lambda j, w: (0, w[j])),
    ]
    if packed:
        weight_specs = [pl.BlockSpec((width, half_columns), fixed)] * 2
        outs += [
            shaped((width, 3 * width), BF),
            shaped((width, width), BF),
            shaped((width, SMALL), BF),
            shaped((32, width), F32),
        ]
        out_specs += [pl.BlockSpec(o.shape, fixed) for o in outs[4:]]
    else:
        weight_specs = [pl.BlockSpec((width, 3 * width), fixed), pl.BlockSpec((32, width), fixed)]
    projected = call(
        functools.partial(project_kernel, slots=groups, gain_at=gain_one_at, placed=not packed),
        outs,
        (where, tok_a, tok_b, cosine, sine) + weight_args,
        grid=(groups,),
        in_specs=[
            pl.BlockSpec((count, width), lambda j, w: (jnp.minimum(j, groups // 2 - 1), 0)),
            pl.BlockSpec((count, width), lambda j, w: (jnp.maximum(j - groups // 2, 0), 0)),
            pl.BlockSpec((count, PAIR), at_rank),
            pl.BlockSpec((count, PAIR), at_rank),
        ]
        + weight_specs,
        out_specs=out_specs,
        name="project",
        micros=10,
    )
    q, k_all, v_all, normed = projected[:4]
    if packed:
        qkv_full, out_full, small, small_t = projected[4:]
    head_rows = pl.BlockSpec((count, PAIR), lambda h, w: (0, h))
    head_keys = pl.BlockSpec((length, PAIR), lambda h, w: (0, h))
    attended, attend_weights = call(
        functools.partial(attend_kernel, slots=groups),
        [shaped((count, width), BF), shaped((pairs, length, 2 * count), BF)],
        (where, q, k_all, v_all),
        grid=(pairs,),
        in_specs=[head_rows, head_keys, head_keys],
        out_specs=[
            head_rows,
            pl.BlockSpec((1, length, 2 * count), lambda h, w: (h, 0, 0)),
        ],
        name="attend",
        micros=12,
    )

    residual, route, cot = gate_residual[0].T, routes[0].T, cotangent[0]
    if packed:
        attended = after(attended, down_onward, down_middle)
    owners = [me_fsdp ^ (2 * j + i) for i in (0, 1) for j in range(4)]
    owners += [core, me_expert // 2]
    slots = jnp.stack([me_expert ^ j for j in range(groups)] + [me_fsdp] + owners)
    block = shaped((2 * MOST, width), BF)
    hidden, low_two, *sends = call(
        functools.partial(route_kernel, groups=groups, gain_at=gain_two_at),
        [shaped((count, width), F32), shaped((count, width), BF)] + [block] * groups,
        (slots, attended, out_full, tok, small, small_t, residual, route, cot),
        scratch=[pltpu.VMEM((groups * MOST, width), BF)] * 2,
        name="route",
        micros=5,
    )
    received, other_low, other_high = exchange(sends)
    if packed:
        far, near = lax.optimization_barrier((far, near, low_two))[:2]
        onward = along(far, OUTWARD)
        middle = along(after(part, far), MIDDLE)
        inner = jnp.logical_or(major == 1, major == 2).astype(jnp.int32)
        places = jnp.stack([major, major ^ 1, major ^ 2, major ^ 3, inner])
        weights = (part, near, far, middle, onward)
        weights += (down, down_near, down_far, down_middle, down_onward)
        grads = [shaped((part.shape[0] + 3 * 256, 256), BF)] * 4
        room = [pltpu.VMEM((width, 2 * units), BF), pltpu.VMEM((units, width), BF)]
    else:
        places = just_minor
        weights = (gate_up_half, down_half)
        grads = [shaped((width, 2 * units), BF), shaped((units, width), BF)]
        room = []
    rows_total = 2 * groups * MOST
    results = call(
        functools.partial(expert_kernel, groups=groups, hidden_units=units, packed=packed),
        [shaped((groups * MOST, width), F32)] * 2 + [shaped((groups * MOST, width), BF)] * 2 + grads,
        (places,) + tuple(received) + (other_low, other_high) + weights,
        scratch=[pltpu.VMEM((rows_total, width), BF)] * 2
        + [pltpu.VMEM((rows_total, width), F32)] * 2
        + [pltpu.VMEM((rows_total, units), BF), pltpu.VMEM((rows_total, 2 * units), BF)]
        + room,
        name="expert",
        micros=18,
    )
    own_low, own_high, part_low, part_high = results[:4]
    grads = results[4:]
    high = (own_high + swap(part_high, "fsdp", 1).astype(F32)).astype(BF)
    low = (own_low + swap(part_low, "fsdp", 1).astype(F32)).astype(BF)
    backs = exchange_back(low, high, groups)

    if packed:
        first = along(grads[3], INWARD)
        sent = added(grads[2], first)
        up, down_way = along(sent, UP[:2]), along(sent, DOWN[:2])
        backs[0] = after(backs[0], sent)
    else:
        scatter = lambda v: lax.psum_scatter(
            v,
            "fsdp",
            scatter_dimension=0,
            tiled=True,
            axis_index_groups=minor_groups(major_count),
        ).astype(F32)
        shard_down = scatter(grads[1])
        part = scatter(grads[0]).reshape(2, shard_rows, FF)
        away = lax.dynamic_index_in_dim(part, 1 - minor, 0, False).astype(BF)
        kept = lax.dynamic_index_in_dim(part, minor, 0, False)
        arrived = swap(away, "fsdp", 1).astype(F32)
        first = jnp.where(minor == 0, kept, arrived).reshape(shard_rows, 2, major_count, 1, unit)
        second = jnp.where(minor == 0, arrived, kept).reshape(shard_rows, 2, major_count, 1, unit)
        shard_gate_up = jnp.concatenate([first, second], axis=3).reshape(shard_rows, 2 * FF)

    columns = (kinds, mix_at, value_at, gain_two_at, square_at)
    part_rows = width // 2 if packed else width
    out_part = shaped((part_rows, width + SMALL), BF)
    outputs, grad_hidden, grad_att, out_away, out_kept, grad_residual = call(
        functools.partial(
            combine_kernel, groups=groups, columns=columns, shard_rows=shard_rows, packed=packed
        ),
        [
            shaped((count, width), BF),
            shaped((count, width), F32),
            shaped((count, width), BF),
            out_part,
            out_part,
            shaped((kinds, count), BF),
        ],
        (slots,) + tuple(backs)
        + (hidden, low_two, cot, route, residual, small, small_t, out_full, attended),
        scratch=[pltpu.VMEM((groups * MOST, width), BF)] * 2
        + [pltpu.VMEM((width, width + SMALL), F32)],
        name="combine",
        micros=10,
    )
    head_half = pairs // 2
    back_where = jnp.stack([jnp.asarray(r, jnp.int32) for r in ranks] + [me_expert] + owners)

    def attend_back(part, grad_rows):
        base = part * head_half
        from_rows = pl.BlockSpec((count, PAIR), lambda h, w: (0, base + h))
        from_keys = pl.BlockSpec((length, PAIR), lambda h, w: (0, base + h))
        to_rows = pl.BlockSpec((count, PAIR), lambda h, w: (0, h))
        to_keys = pl.BlockSpec((length, PAIR), lambda h, w: (0, h))
        grads_part = shaped((part_rows, 3 * width // 2), BF)
        return call(
            functools.partial(attend_back_kernel, slots=groups, packed=packed),
            [
                shaped((count, width // 2), BF),
                shaped((length, width // 2), BF),
                shaped((length, width // 2), BF),
                grads_part,
                grads_part,
            ],
            (back_where, q, k_all, v_all, grad_rows, attend_weights, cosine, sine, normed, normed),
            grid=(head_half,),
            in_specs=[
                from_rows,
                from_keys,
                from_keys,
                from_rows,
                pl.BlockSpec((1, length, 2 * count), lambda h, w: (base + h, 0, 0)),
                pl.BlockSpec((length, PAIR), fixed),
                pl.BlockSpec((length, PAIR), fixed),
                pl.BlockSpec((width, length), fixed),
                pl.BlockSpec((width, count), lambda h, w: (0, w[groups])),
            ],
            out_specs=[
                to_rows,
                to_keys,
                to_keys,
                pl.BlockSpec(grads_part.shape, fixed),
                pl.BlockSpec(grads_part.shape, fixed),
            ],
            scratch=[pltpu.VMEM((width, 3 * width // 2), F32)],
            name="attend_back",
            micros=11,
        )

    dq_a, dk_a, dv_a, a_away, a_kept = attend_back(0, grad_att)
    if packed:
        a_away, a_kept, out_kept = lax.optimization_barrier(
            (a_away, a_kept, out_kept, up, down_way)
        )[:3]
        up = along(added(jnp.where(major == 1, grads[3], grads[1]), up), UP)
        down_way = along(added(jnp.where(major == 2, grads[3], grads[1]), down_way), DOWN)
        out_both = added(out_kept, swap(out_away, "expert", 1))
        a_both = added(a_kept, swap(a_away, "expert", 1))
        grad_att = after(grad_att, a_both, out_both)
    dq_b, dk_b, dv_b, b_away, b_kept = attend_back(1, grad_att)
    def project_back(dq_late):
        half_rows = pl.BlockSpec((count, width // 2), fixed)
        half_keys = pl.BlockSpec((count, width // 2), at_rank)
        return call(
            functools.partial(project_back_kernel, slots=groups),
            [shaped((length, width), BF), shaped((count, width), F32)],
            (back_where, dq_a, dq_late, dk_a, dk_b, dv_a, dv_b, qkv_full),
            grid=(groups,),
            in_specs=[half_rows] * 2 + [half_keys] * 4 + [pl.BlockSpec((width, 3 * width), fixed)],
            out_specs=[pl.BlockSpec((count, width), at_rank), pl.BlockSpec((count, width), fixed)],
            name="project_back",
            micros=6,
        )

    if packed:
        out_sum, a_sum = along_chips(out_both, (b_kept,)), along_chips(a_both, (b_kept,))
        b_both = added(b_kept, swap(b_away, "expert", 1))
        dq_b = after(dq_b, b_both)
        b_sum = along_chips(b_both, ())
        parts_all = jnp.concatenate([a_sum, b_sum, out_sum], axis=1)
        rows_back, own_back = project_back(dq_b)
        pieces = across_major(
            after(parts_all, rows_back, up, down_way), shard_rows // 4
        )
        own_grads = after(grads[0], pieces[1])
        away, kept, shard_down = call(
            sum_parts_kernel,
            [
                shaped((8 * shard_rows, 256), BF),
                shaped((8 * shard_rows, 256), F32),
                shaped((256, width), F32),
            ],
            (just_minor, own_grads, up, down_way),
            name="sum_parts",
            micros=3,
        )
        shard_gate_up = call(
            unpack_kernel,
            shaped((shard_rows, 2 * FF), F32),
            (just_minor, kept, swap(away, "fsdp", 1)),
            name="unpack_expert",
            micros=2,
        )
    else:
        both = jnp.concatenate([a_kept, b_kept, out_kept], axis=1)
        both = lax.psum_scatter(both, "fsdp", scatter_dimension=0, tiled=True)
        total = lax.psum(both, "expert")
        other = total
        rows_back, own_back = project_back(dq_b)
    rows_sum = sequence_scatter_sum(rows_back, count)
    grad_tokens = call(
        functools.partial(finish_kernel, gain_at=gain_one_at),
        shaped((count, width), BF),
        (just_minor, tok, small_t, grad_hidden, own_back, rows_sum),
        name="finish",
        micros=3,
    )

    if packed:
        total = summed_up(pieces[:3] + [after(pieces[3], away)])
        total = jnp.concatenate([total, swap(total, "expert", 2)], axis=0)
        other = swap(total, "expert", 1)
    shared_grads = call(
        functools.partial(
            shared_kernel, columns=columns, width=width, entries=length * width, packed=packed
        ),
        [
            shaped((shard_rows, 3 * width), F32),
            shaped((shard_rows, width), F32),
            shaped((kinds, shard_rows), F32),
            shaped((2 * NCONST, shard_rows), F32),
            shaped((NCONST, shard_rows), F32),
            shaped((1, shard_rows), F32),
            shaped((1, shard_rows), F32),
            shaped((1, 2), F32),
        ],
        (jnp.stack([me_expert]), total, other, qkv_weight, gain_one[None]),
        scratch=[pltpu.VMEM((shard_rows, 4 * width + SMALL), F32)],
        name="shared_grads",
        micros=3,
    )
    grad_qkv, grad_out, grad_router, grad_gate, grad_value, grad_one, grad_two, stream = shared_grads
    return (
        outputs[None],
        grad_tokens[None],
        grad_one[0],
        grad_qkv,
        grad_out,
        grad_two[0],
        grad_router.T,
        grad_gate.T,
        grad_value.T,
        shard_gate_up[None],
        shard_down[None],
        grad_residual.T[None],
        stream,
    )


def solution(mesh):
    return jax.shard_map(
        on_device,
        mesh=mesh,
        in_specs=(
            P("fsdp", "expert", None),
            P("fsdp"),
            P("fsdp", None),
            P("fsdp", None),
            P("fsdp"),
            P("fsdp", None),
            P("fsdp", None),
            P("fsdp", None),
            P("expert", "fsdp", None),
            P("expert", "fsdp", None),
            P("fsdp", "expert", None),
            P("fsdp", "expert", None),
            P("fsdp", "expert", None),
        ),
        out_specs=(
            P("fsdp", "expert", None),
            P("fsdp", "expert", None),
            P("fsdp"),
            P("fsdp", None),
            P("fsdp", None),
            P("fsdp"),
            P("fsdp", None),
            P("fsdp", None),
            P("fsdp", None),
            P("expert", "fsdp", None),
            P("expert", "fsdp", None),
            P("fsdp", "expert", None),
            P("fsdp", None),
        ),
        check_vma=False,
    )
```

```python
import functools

import jax
import jax.numpy as jnp
from jax import lax
from jax.experimental import pallas as pl
from jax.experimental.pallas import tpu as pltpu
from jax.sharding import PartitionSpec as P

HEAD = 64
FF = 2048
NCONST = 2
MOST = 80
PAIR = 2 * HEAD
SMALL = 128

epsilon = 1e-06
masked_score = -1e30
BF = jnp.bfloat16
F32 = jnp.float32


def mm(a, b):
    return jnp.dot(a, b, preferred_element_type=F32)


def mm_nt(a, b):
    return lax.dot_general(a, b, (((1,), (1,)), ((), ())), preferred_element_type=F32)


def mm_tn(a, b):
    return lax.dot_general(a, b, (((0,), (0,)), ((), ())), preferred_element_type=F32)


def split_low(values):
    high = values.astype(BF)
    return high, (values - high.astype(F32)).astype(BF)


def lanes(shape):
    return lax.broadcasted_iota(jnp.int32, shape, len(shape) - 1)


def rows_of(shape):
    return lax.broadcasted_iota(jnp.int32, shape, 0)


def rms_scale(values):
    return lax.rsqrt(jnp.mean(values * values, axis=-1, keepdims=True) + epsilon)


def turned(values, cosine, sine):
    lane = lanes(values.shape) % HEAD
    swapped = jnp.where(
        lane < HEAD // 2,
        pltpu.roll(values, PAIR - HEAD // 2, 1),
        pltpu.roll(values, HEAD // 2, 1),
    )
    return values * cosine + swapped * sine


def call(kernel, outs, args, grid=(), in_specs=None, out_specs=None, scratch=(), scalars=1, name=None, micros=2):
    whole = pl.BlockSpec(memory_space=pltpu.VMEM)
    multi = isinstance(outs, (tuple, list))
    if in_specs is None:
        in_specs = [whole] * (len(args) - scalars)
    if out_specs is None:
        out_specs = [whole] * len(outs) if multi else whole
    return pl.pallas_call(
        kernel,
        out_shape=outs,
        grid_spec=pltpu.PrefetchScalarGridSpec(
            num_scalar_prefetch=scalars,
            grid=grid,
            in_specs=in_specs,
            out_specs=out_specs,
            scratch_shapes=list(scratch),
        ),
        compiler_params=pltpu.CompilerParams(vmem_limit_bytes=56 * 1024 * 1024),
        cost_estimate=pl.CostEstimate(
            flops=micros * 90_000_000, transcendentals=0, bytes_accessed=micros * 300_000
        ),
        name=name,
    )(*args)


def shaped(shape, dtype):
    return jax.ShapeDtypeStruct(shape, dtype)


def swap(values, axis, bits):
    size = lax.axis_size(axis)
    return lax.ppermute(values, axis, [(i, i ^ bits) for i in range(size)])


def along(values, pairs):
    return lax.ppermute(
        values, "fsdp", [(2 * i + b, 2 * j + b) for i, j in pairs for b in (0, 1)]
    )


def after(values, *others):
    return lax.optimization_barrier((values,) + tuple(others))[0]


FAR = ((0, 2), (2, 0), (1, 3), (3, 1))
NEAR = ((0, 1), (1, 0), (2, 3), (3, 2))
MIDDLE = ((1, 2), (2, 1))
OUTWARD = ((2, 3), (1, 0))
INWARD = ((0, 1), (3, 2))


def minor_groups(major):
    return [[2 * i + b for i in range(major)] for b in (0, 1)]


def blocks_kernel(where, gate_up, out):
    rows = gate_up.shape[0]
    for block in range(8):
        at = (2 * block + 1 - where[0]) * 256
        out[block * rows : (block + 1) * rows, :] = gate_up[:, pl.ds(pl.multiple_of(at, 256), 256)]


def pack_kernel(where, gate_up, arrived, out):
    rows = gate_up.shape[0]
    mine = where[0]
    for block in range(8):
        at = (2 * block + mine) * 256
        own = pl.ds(pl.multiple_of(2 * block * rows + mine * rows, rows), rows)
        other = pl.ds(pl.multiple_of(2 * block * rows + (1 - mine) * rows, rows), rows)
        out[own, :] = gate_up[:, pl.ds(pl.multiple_of(at, 256), 256)]
        out[other, :] = arrived[block * rows : (block + 1) * rows, :]


def sum_parts_kernel(where, a, b, c, d0, d1, d2, away, kept, down):
    rows = away.shape[0] // 8
    mine = where[0]

    def total(start, size, d, base):
        source, shifted = pl.ds(start, size), pl.ds(start - base, size)
        return (
            a[source, :].astype(F32)
            + b[source, :].astype(F32)
            + c[source, :].astype(F32)
            + d[shifted, :].astype(F32)
        )

    for block in range(8):
        here = slice(block * rows, (block + 1) * rows)
        base = 2 * block * rows
        d, cut = ((d0, 0), (d1, 8 * rows), (d2, 14 * rows))[(block > 3) + (block > 6)]
        own = pl.multiple_of(base + mine * rows, rows)
        other = pl.multiple_of(base + (1 - mine) * rows, rows)
        away[here, :] = total(other, rows, d, cut).astype(BF)
        kept[here, :] = total(own, rows, d, cut)
    for block in range(3):
        base = 16 * rows + block * 256
        down[:, block * 256 : (block + 1) * 256] = total(base, 256, d2, 14 * rows)


def unpack_kernel(where, kept, arrived, out):
    rows = out.shape[0]
    mine = where[0]
    for block in range(8):
        here = slice(block * rows, (block + 1) * rows)
        own = pl.ds(pl.multiple_of((2 * block + mine) * 256, 256), 256)
        other = pl.ds(pl.multiple_of((2 * block + 1 - mine) * 256, 256), 256)
        out[:, own] = kept[here, :]
        out[:, other] = arrived[here, :].astype(F32)


def shared_pack(qkv, out, small):
    core = lax.axis_index("expert") % 2
    half_qkv, half_out = qkv.shape[1] // 2, out.shape[1] // 2
    rows = qkv.shape[0]

    def kernel(where, qkv_ref, out_ref, *refs):
        small_refs, (packed, room) = refs[:-2], refs[-2:]
        packed[:, :half_qkv] = qkv_ref[:, pl.ds(pl.multiple_of(where[0] * half_qkv, 128), half_qkv)]
        packed[:, half_qkv : half_qkv + half_out] = out_ref[
            :, pl.ds(pl.multiple_of(where[0] * half_out, 128), half_out)
        ]
        room[...] = jnp.zeros_like(room)
        at = 0
        for ref in small_refs:
            room[at : at + ref.shape[0], : ref.shape[1]] = ref[...].astype(F32)
            at += ref.shape[0]
        packed[:, half_qkv + half_out :] = room[...].astype(BF)

    return call(
        kernel,
        shaped((rows, half_qkv + half_out + SMALL), BF),
        (jnp.stack([core]).astype(jnp.int32), qkv, out) + small,
        scratch=[pltpu.VMEM((rows, SMALL), F32)],
        name="pack_shared",
        micros=1,
    )


def shared_gather(mine, down, early, late):
    me = lax.axis_index("fsdp")
    major = [mine, swap(mine, "fsdp", 2), swap(mine, "fsdp", 4)]
    minor = [swap(mine, "fsdp", 1)]
    major.append(swap(after(mine, minor[0]), "fsdp", 6))
    minor.append(swap(after(major[1], minor[0]), "fsdp", 1))
    minor.append(swap(after(major[2], *early), "fsdp", 1))
    minor.append(swap(after(major[3], minor[1], *late), "fsdp", 1))
    down_near = along(after(down, major[3]), NEAR)
    down_far = along(after(down, major[3]), FAR)
    slots = [2 * j for j in range(4)] + [2 * j + 1 for j in range(4)]
    own = after(jnp.concatenate(major + minor, axis=0), down_near, down_far)
    return own, swap(own, "expert", 1), [me ^ s for s in slots], down_near, down_far


def added(kept, arrived):
    return (kept.astype(F32) + arrived.astype(F32)).astype(BF)


def along_chips(both, gate):
    for axis, bits in (("expert", 2), ("fsdp", 1)):
        half = both.shape[0] // 2
        both = added(after(both[:half], *gate), swap(both[half:], axis, bits))
        gate = ()
    return both


def across_major(parts, rows):
    pieces = [swap(parts[j * rows : (j + 1) * rows], "fsdp", 2 * j) for j in (1, 2, 3)]
    total = parts[:rows].astype(F32)
    for piece in pieces:
        total += piece.astype(F32)
    return total.astype(BF), pieces[0]


def sequence_gather(values, across):
    size = lax.axis_size("expert")
    me = lax.axis_index("expert")
    if size != 4:
        every = lax.all_gather(values, "expert", axis=0, tiled=True)
        middle = every.shape[0] // 2
        return every[:middle], every[middle:], list(range(size))
    pair = jnp.concatenate([values, across], axis=0)
    return pair, swap(pair, "expert", 1), [me, me ^ 2, me ^ 1, me ^ 3]


def exchange(sends):
    half = len(sends) // 2
    received = [swap(v, "expert", j) if j else v for j, v in enumerate(sends)]
    low = swap(jnp.concatenate(received[:half], axis=0), "fsdp", 1)
    high = swap(after(jnp.concatenate(received[half:], axis=0), low), "fsdp", 1)
    return received, low, high


def exchange_back(low, high, size):
    rows = 2 * low.shape[0] // size
    if size == 4:
        upper = swap(high, "expert", 2)
        joined = swap(jnp.concatenate([low[rows:], upper[rows:]], axis=0), "expert", 1)
        return [low[:rows], joined[:rows], upper[:rows], joined[rows:]]
    pieces = [w[i : i + rows] for w in (low, high) for i in range(0, w.shape[0], rows)]
    return [swap(piece, "expert", j) if j else piece for j, piece in enumerate(pieces)]


def sequence_scatter_sum(full, rows):
    size = lax.axis_size("expert")
    me = lax.axis_index("expert")
    if size != 4:
        return lax.psum_scatter(full, "expert", scatter_dimension=0, tiled=True).astype(F32)

    def block(bits):
        return lax.dynamic_slice_in_dim(full, (me ^ bits) * rows, rows, 0)

    away = jnp.concatenate([block(1), block(3)], axis=0)
    kept = jnp.concatenate([block(0), block(2)], axis=0)
    both = kept.astype(F32) + swap(away, "expert", 1).astype(F32)
    return both[:rows] + swap(both[rows:].astype(BF), "expert", 2).astype(F32)


def project_kernel(where, *refs, slots, gain_at, placed):
    if placed:
        tok_a, tok_b, cosine, sine, weight, small_t, q, k, v, normed = refs
    else:
        tok_a, tok_b, cosine, sine, own_ref, other_ref = refs[:6]
        q, k, v, normed, weight, out_ref, small_ref, small_t = refs[6:]
    step = pl.program_id(0)
    rank = where[step]
    own = where[slots]
    width = tok_a.shape[1]

    if not placed:

        @pl.when(step == 0)
        def _():
            first = where[slots + 9] == 0
            rows = width // 8
            half_qkv, half_out = 3 * width // 2, width // 2
            for index in range(8):
                source = pl.ds(index * rows, rows)
                target = pl.ds(pl.multiple_of(where[slots + 1 + index] * rows, rows), rows)
                a, b = own_ref[source, :], other_ref[source, :]
                left = jnp.where(first, a, b)
                right = jnp.where(first, b, a)
                weight[target, :half_qkv] = left[:, :half_qkv]
                weight[target, half_qkv:] = right[:, :half_qkv]
                out_ref[target, :half_out] = left[:, half_qkv : half_qkv + half_out]
                out_ref[target, half_out:] = right[:, half_qkv : half_qkv + half_out]
                of_rows = jnp.zeros((SMALL, SMALL), F32)
                of_rows = jnp.concatenate(
                    [a[:32, half_qkv + half_out :].astype(F32), of_rows[32:]], axis=0
                ).T
                small_ref[target, :] = of_rows[:rows].astype(BF)
            small_t[...] = small_ref[...].astype(F32).T[:32]

    @pl.when(rank > own)
    def _():
        k[...] = jnp.zeros_like(k)
        v[...] = jnp.zeros_like(v)
        normed[...] = jnp.zeros_like(normed)

    @pl.when(rank <= own)
    def _():
        x = jnp.where(step < slots // 2, tok_a[...], tok_b[...]).astype(F32)
        wide = (x * rms_scale(x)) * small_t[gain_at : gain_at + 1, :]
        low = wide.astype(BF)
        normed[...] = low.T
        cos, sin = cosine[...], sine[...]
        keys = mm(low, weight[:, width : 2 * width])
        for at in range(0, width, PAIR):
            k[:, at : at + PAIR] = turned(keys[:, at : at + PAIR], cos, sin).astype(BF)
        v[...] = mm(low, weight[:, 2 * width :]).astype(BF)

        @pl.when(rank == own)
        def _():
            queries = mm(low, weight[:, :width])
            for at in range(0, width, PAIR):
                q[:, at : at + PAIR] = turned(queries[:, at : at + PAIR], cos, sin).astype(BF)


def stacked_heads(values, scale=None):
    lane = lanes(values.shape)
    if scale is not None:
        values = values * jnp.asarray(scale, values.dtype)
    zero = jnp.zeros_like(values)
    return jnp.concatenate(
        [jnp.where(lane < HEAD, values, zero), jnp.where(lane < HEAD, zero, values)], axis=0
    )


def visible_keys(own, keys, count):
    key = lax.broadcasted_iota(jnp.int32, (keys, 2 * count), 0)
    query = lax.broadcasted_iota(jnp.int32, (keys, 2 * count), 1) % count
    return key <= query + own * count


def attend_kernel(where, q, k, v, attended, kept, *, slots):
    own = where[slots]
    count, keys = q.shape[0], k.shape[0]
    query = stacked_heads(q[...], HEAD ** (-0.5))
    scores = mm_nt(k[...], query)
    scores = jnp.where(visible_keys(own, keys, count), scores, masked_score)
    top = jnp.max(scores, axis=0, keepdims=True)
    weights = jnp.exp(scores - top)
    total = jnp.sum(weights, axis=0, keepdims=True)
    weights = (weights * (1.0 / total)).astype(BF)
    kept[0] = weights
    both = mm_tn(v[...], weights).T
    lane = lanes((count, PAIR))
    attended[...] = jnp.where(lane < HEAD, both[:count], both[count:]).astype(BF)


def attend_back_kernel(where, q, k, v, grad_att, kept_weights, cosine, sine, normed, normed_own, dq, dk, dv, away, kept, sums, *, slots, packed):
    step = pl.program_id(0)
    own = where[slots]
    count = q.shape[0]
    query = stacked_heads(q[...], HEAD ** (-0.5))
    grad_rows = stacked_heads(grad_att[...])
    key_rows = k[...]
    low_weights = kept_weights[0]
    weights = low_weights.astype(F32)
    grad_weights = mm_nt(v[...], grad_rows)
    delta = jnp.sum(weights * grad_weights, axis=0, keepdims=True)
    grad_scores = (weights * (grad_weights - delta)).astype(BF)
    grad_v = mm(low_weights, grad_rows).astype(BF)
    dv[...] = grad_v
    grad_k = turned(mm(grad_scores, query), cosine[...], -sine[...]).astype(BF)
    dk[...] = grad_k
    both = mm_tn(key_rows, grad_scores).T
    lane = lanes((count, PAIR))
    grad_q = jnp.where(lane < HEAD, both[:count], both[count:]) * HEAD ** (-0.5)
    mine = pl.ds(pl.multiple_of(own * count, count), count)
    grad_q = turned(grad_q, cosine[mine, :], -sine[mine, :]).astype(BF)
    dq[...] = grad_q
    of_keys = mm(normed[...], jnp.concatenate([grad_k, grad_v], axis=1))
    of_queries = mm(normed_own[...], grad_q)
    steps = kept.shape[1] // (3 * PAIR)
    for index in range(steps):

        @pl.when(step == index)
        def _():
            for part, values in enumerate((of_queries, of_keys[:, :PAIR], of_keys[:, PAIR:])):
                at = (part * steps + index) * PAIR
                sums[:, at : at + PAIR] = values

    @pl.when(step == steps - 1)
    def _():
        if packed:
            split_rows(where, slots + 1, sums, away, kept)
        else:
            kept[...] = sums[...].astype(BF)
            away[...] = jnp.zeros_like(away)


def split_rows(where, at, values, away, kept):
    core, chip = where[at + 8], where[at + 9]
    rows = values.shape[0] // 32
    for index in range(0, 16, 2):
        target = slice(index * rows, (index + 2) * rows)
        for ref, side in ((kept, core), (away, 1 - core)):
            pieces = []
            for step in (index, index + 1):
                rank = 2 * (chip ^ (step // 8)) + side
                base = (where[at + step % 8] * 4 + rank) * rows
                pieces.append(values[pl.ds(pl.multiple_of(base, 8), rows), :])
            ref[target, :] = jnp.concatenate(pieces, axis=0).astype(BF)


def as_lanes(rows):
    rows = rows.astype(F32)
    spare = jnp.zeros((SMALL - rows.shape[0], rows.shape[1]), F32)
    return jnp.concatenate([rows, spare], axis=0).T


def routing(routes, resid, logits, groups):
    count = routes.shape[0]
    lane = lanes((count, SMALL))
    logits = logits + resid
    hot, picked = [], []
    for choice in range(2):
        route = routes[:, choice : choice + 1]
        hot.append(lane == route)
        picked.append(jnp.sum(jnp.where(hot[choice], logits, 0.0), axis=-1, keepdims=True))
    top = jnp.maximum(picked[0], picked[1])
    first, second = jnp.exp(picked[0] - top), jnp.exp(picked[1] - top)
    gates = [first / (first + second), second / (first + second)]
    named = jnp.logical_or(hot[0], hot[1]).astype(BF)
    earlier = (lanes((count, count)) < rows_of((count, count))).astype(BF)
    place = mm(earlier, named)
    dispatch = []
    column = lanes((count, groups * MOST))
    for choice in range(2):
        route = routes[:, choice : choice + 1]
        slot = jnp.sum(jnp.where(hot[choice], place, 0.0), axis=-1, keepdims=True)
        target = jnp.where(route < groups, route * MOST + slot.astype(jnp.int32), -1)
        dispatch.append((column == target).astype(BF))
    return gates, hot, dispatch


def route_kernel(where, att, out_weight, tok, small, small_t, resid, routes, cot, hidden_ref, low_ref, *rest, groups, gain_at):
    sends = rest[:groups]
    rows_x, rows_g = rest[groups], rest[groups + 1]
    hidden = tok[...].astype(F32) + mm(att[...], out_weight[...])
    hidden_ref[...] = hidden
    low = ((hidden * rms_scale(hidden)) * small_t[gain_at : gain_at + 1, :]).astype(BF)
    low_ref[...] = low
    logits = mm(low, small[...])
    route = as_lanes(routes[...])[:, :2].astype(jnp.int32)
    gates, _, dispatch = routing(route, as_lanes(resid[...]), logits, groups)
    grad = cot[...].astype(F32)
    rows_x[...] = mm_tn(dispatch[0] + dispatch[1], low).astype(BF)
    rows_g[...] = (
        mm_tn(dispatch[0], (gates[0] * grad).astype(BF))
        + mm_tn(dispatch[1], (gates[1] * grad).astype(BF))
    ).astype(BF)
    for slot in range(groups):
        source = pl.ds(pl.multiple_of(where[slot] * MOST, MOST), MOST)
        sends[slot][:MOST, :] = rows_x[source, :]
        sends[slot][MOST:, :] = rows_g[source, :]


def expert_kernel(where, *refs, groups, hidden_units, packed):
    refs = list(refs)

    def take(amount):
        taken = refs[:amount]
        del refs[:amount]
        return taken

    received = take(groups) + take(2)
    if packed:
        unit_parts, down_parts = take(5), take(5)
    else:
        gate_up, down = take(2)
    own_out, other_out = take(2), take(2)
    if packed:
        messages = take(4)
    else:
        grad_gate_up, grad_down = take(2)
    rows, grads, out_rows, back_rows, acts, grad_units = take(6)
    if packed:
        gate_up, down, rows_t = take(3)
    width = rows.shape[1]
    total = 2 * groups * MOST
    index = 0
    for ref in received:
        for base in range(0, ref.shape[0], 2 * MOST):
            target = slice(index * MOST, (index + 1) * MOST)
            rows[target, :] = ref[base : base + MOST, :]
            grads[target, :] = ref[base + MOST : base + 2 * MOST, :]
            index += 1
    if packed:
        part = width // 4

        def place(slot, ref, down_ref):
            target = pl.ds(pl.multiple_of(where[slot] * part, part), part)
            for block in range(8):
                gate_up[target, block * 256 : (block + 1) * 256] = ref[
                    block * part : (block + 1) * part, :
                ]
            down[pl.ds(pl.multiple_of(where[slot] * 256, 256), 256), :] = down_ref[...]

        for slot in range(3):
            place(slot, unit_parts[slot], down_parts[slot])

        @pl.when(where[4] == 1)
        def _():
            place(3, unit_parts[3], down_parts[3])

        @pl.when(where[4] == 0)
        def _():
            place(3, unit_parts[4], down_parts[4])

    x, g = rows[...], grads[...]
    chunk = 256
    out_rows[...] = jnp.zeros_like(out_rows)
    back_rows[...] = jnp.zeros_like(back_rows)

    def forward_back(step, carry):
        first = pl.ds(pl.multiple_of(step * chunk, chunk), chunk)
        second = pl.ds(pl.multiple_of(hidden_units + step * chunk, chunk), chunk)
        gate_w, up_w, down_w = gate_up[:, first], gate_up[:, second], down[first, :]
        gate, up = mm(x, gate_w), mm(x, up_w)
        sig = 1.0 / (1.0 + jnp.exp(-gate))
        silu = gate * sig
        act = (silu * up).astype(BF)
        acts[:, first] = act
        grad_act = mm_nt(g, down_w)
        grad_gate = (grad_act * up * sig * (1.0 + gate * (1.0 - sig))).astype(BF)
        grad_up = (grad_act * silu).astype(BF)
        grad_units[:, first] = grad_gate
        grad_units[:, second] = grad_up
        out_rows[...] += mm(act, down_w)
        back_rows[...] += mm_nt(grad_gate, gate_w) + mm_nt(grad_up, up_w)
        return carry

    lax.fori_loop(0, hidden_units // chunk, forward_back, 0)
    index = 0
    for ref in own_out + other_out:
        for base in range(0, ref.shape[0], 2 * MOST):
            source = slice(index * MOST, (index + 1) * MOST)
            ref[base : base + MOST, :] = out_rows[source, :].astype(ref.dtype)
            ref[base + MOST : base + 2 * MOST, :] = back_rows[source, :].astype(ref.dtype)
            index += 1
    if not packed:
        grad_gate_up[...] = mm_tn(x, grad_units[...]).astype(BF)
        grad_down[...] = mm_tn(acts[...], g).astype(BF)
        return
    part = width // 4

    def weight_grad(step, carry):
        block = pl.ds(pl.multiple_of(step * 512, 512), 512)
        gate_up[:, block] = mm(rows_t[...], grad_units[:, block]).astype(BF)
        return carry

    rows_t[...] = x.T
    lax.fori_loop(0, 4, weight_grad, 0)
    for slot, ref in enumerate(messages):
        source = pl.ds(pl.multiple_of(where[slot] * part, part), part)
        for block in range(8):
            ref[block * part : (block + 1) * part, :] = gate_up[
                source, block * 256 : (block + 1) * 256
            ]
        mine = acts[:, pl.ds(pl.multiple_of(where[slot] * 256, 256), 256)]
        of_down = mm_tn(mine, g).astype(BF)
        for block in range(3):
            base = 8 * part + block * 256
            ref[base : base + 256, :] = of_down[:, block * 256 : (block + 1) * 256]


def combine_kernel(where, *refs, groups, columns, shard_rows, packed):
    backs = refs[:groups]
    (hidden_ref, low_ref, cot, routes, resid, small, small_t, out_weight, att,
     out_ref, grad_hidden_ref, grad_att_ref, grad_away, grad_kept, grad_resid,
     rows_y, rows_d, sums) = refs[groups:]
    kinds, mix_at, value_at, gain_two_at, square_at = columns
    for slot in range(groups):
        target = pl.ds(pl.multiple_of(where[slot] * MOST, MOST), MOST)
        rows_y[target, :] = backs[slot][:MOST, :]
        rows_d[target, :] = backs[slot][MOST:, :]
    hidden, low = hidden_ref[...], low_ref[...]
    count = low.shape[0]
    normed_input = low.astype(F32)
    grad_low_type = cot[...]
    grad = grad_low_type.astype(F32)
    logits = mm(low, small[...])
    grad_small_dot = mm(grad_low_type, small[...])
    route = as_lanes(routes[...])[:, :2].astype(jnp.int32)
    gates, hot, dispatch = routing(route, as_lanes(resid[...]), logits, groups)
    returned = [mm(dispatch[c], rows_y[...]) for c in range(2)]
    grad_back = mm(dispatch[0] + dispatch[1], rows_d[...])
    grad_dot = jnp.sum(grad * normed_input, axis=-1, keepdims=True)
    is_copy = [(route[:, c : c + 1] == groups + 1).astype(F32) for c in range(2)]
    grad_gates = [
        jnp.sum(grad * returned[c], axis=-1, keepdims=True) + is_copy[c] * grad_dot
        for c in range(2)
    ]
    direct = gates[0] * is_copy[0] + gates[1] * is_copy[1]
    mixture = gates[0] * returned[0] + gates[1] * returned[1]
    lane = lanes((count, SMALL))
    grad_logits = jnp.zeros((count, SMALL), F32)
    value_weights = jnp.zeros((count, SMALL), F32)
    for const in range(NCONST):
        first = logits[:, mix_at + 2 * const : mix_at + 2 * const + 1]
        second = logits[:, mix_at + 2 * const + 1 : mix_at + 2 * const + 2]
        top = jnp.maximum(first, second)
        first, second = jnp.exp(first - top), jnp.exp(second - top)
        mix = [first / (first + second), second / (first + second)]
        value_dot = grad_small_dot[:, value_at + const : value_at + const + 1]
        named = [(route[:, c : c + 1] == groups + 2 + const).astype(F32) for c in range(2)]
        for c in range(2):
            grad_gates[c] += named[c] * (mix[0] * grad_dot + mix[1] * value_dot)
        weight = gates[0] * named[0] + gates[1] * named[1]
        direct += weight * mix[0]
        of_value = weight * mix[1]
        mixture += of_value * small_t[value_at + const : value_at + const + 1, :]
        value_weights = jnp.where(lane == value_at + const, of_value, value_weights)
        grad_mix = [weight * grad_dot, weight * value_dot]
        common = mix[0] * grad_mix[0] + mix[1] * grad_mix[1]
        for c in range(2):
            grad_logits = jnp.where(
                lane == mix_at + 2 * const + c, mix[c] * (grad_mix[c] - common), grad_logits
            )
    outputs = hidden + mixture + direct * normed_input
    out_ref[...] = outputs.astype(BF)
    common = gates[0] * grad_gates[0] + gates[1] * grad_gates[1]
    for c in range(2):
        grad_logits = jnp.where(hot[c], gates[c] * (grad_gates[c] - common), grad_logits)
    grad_resid[...] = grad_logits.T[:kinds].astype(BF)
    high, rest = split_low(grad_logits)
    weights = small[...]
    grad_low = grad_back + direct * grad + mm_nt(high, weights) + mm_nt(rest, weights)
    scale = rms_scale(hidden)
    normed = hidden * scale
    of_gain = jnp.sum((grad_low * normed).reshape(-1, 8, normed.shape[1]), axis=0)
    of_gain = jnp.sum(of_gain, axis=0, keepdims=True)
    value_high, value_rest = split_low(value_weights)
    summed = mm_tn(low, jnp.concatenate([high, rest], axis=1))
    summed += mm_tn(grad_low_type, jnp.concatenate([value_high, value_rest], axis=1))
    summed = summed[:, :SMALL] + summed[:, SMALL:]
    wide = (SMALL, normed.shape[1])
    summed += jnp.where(rows_of(wide) == gain_two_at, of_gain, 0.0).T
    column, row = lanes(summed.shape), rows_of(summed.shape)
    mine = row // shard_rows == where[groups]
    for index, total in enumerate((jnp.sum(hidden * hidden), jnp.sum(outputs * outputs))):
        for part, value in enumerate(split_low(jnp.full((1, 1), total, F32))):
            spot = jnp.logical_and(mine, column == square_at + 2 * index + part)
            summed = jnp.where(spot, value.astype(F32), summed)
    grad_normed = grad_low * small_t[gain_two_at : gain_two_at + 1, :]
    grad_hidden = grad + scale * (
        grad_normed - normed * jnp.mean(grad_normed * normed, axis=-1, keepdims=True)
    )
    grad_hidden_ref[...] = grad_hidden
    branch = grad_hidden.astype(BF)
    grad_att_ref[...] = mm_nt(branch, out_weight[...]).astype(BF)
    width = branch.shape[1]
    sums[:, :width] = mm_tn(att[...], branch)
    sums[:, width:] = summed
    if packed:
        split_rows(where, groups + 1, sums, grad_away, grad_kept)
    else:
        grad_kept[...] = sums[...].astype(BF)
        grad_away[...] = jnp.zeros_like(grad_away)


def project_back_kernel(where, *refs, slots):
    queries, keys, values = refs[0:2], refs[2:4], refs[4:6]
    weight, rows_back, own_back = refs[6:]
    rank = where[pl.program_id(0)]
    own = where[slots]
    half = keys[0].shape[1]
    width = 2 * half

    def through(parts, base):
        result = mm_nt(parts[0][...], weight[:, base : base + half])
        return result + mm_nt(parts[1][...], weight[:, base + half : base + width])

    @pl.when(rank > own)
    def _():
        rows_back[...] = jnp.zeros_like(rows_back)

    @pl.when(rank <= own)
    def _():
        rows_back[...] = (through(keys, width) + through(values, 2 * width)).astype(BF)

        @pl.when(rank == own)
        def _():
            own_back[...] = through(queries, 0)


def finish_kernel(where, tok, small_t, grad_hidden, own_back, rows_back, out, *, gain_at):
    x = tok[...].astype(F32)
    scale = rms_scale(x)
    normed = x * scale
    grad = (own_back[...] + rows_back[...]) * small_t[gain_at : gain_at + 1, :]
    out[...] = (
        grad_hidden[...]
        + scale * (grad - normed * jnp.mean(grad * normed, axis=-1, keepdims=True))
    ).astype(BF)


def shared_kernel(where, total, other, weight, gain, qkv, out, router, gate, value, gain_one, gain_two, stream, room, *, columns, width, entries, packed):
    kinds, mix_at, value_at, gain_two_at, square_at = columns
    if packed:
        rows = room.shape[0] // 4
        for parts, rank in ((total, where[0]), (other, where[0] ^ 1)):
            both = parts[...].astype(F32)
            room[pl.ds(pl.multiple_of(rank * rows, 8), rows), :] = both[:rows]
            room[pl.ds(pl.multiple_of((rank ^ 2) * rows, 8), rows), :] = both[rows:]
    else:
        room[...] = total[...].astype(F32)
    values = room[...]
    half = width // 2
    for part in range(3):
        for side in range(2):
            at = (3 * side + part) * half
            to = part * width + side * half
            qkv[:, to : to + half] = values[:, at : at + half]
    out[...] = values[:, 3 * width : 4 * width]
    rows = values.shape[0]

    def as_columns(block):
        spare = jnp.zeros((SMALL - rows, SMALL), F32)
        return jnp.concatenate([block, spare], axis=0).T[:, :rows]

    small = values[:, 4 * width :]
    turned_small = as_columns(small)
    router[...] = turned_small[:kinds]
    gate[...] = turned_small[mix_at : mix_at + 2 * NCONST]
    value[...] = turned_small[value_at : value_at + NCONST]
    gain_two[...] = turned_small[gain_two_at : gain_two_at + 1]
    of_gain = jnp.sum(qkv[...] * weight[...].astype(F32), axis=-1, keepdims=True)
    gain_one[...] = as_columns(jnp.broadcast_to(of_gain, (rows, SMALL)))[:1] / gain[...].astype(F32)
    squares = small[:1, square_at : square_at + 4]
    hidden = squares[:, 0:1] + squares[:, 1:2]
    outputs = squares[:, 2:3] + squares[:, 3:4]
    stream[...] = jnp.sqrt(jnp.where(lanes((1, 2)) == 0, hidden, outputs) / entries)


def on_device(
    tokens,
    gain_one,
    qkv_weight,
    out_weight,
    gain_two,
    router_weight,
    const_gate,
    const_value,
    expert_gate_up,
    expert_down,
    gate_residual,
    routes,
    cotangent,
):
    parts = lax.axis_size("fsdp")
    groups = lax.axis_size("expert")
    me_fsdp = lax.axis_index("fsdp").astype(jnp.int32)
    me_expert = lax.axis_index("expert").astype(jnp.int32)
    minor, major, core = me_fsdp % 2, me_fsdp // 2, me_expert % 2
    packed = parts == 8 and groups == 4
    major_count = parts // 2
    tok = tokens[0]
    count, width = tok.shape
    length = groups * count
    pairs = width // PAIR
    kinds = router_weight.shape[1]
    mix_at, value_at = kinds, kinds + 2 * NCONST
    gain_one_at = value_at + NCONST
    gain_two_at = gain_one_at + 1
    square_at = gain_two_at + 1
    shard_rows = width // parts
    unit = FF // parts
    units = FF // 2
    fixed = lambda j, w: (0, 0)
    at_slot = lambda j, w: (j, 0)
    at_rank = lambda j, w: (w[j], 0)
    just_minor = jnp.stack([minor])

    small_parts = (router_weight.T, const_gate.T, const_value.T, gain_one[None], gain_two[None])
    frequency = 10000.0 ** (-jnp.arange(HEAD // 2, dtype=F32) / (HEAD // 2))
    angles = jnp.arange(length, dtype=F32)[:, None] * frequency[None, :]
    cosine, sine = jnp.cos(angles), jnp.sin(angles)
    cosine = jnp.concatenate([cosine, cosine, cosine, cosine], axis=1)
    sine = jnp.concatenate([-sine, sine, -sine, sine], axis=1)

    weight_args, order, across = (), [], None
    if packed:
        shared = shared_pack(qkv_weight, out_weight, small_parts)
        across = swap(tok, "expert", 2)
        tok_a, tok_b, ranks = sequence_gather(tok, across)
        away = call(
            blocks_kernel,
            shaped((8 * shard_rows, 256), BF),
            (just_minor, expert_gate_up[0]),
            name="blocks",
            micros=1,
        )
        arrived = swap(away, "fsdp", 1)
        part = call(
            pack_kernel,
            shaped((16 * shard_rows, 256), BF),
            (just_minor, expert_gate_up[0], arrived),
            name="pack_expert",
            micros=1,
        )
        down = expert_down[0]
        own_half, other_half, order, down_near, down_far = shared_gather(
            shared, down, (across, arrived), (part, tok_b, cosine, sine)
        )
        down_onward = along(down_far, OUTWARD)
        down_middle = along(after(down, down_far), MIDDLE)
        weight_args = (own_half, other_half)
        far, near = along(part, FAR), along(part, NEAR)
    else:
        qkv_full = lax.all_gather(qkv_weight, "fsdp", axis=0, tiled=True)
        out_full = lax.all_gather(out_weight, "fsdp", axis=0, tiled=True)
        small_rows = jnp.concatenate(small_parts, axis=0)
        small = lax.all_gather(small_rows, "fsdp", axis=1, tiled=True).T
        small = jnp.pad(small, ((0, 0), (0, SMALL - small.shape[1])))
        small_t = small.astype(F32).T[:32]
        weight_args = (qkv_full, small_t)
        halves = expert_gate_up[0].reshape(shard_rows, 2, major_count, 2, unit)
        away = lax.dynamic_index_in_dim(halves, 1 - minor, 3, False).reshape(shard_rows, FF)
        kept = lax.dynamic_index_in_dim(halves, minor, 3, False).reshape(shard_rows, FF)
        arrived = swap(away, "fsdp", 1)
        part = jnp.concatenate(
            [jnp.where(minor == 0, kept, arrived), jnp.where(minor == 0, arrived, kept)], axis=0
        )
        gather = functools.partial(
            lax.all_gather,
            axis_name="fsdp",
            axis=0,
            tiled=True,
            axis_index_groups=minor_groups(major_count),
        )
        gate_up_half, down_half = gather(part), gather(expert_down[0])
        tok_a, tok_b, ranks = sequence_gather(tok, across)
    where = jnp.stack(
        [jnp.asarray(r, jnp.int32) for r in ranks] + [me_expert] + order + [core]
    )

    half_columns = 2 * width + SMALL
    outs = [
        shaped((count, width), BF),
        shaped((length, width), BF),
        shaped((length, width), BF),
        shaped((width, length), BF),
    ]
    out_specs = [
        pl.BlockSpec((count, width), fixed),
        pl.BlockSpec((count, width), at_rank),
        pl.BlockSpec((count, width), at_rank),
        pl.BlockSpec((width, count), lambda j, w: (0, w[j])),
    ]
    if packed:
        weight_specs = [pl.BlockSpec((width, half_columns), fixed)] * 2
        outs += [
            shaped((width, 3 * width), BF),
            shaped((width, width), BF),
            shaped((width, SMALL), BF),
            shaped((32, width), F32),
        ]
        out_specs += [pl.BlockSpec(o.shape, fixed) for o in outs[4:]]
    else:
        weight_specs = [pl.BlockSpec((width, 3 * width), fixed), pl.BlockSpec((32, width), fixed)]
    projected = call(
        functools.partial(project_kernel, slots=groups, gain_at=gain_one_at, placed=not packed),
        outs,
        (where, tok_a, tok_b, cosine, sine) + weight_args,
        grid=(groups,),
        in_specs=[
            pl.BlockSpec((count, width), lambda j, w: (jnp.minimum(j, groups // 2 - 1), 0)),
            pl.BlockSpec((count, width), lambda j, w: (jnp.maximum(j - groups // 2, 0), 0)),
            pl.BlockSpec((count, PAIR), at_rank),
            pl.BlockSpec((count, PAIR), at_rank),
        ]
        + weight_specs,
        out_specs=out_specs,
        name="project",
        micros=10,
    )
    q, k_all, v_all, normed = projected[:4]
    if packed:
        qkv_full, out_full, small, small_t = projected[4:]
    head_rows = pl.BlockSpec((count, PAIR), lambda h, w: (0, h))
    head_keys = pl.BlockSpec((length, PAIR), lambda h, w: (0, h))
    attended, attend_weights = call(
        functools.partial(attend_kernel, slots=groups),
        [shaped((count, width), BF), shaped((pairs, length, 2 * count), BF)],
        (where, q, k_all, v_all),
        grid=(pairs,),
        in_specs=[head_rows, head_keys, head_keys],
        out_specs=[
            head_rows,
            pl.BlockSpec((1, length, 2 * count), lambda h, w: (h, 0, 0)),
        ],
        name="attend",
        micros=12,
    )

    residual, route, cot = gate_residual[0].T, routes[0].T, cotangent[0]
    if packed:
        attended = after(attended, down_onward, down_middle)
    owners = [me_fsdp ^ (2 * j + i) for i in (0, 1) for j in range(4)]
    owners += [core, me_expert // 2]
    slots = jnp.stack([me_expert ^ j for j in range(groups)] + [me_fsdp] + owners)
    block = shaped((2 * MOST, width), BF)
    hidden, low_two, *sends = call(
        functools.partial(route_kernel, groups=groups, gain_at=gain_two_at),
        [shaped((count, width), F32), shaped((count, width), BF)] + [block] * groups,
        (slots, attended, out_full, tok, small, small_t, residual, route, cot),
        scratch=[pltpu.VMEM((groups * MOST, width), BF)] * 2,
        name="route",
        micros=5,
    )
    received, other_low, other_high = exchange(sends)
    if packed:
        far, near = lax.optimization_barrier((far, near, low_two))[:2]
        onward = along(far, OUTWARD)
        middle = along(after(part, far), MIDDLE)
        inner = jnp.logical_or(major == 1, major == 2).astype(jnp.int32)
        places = jnp.stack([major, major ^ 1, major ^ 2, major ^ 3, inner])
        weights = (part, near, far, middle, onward)
        weights += (down, down_near, down_far, down_middle, down_onward)
        grads = [shaped((part.shape[0] + 3 * 256, 256), BF)] * 4
        room = [pltpu.VMEM((width, 2 * units), BF), pltpu.VMEM((units, width), BF)]
        room += [pltpu.VMEM((width, 2 * groups * MOST), BF)]
    else:
        places = just_minor
        weights = (gate_up_half, down_half)
        grads = [shaped((width, 2 * units), BF), shaped((units, width), BF)]
        room = []
    rows_total = 2 * groups * MOST
    results = call(
        functools.partial(expert_kernel, groups=groups, hidden_units=units, packed=packed),
        [shaped((groups * MOST, width), F32)] * 2 + [shaped((groups * MOST, width), BF)] * 2 + grads,
        (places,) + tuple(received) + (other_low, other_high) + weights,
        scratch=[pltpu.VMEM((rows_total, width), BF)] * 2
        + [pltpu.VMEM((rows_total, width), F32)] * 2
        + [pltpu.VMEM((rows_total, units), BF), pltpu.VMEM((rows_total, 2 * units), BF)]
        + room,
        name="expert",
        micros=18,
    )
    own_low, own_high, part_low, part_high = results[:4]
    grads = results[4:]
    high = (own_high + swap(part_high, "fsdp", 1).astype(F32)).astype(BF)
    low = (own_low + swap(part_low, "fsdp", 1).astype(F32)).astype(BF)
    backs = exchange_back(low, high, groups)

    if packed:
        first = along(grads[3], INWARD)
        middle = along(grads[3], MIDDLE)
        sent = added(grads[2], first)
        near = along(after(grads[1], first), NEAR)
        cuts = (0, 8 * shard_rows, 14 * shard_rows, sent.shape[0])
        far = [along(sent[a:b], FAR) for a, b in zip(cuts, cuts[1:])]
        backs[0] = after(backs[0], sent, middle)
    else:
        scatter = lambda v: lax.psum_scatter(
            v,
            "fsdp",
            scatter_dimension=0,
            tiled=True,
            axis_index_groups=minor_groups(major_count),
        ).astype(F32)
        shard_down = scatter(grads[1])
        part = scatter(grads[0]).reshape(2, shard_rows, FF)
        away = lax.dynamic_index_in_dim(part, 1 - minor, 0, False).astype(BF)
        kept = lax.dynamic_index_in_dim(part, minor, 0, False)
        arrived = swap(away, "fsdp", 1).astype(F32)
        first = jnp.where(minor == 0, kept, arrived).reshape(shard_rows, 2, major_count, 1, unit)
        second = jnp.where(minor == 0, arrived, kept).reshape(shard_rows, 2, major_count, 1, unit)
        shard_gate_up = jnp.concatenate([first, second], axis=3).reshape(shard_rows, 2 * FF)

    columns = (kinds, mix_at, value_at, gain_two_at, square_at)
    part_rows = width // 2 if packed else width
    out_part = shaped((part_rows, width + SMALL), BF)
    outputs, grad_hidden, grad_att, out_away, out_kept, grad_residual = call(
        functools.partial(
            combine_kernel, groups=groups, columns=columns, shard_rows=shard_rows, packed=packed
        ),
        [
            shaped((count, width), BF),
            shaped((count, width), F32),
            shaped((count, width), BF),
            out_part,
            out_part,
            shaped((kinds, count), BF),
        ],
        (slots,) + tuple(backs)
        + (hidden, low_two, cot, route, residual, small, small_t, out_full, attended),
        scratch=[pltpu.VMEM((groups * MOST, width), BF)] * 2
        + [pltpu.VMEM((width, width + SMALL), F32)],
        name="combine",
        micros=10,
    )
    head_half = pairs // 2
    back_where = jnp.stack([jnp.asarray(r, jnp.int32) for r in ranks] + [me_expert] + owners)

    def attend_back(part, grad_rows):
        base = part * head_half
        from_rows = pl.BlockSpec((count, PAIR), lambda h, w: (0, base + h))
        from_keys = pl.BlockSpec((length, PAIR), lambda h, w: (0, base + h))
        to_rows = pl.BlockSpec((count, PAIR), lambda h, w: (0, h))
        to_keys = pl.BlockSpec((length, PAIR), lambda h, w: (0, h))
        grads_part = shaped((part_rows, 3 * width // 2), BF)
        return call(
            functools.partial(attend_back_kernel, slots=groups, packed=packed),
            [
                shaped((count, width // 2), BF),
                shaped((length, width // 2), BF),
                shaped((length, width // 2), BF),
                grads_part,
                grads_part,
            ],
            (back_where, q, k_all, v_all, grad_rows, attend_weights, cosine, sine, normed, normed),
            grid=(head_half,),
            in_specs=[
                from_rows,
                from_keys,
                from_keys,
                from_rows,
                pl.BlockSpec((1, length, 2 * count), lambda h, w: (base + h, 0, 0)),
                pl.BlockSpec((length, PAIR), fixed),
                pl.BlockSpec((length, PAIR), fixed),
                pl.BlockSpec((width, length), fixed),
                pl.BlockSpec((width, count), lambda h, w: (0, w[groups])),
            ],
            out_specs=[
                to_rows,
                to_keys,
                to_keys,
                pl.BlockSpec(grads_part.shape, fixed),
                pl.BlockSpec(grads_part.shape, fixed),
            ],
            scratch=[pltpu.VMEM((width, 3 * width // 2), F32)],
            name="attend_back",
            micros=11,
        )

    dq_a, dk_a, dv_a, a_away, a_kept = attend_back(0, grad_att)
    if packed:
        a_away, a_kept, out_kept = lax.optimization_barrier(
            (a_away, a_kept, out_kept, far[0], near)
        )[:3]
        out_both = added(out_kept, swap(out_away, "expert", 1))
        a_both = added(a_kept, swap(a_away, "expert", 1))
        grad_att = after(grad_att, a_both, out_both)
    dq_b, dk_b, dv_b, b_away, b_kept = attend_back(1, grad_att)
    def project_back(dq_late):
        half_rows = pl.BlockSpec((count, width // 2), fixed)
        half_keys = pl.BlockSpec((count, width // 2), at_rank)
        return call(
            functools.partial(project_back_kernel, slots=groups),
            [shaped((length, width), BF), shaped((count, width), F32)],
            (back_where, dq_a, dq_late, dk_a, dk_b, dv_a, dv_b, qkv_full),
            grid=(groups,),
            in_specs=[half_rows] * 2 + [half_keys] * 4 + [pl.BlockSpec((width, 3 * width), fixed)],
            out_specs=[pl.BlockSpec((count, width), at_rank), pl.BlockSpec((count, width), fixed)],
            name="project_back",
            micros=6,
        )

    if packed:
        b_away = after(b_away, far[1])
        out_sum, a_sum = along_chips(out_both, (b_kept,)), along_chips(a_both, (b_kept,))
        b_both = added(b_kept, swap(b_away, "expert", 1))
        dq_b = after(dq_b, b_both)
        b_sum = along_chips(b_both, ())
        parts_all = jnp.concatenate([a_sum, b_sum, out_sum], axis=1)
        rows_back, own_back = project_back(dq_b)
        total, piece = across_major(after(parts_all, rows_back), shard_rows // 4)
        own_grads = after(grads[0], piece)
        away, kept, shard_down = call(
            sum_parts_kernel,
            [
                shaped((8 * shard_rows, 256), BF),
                shaped((8 * shard_rows, 256), F32),
                shaped((256, width), F32),
            ],
            (just_minor, own_grads, near, middle) + tuple(far),
            name="sum_parts",
            micros=3,
        )
        shard_gate_up = call(
            unpack_kernel,
            shaped((shard_rows, 2 * FF), F32),
            (just_minor, kept, swap(away, "fsdp", 1)),
            name="unpack_expert",
            micros=2,
        )
    else:
        both = jnp.concatenate([a_kept, b_kept, out_kept], axis=1)
        both = lax.psum_scatter(both, "fsdp", scatter_dimension=0, tiled=True)
        total = lax.psum(both, "expert")
        other = total
        rows_back, own_back = project_back(dq_b)
    rows_sum = sequence_scatter_sum(rows_back, count)
    grad_tokens = call(
        functools.partial(finish_kernel, gain_at=gain_one_at),
        shaped((count, width), BF),
        (just_minor, tok, small_t, grad_hidden, own_back, rows_sum),
        name="finish",
        micros=3,
    )

    if packed:
        total = after(total, grad_tokens, shard_gate_up)
        total = jnp.concatenate([total, swap(total, "expert", 2)], axis=0)
        other = swap(total, "expert", 1)
    shared_grads = call(
        functools.partial(
            shared_kernel, columns=columns, width=width, entries=length * width, packed=packed
        ),
        [
            shaped((shard_rows, 3 * width), F32),
            shaped((shard_rows, width), F32),
            shaped((kinds, shard_rows), F32),
            shaped((2 * NCONST, shard_rows), F32),
            shaped((NCONST, shard_rows), F32),
            shaped((1, shard_rows), F32),
            shaped((1, shard_rows), F32),
            shaped((1, 2), F32),
        ],
        (jnp.stack([me_expert]), total, other, qkv_weight, gain_one[None]),
        scratch=[pltpu.VMEM((shard_rows, 4 * width + SMALL), F32)],
        name="shared_grads",
        micros=3,
    )
    grad_qkv, grad_out, grad_router, grad_gate, grad_value, grad_one, grad_two, stream = shared_grads
    return (
        outputs[None],
        grad_tokens[None],
        grad_one[0],
        grad_qkv,
        grad_out,
        grad_two[0],
        grad_router.T,
        grad_gate.T,
        grad_value.T,
        shard_gate_up[None],
        shard_down[None],
        grad_residual.T[None],
        stream,
    )


def solution(mesh):
    return jax.shard_map(
        on_device,
        mesh=mesh,
        in_specs=(
            P("fsdp", "expert", None),
            P("fsdp"),
            P("fsdp", None),
            P("fsdp", None),
            P("fsdp"),
            P("fsdp", None),
            P("fsdp", None),
            P("fsdp", None),
            P("expert", "fsdp", None),
            P("expert", "fsdp", None),
            P("fsdp", "expert", None),
            P("fsdp", "expert", None),
            P("fsdp", "expert", None),
        ),
        out_specs=(
            P("fsdp", "expert", None),
            P("fsdp", "expert", None),
            P("fsdp"),
            P("fsdp", None),
            P("fsdp", None),
            P("fsdp"),
            P("fsdp", None),
            P("fsdp", None),
            P("fsdp", None),
            P("expert", "fsdp", None),
            P("expert", "fsdp", None),
            P("fsdp", "expert", None),
            P("fsdp", None),
        ),
        check_vma=False,
    )
```

```python
import functools

import jax
import jax.numpy as jnp
from jax import lax
from jax.experimental import pallas as pl
from jax.experimental.pallas import tpu as pltpu
from jax.sharding import PartitionSpec as P

HEAD = 64
FF = 2048
NCONST = 2
MOST = 80
PAIR = 2 * HEAD
SMALL = 128

epsilon = 1e-06
masked_score = -1e30
BF = jnp.bfloat16
F32 = jnp.float32


def mm(a, b):
    return jnp.dot(a, b, preferred_element_type=F32)


def mm_nt(a, b):
    return lax.dot_general(a, b, (((1,), (1,)), ((), ())), preferred_element_type=F32)


def mm_tn(a, b):
    return lax.dot_general(a, b, (((0,), (0,)), ((), ())), preferred_element_type=F32)


def split_low(values):
    high = values.astype(BF)
    return high, (values - high.astype(F32)).astype(BF)


def lanes(shape):
    return lax.broadcasted_iota(jnp.int32, shape, len(shape) - 1)


def rows_of(shape):
    return lax.broadcasted_iota(jnp.int32, shape, 0)


def rms_scale(values):
    return lax.rsqrt(jnp.mean(values * values, axis=-1, keepdims=True) + epsilon)


def turned(values, cosine, sine):
    lane = lanes(values.shape) % HEAD
    swapped = jnp.where(
        lane < HEAD // 2,
        pltpu.roll(values, PAIR - HEAD // 2, 1),
        pltpu.roll(values, HEAD // 2, 1),
    )
    return values * cosine + swapped * sine


def call(kernel, outs, args, grid=(), in_specs=None, out_specs=None, scratch=(), scalars=1, name=None, micros=2):
    whole = pl.BlockSpec(memory_space=pltpu.VMEM)
    multi = isinstance(outs, (tuple, list))
    if in_specs is None:
        in_specs = [whole] * (len(args) - scalars)
    if out_specs is None:
        out_specs = [whole] * len(outs) if multi else whole
    return pl.pallas_call(
        kernel,
        out_shape=outs,
        grid_spec=pltpu.PrefetchScalarGridSpec(
            num_scalar_prefetch=scalars,
            grid=grid,
            in_specs=in_specs,
            out_specs=out_specs,
            scratch_shapes=list(scratch),
        ),
        compiler_params=pltpu.CompilerParams(vmem_limit_bytes=56 * 1024 * 1024),
        cost_estimate=pl.CostEstimate(
            flops=micros * 90_000_000, transcendentals=0, bytes_accessed=micros * 300_000
        ),
        name=name,
    )(*args)


def shaped(shape, dtype):
    return jax.ShapeDtypeStruct(shape, dtype)


def swap(values, axis, bits):
    size = lax.axis_size(axis)
    return lax.ppermute(values, axis, [(i, i ^ bits) for i in range(size)])


def along(values, pairs):
    return lax.ppermute(
        values, "fsdp", [(2 * i + b, 2 * j + b) for i, j in pairs for b in (0, 1)]
    )


def after(values, *others):
    return lax.optimization_barrier((values,) + tuple(others))[0]


FAR = ((0, 2), (2, 0), (1, 3), (3, 1))
NEAR = ((0, 1), (1, 0), (2, 3), (3, 2))
MIDDLE = ((1, 2), (2, 1))
OUTWARD = ((2, 3), (1, 0))
INWARD = ((0, 1), (3, 2))


def minor_groups(major):
    return [[2 * i + b for i in range(major)] for b in (0, 1)]


def blocks_kernel(where, gate_up, out):
    rows = gate_up.shape[0]
    for block in range(8):
        at = (2 * block + 1 - where[0]) * 256
        out[block * rows : (block + 1) * rows, :] = gate_up[:, pl.ds(pl.multiple_of(at, 256), 256)]


def pack_kernel(where, gate_up, arrived, out):
    rows = gate_up.shape[0]
    mine = where[0]
    for block in range(8):
        at = (2 * block + mine) * 256
        own = pl.ds(pl.multiple_of(2 * block * rows + mine * rows, rows), rows)
        other = pl.ds(pl.multiple_of(2 * block * rows + (1 - mine) * rows, rows), rows)
        out[own, :] = gate_up[:, pl.ds(pl.multiple_of(at, 256), 256)]
        out[other, :] = arrived[block * rows : (block + 1) * rows, :]


def sum_parts_kernel(where, a, b, c, d0, d1, d2, away, kept, down):
    rows = away.shape[0] // 8
    mine = where[0]

    def total(start, size, d, base):
        source, shifted = pl.ds(start, size), pl.ds(start - base, size)
        return (
            a[source, :].astype(F32)
            + b[source, :].astype(F32)
            + c[source, :].astype(F32)
            + d[shifted, :].astype(F32)
        )

    for block in range(8):
        here = slice(block * rows, (block + 1) * rows)
        base = 2 * block * rows
        d, cut = ((d0, 0), (d1, 8 * rows), (d2, 14 * rows))[(block > 3) + (block > 6)]
        own = pl.multiple_of(base + mine * rows, rows)
        other = pl.multiple_of(base + (1 - mine) * rows, rows)
        away[here, :] = total(other, rows, d, cut).astype(BF)
        kept[here, :] = total(own, rows, d, cut)
    for block in range(3):
        base = 16 * rows + block * 256
        down[:, block * 256 : (block + 1) * 256] = total(base, 256, d2, 14 * rows)


def unpack_kernel(where, kept, arrived, out):
    rows = out.shape[0]
    mine = where[0]
    for block in range(8):
        here = slice(block * rows, (block + 1) * rows)
        own = pl.ds(pl.multiple_of((2 * block + mine) * 256, 256), 256)
        other = pl.ds(pl.multiple_of((2 * block + 1 - mine) * 256, 256), 256)
        out[:, own] = kept[here, :]
        out[:, other] = arrived[here, :].astype(F32)


def shared_pack(qkv, out, small):
    core = lax.axis_index("expert") % 2
    half_qkv, half_out = qkv.shape[1] // 2, out.shape[1] // 2
    rows = qkv.shape[0]

    def kernel(where, qkv_ref, out_ref, *refs):
        small_refs, (packed, room) = refs[:-2], refs[-2:]
        packed[:, :half_qkv] = qkv_ref[:, pl.ds(pl.multiple_of(where[0] * half_qkv, 128), half_qkv)]
        packed[:, half_qkv : half_qkv + half_out] = out_ref[
            :, pl.ds(pl.multiple_of(where[0] * half_out, 128), half_out)
        ]
        room[...] = jnp.zeros_like(room)
        at = 0
        for ref in small_refs:
            room[at : at + ref.shape[0], : ref.shape[1]] = ref[...].astype(F32)
            at += ref.shape[0]
        packed[:, half_qkv + half_out :] = room[...].astype(BF)

    return call(
        kernel,
        shaped((rows, half_qkv + half_out + SMALL), BF),
        (jnp.stack([core]).astype(jnp.int32), qkv, out) + small,
        scratch=[pltpu.VMEM((rows, SMALL), F32)],
        name="pack_shared",
        micros=1,
    )


def shared_gather(mine, down, early, late):
    me = lax.axis_index("fsdp")
    major = [mine, swap(mine, "fsdp", 2), swap(mine, "fsdp", 4)]
    minor = [swap(mine, "fsdp", 1)]
    major.append(swap(after(mine, minor[0]), "fsdp", 6))
    minor.append(swap(after(major[1], minor[0]), "fsdp", 1))
    minor.append(swap(after(major[2], *early), "fsdp", 1))
    minor.append(swap(after(major[3], minor[1], *late), "fsdp", 1))
    down_near = along(after(down, major[3]), NEAR)
    down_far = along(after(down, major[3]), FAR)
    slots = [2 * j for j in range(4)] + [2 * j + 1 for j in range(4)]
    own = after(jnp.concatenate(major + minor, axis=0), down_near, down_far)
    return own, swap(own, "expert", 1), [me ^ s for s in slots], down_near, down_far


def added(kept, arrived):
    return (kept.astype(F32) + arrived.astype(F32)).astype(BF)


def along_chips(both, gate):
    for axis, bits in (("expert", 2), ("fsdp", 1)):
        half = both.shape[0] // 2
        both = added(after(both[:half], *gate), swap(both[half:], axis, bits))
        gate = ()
    return both


def across_major(parts, rows):
    pieces = [swap(parts[j * rows : (j + 1) * rows], "fsdp", 2 * j) for j in (1, 2, 3)]
    total = parts[:rows].astype(F32)
    for piece in pieces:
        total += piece.astype(F32)
    return total.astype(BF), pieces[0]


def sequence_gather(values, across):
    size = lax.axis_size("expert")
    me = lax.axis_index("expert")
    if size != 4:
        every = lax.all_gather(values, "expert", axis=0, tiled=True)
        middle = every.shape[0] // 2
        return every[:middle], every[middle:], list(range(size))
    pair = jnp.concatenate([values, across], axis=0)
    return pair, swap(pair, "expert", 1), [me, me ^ 2, me ^ 1, me ^ 3]


def exchange(sends):
    half = len(sends) // 2
    received = [swap(v, "expert", j) if j else v for j, v in enumerate(sends)]
    low = swap(jnp.concatenate(received[:half], axis=0), "fsdp", 1)
    high = swap(after(jnp.concatenate(received[half:], axis=0), low), "fsdp", 1)
    return received, low, high


def exchange_back(low, high, size):
    rows = 2 * low.shape[0] // size
    if size == 4:
        upper = swap(high, "expert", 2)
        joined = swap(jnp.concatenate([low[rows:], upper[rows:]], axis=0), "expert", 1)
        return [low[:rows], joined[:rows], upper[:rows], joined[rows:]]
    pieces = [w[i : i + rows] for w in (low, high) for i in range(0, w.shape[0], rows)]
    return [swap(piece, "expert", j) if j else piece for j, piece in enumerate(pieces)]


def sequence_scatter_sum(full, rows):
    size = lax.axis_size("expert")
    me = lax.axis_index("expert")
    if size != 4:
        return lax.psum_scatter(full, "expert", scatter_dimension=0, tiled=True).astype(F32)

    def block(bits):
        return lax.dynamic_slice_in_dim(full, (me ^ bits) * rows, rows, 0)

    away = jnp.concatenate([block(1), block(3)], axis=0)
    kept = jnp.concatenate([block(0), block(2)], axis=0)
    both = kept.astype(F32) + swap(away, "expert", 1).astype(F32)
    return both[:rows] + swap(both[rows:].astype(BF), "expert", 2).astype(F32)


def project_kernel(where, *refs, slots, gain_at, placed):
    if placed:
        tok_a, tok_b, cosine, sine, weight, small_t, q, k, v, normed = refs
    else:
        tok_a, tok_b, cosine, sine, own_ref, other_ref = refs[:6]
        q, k, v, normed, weight, out_ref, small_ref, small_t = refs[6:]
    step = pl.program_id(0)
    rank = where[step]
    own = where[slots]
    width = tok_a.shape[1]

    if not placed:

        @pl.when(step == 0)
        def _():
            first = where[slots + 9] == 0
            rows = width // 8
            half_qkv, half_out = 3 * width // 2, width // 2
            for index in range(8):
                source = pl.ds(index * rows, rows)
                target = pl.ds(pl.multiple_of(where[slots + 1 + index] * rows, rows), rows)
                a, b = own_ref[source, :], other_ref[source, :]
                left = jnp.where(first, a, b)
                right = jnp.where(first, b, a)
                weight[target, :half_qkv] = left[:, :half_qkv]
                weight[target, half_qkv:] = right[:, :half_qkv]
                out_ref[target, :half_out] = left[:, half_qkv : half_qkv + half_out]
                out_ref[target, half_out:] = right[:, half_qkv : half_qkv + half_out]
                of_rows = jnp.zeros((SMALL, SMALL), F32)
                of_rows = jnp.concatenate(
                    [a[:32, half_qkv + half_out :].astype(F32), of_rows[32:]], axis=0
                ).T
                small_ref[target, :] = of_rows[:rows].astype(BF)
            small_t[...] = small_ref[...].astype(F32).T[:32]

    @pl.when(rank > own)
    def _():
        k[...] = jnp.zeros_like(k)
        v[...] = jnp.zeros_like(v)
        normed[...] = jnp.zeros_like(normed)

    @pl.when(rank <= own)
    def _():
        x = jnp.where(step < slots // 2, tok_a[...], tok_b[...]).astype(F32)
        wide = (x * rms_scale(x)) * small_t[gain_at : gain_at + 1, :]
        low = wide.astype(BF)
        normed[...] = low.T
        cos, sin = cosine[...], sine[...]
        keys = mm(low, weight[:, width : 2 * width])
        for at in range(0, width, PAIR):
            k[:, at : at + PAIR] = turned(keys[:, at : at + PAIR], cos, sin).astype(BF)
        v[...] = mm(low, weight[:, 2 * width :]).astype(BF)

        @pl.when(rank == own)
        def _():
            queries = mm(low, weight[:, :width])
            for at in range(0, width, PAIR):
                q[:, at : at + PAIR] = turned(queries[:, at : at + PAIR], cos, sin).astype(BF)


def stacked_heads(values, scale=None):
    lane = lanes(values.shape)
    if scale is not None:
        values = values * jnp.asarray(scale, values.dtype)
    zero = jnp.zeros_like(values)
    return jnp.concatenate(
        [jnp.where(lane < HEAD, values, zero), jnp.where(lane < HEAD, zero, values)], axis=0
    )


def visible_keys(own, keys, count):
    key = lax.broadcasted_iota(jnp.int32, (keys, 2 * count), 0)
    query = lax.broadcasted_iota(jnp.int32, (keys, 2 * count), 1) % count
    return key <= query + own * count


def attend_kernel(where, q, k, v, attended, kept, *, slots):
    own = where[slots]
    count, keys = q.shape[0], k.shape[0]
    query = stacked_heads(q[...], HEAD ** (-0.5))
    scores = mm_nt(k[...], query)
    scores = jnp.where(visible_keys(own, keys, count), scores, masked_score)
    top = jnp.max(scores, axis=0, keepdims=True)
    weights = jnp.exp(scores - top)
    total = jnp.sum(weights, axis=0, keepdims=True)
    weights = (weights * (1.0 / total)).astype(BF)
    kept[0] = weights
    both = mm_tn(v[...], weights).T
    lane = lanes((count, PAIR))
    attended[...] = jnp.where(lane < HEAD, both[:count], both[count:]).astype(BF)


def attend_back_kernel(where, q, k, v, grad_att, kept_weights, cosine, sine, normed, normed_own, dq, dk, dv, away, kept, sums, *, slots, packed):
    step = pl.program_id(0)
    own = where[slots]
    count = q.shape[0]
    query = stacked_heads(q[...], HEAD ** (-0.5))
    grad_rows = stacked_heads(grad_att[...])
    key_rows = k[...]
    low_weights = kept_weights[0]
    weights = low_weights.astype(F32)
    grad_weights = mm_nt(v[...], grad_rows)
    delta = jnp.sum(weights * grad_weights, axis=0, keepdims=True)
    grad_scores = (weights * (grad_weights - delta)).astype(BF)
    grad_v = mm(low_weights, grad_rows).astype(BF)
    dv[...] = grad_v
    grad_k = turned(mm(grad_scores, query), cosine[...], -sine[...]).astype(BF)
    dk[...] = grad_k
    both = mm_tn(key_rows, grad_scores).T
    lane = lanes((count, PAIR))
    grad_q = jnp.where(lane < HEAD, both[:count], both[count:]) * HEAD ** (-0.5)
    mine = pl.ds(pl.multiple_of(own * count, count), count)
    grad_q = turned(grad_q, cosine[mine, :], -sine[mine, :]).astype(BF)
    dq[...] = grad_q
    of_keys = mm(normed[...], jnp.concatenate([grad_k, grad_v], axis=1))
    of_queries = mm(normed_own[...], grad_q)
    steps = kept.shape[1] // (3 * PAIR)
    for index in range(steps):

        @pl.when(step == index)
        def _():
            for part, values in enumerate((of_queries, of_keys[:, :PAIR], of_keys[:, PAIR:])):
                at = (part * steps + index) * PAIR
                sums[:, at : at + PAIR] = values

    @pl.when(step == steps - 1)
    def _():
        if packed:
            split_rows(where, slots + 1, sums, away, kept)
        else:
            kept[...] = sums[...].astype(BF)
            away[...] = jnp.zeros_like(away)


def split_rows(where, at, values, away, kept):
    core, chip = where[at + 8], where[at + 9]
    rows = values.shape[0] // 32
    for index in range(0, 16, 2):
        target = slice(index * rows, (index + 2) * rows)
        for ref, side in ((kept, core), (away, 1 - core)):
            pieces = []
            for step in (index, index + 1):
                rank = 2 * (chip ^ (step // 8)) + side
                base = (where[at + step % 8] * 4 + rank) * rows
                pieces.append(values[pl.ds(pl.multiple_of(base, 8), rows), :])
            ref[target, :] = jnp.concatenate(pieces, axis=0).astype(BF)


def as_lanes(rows):
    rows = rows.astype(F32)
    spare = jnp.zeros((SMALL - rows.shape[0], rows.shape[1]), F32)
    return jnp.concatenate([rows, spare], axis=0).T


def routing(routes, resid, logits, groups):
    count = routes.shape[0]
    lane = lanes((count, SMALL))
    logits = logits + resid
    hot, picked = [], []
    for choice in range(2):
        route = routes[:, choice : choice + 1]
        hot.append(lane == route)
        picked.append(jnp.sum(jnp.where(hot[choice], logits, 0.0), axis=-1, keepdims=True))
    top = jnp.maximum(picked[0], picked[1])
    first, second = jnp.exp(picked[0] - top), jnp.exp(picked[1] - top)
    gates = [first / (first + second), second / (first + second)]
    named = jnp.logical_or(hot[0], hot[1]).astype(BF)
    earlier = (lanes((count, count)) < rows_of((count, count))).astype(BF)
    place = mm(earlier, named)
    dispatch = []
    column = lanes((count, groups * MOST))
    for choice in range(2):
        route = routes[:, choice : choice + 1]
        slot = jnp.sum(jnp.where(hot[choice], place, 0.0), axis=-1, keepdims=True)
        target = jnp.where(route < groups, route * MOST + slot.astype(jnp.int32), -1)
        dispatch.append((column == target).astype(BF))
    return gates, hot, dispatch


def route_kernel(where, att, out_weight, tok, small, small_t, resid, routes, cot, hidden_ref, low_ref, *rest, groups, gain_at):
    sends = rest[:groups]
    rows_x, rows_g = rest[groups], rest[groups + 1]
    hidden = tok[...].astype(F32) + mm(att[...], out_weight[...])
    hidden_ref[...] = hidden
    low = ((hidden * rms_scale(hidden)) * small_t[gain_at : gain_at + 1, :]).astype(BF)
    low_ref[...] = low
    logits = mm(low, small[...])
    route = as_lanes(routes[...])[:, :2].astype(jnp.int32)
    gates, _, dispatch = routing(route, as_lanes(resid[...]), logits, groups)
    grad = cot[...].astype(F32)
    rows_x[...] = mm_tn(dispatch[0] + dispatch[1], low).astype(BF)
    rows_g[...] = (
        mm_tn(dispatch[0], (gates[0] * grad).astype(BF))
        + mm_tn(dispatch[1], (gates[1] * grad).astype(BF))
    ).astype(BF)
    for slot in range(groups):
        source = pl.ds(pl.multiple_of(where[slot] * MOST, MOST), MOST)
        sends[slot][:MOST, :] = rows_x[source, :]
        sends[slot][MOST:, :] = rows_g[source, :]


def expert_kernel(where, *refs, groups, hidden_units, packed):
    refs = list(refs)

    def take(amount):
        taken = refs[:amount]
        del refs[:amount]
        return taken

    received = take(groups) + take(2)
    if packed:
        unit_parts, down_parts = take(5), take(5)
    else:
        gate_up, down = take(2)
    own_out, other_out = take(2), take(2)
    if packed:
        messages = take(4)
    else:
        grad_gate_up, grad_down = take(2)
    rows, grads, out_rows, back_rows, acts, grad_units = take(6)
    if packed:
        gate_up, down, rows_t = take(3)
    width = rows.shape[1]
    total = 2 * groups * MOST
    index = 0
    for ref in received:
        for base in range(0, ref.shape[0], 2 * MOST):
            target = slice(index * MOST, (index + 1) * MOST)
            rows[target, :] = ref[base : base + MOST, :]
            grads[target, :] = ref[base + MOST : base + 2 * MOST, :]
            index += 1
    if packed:
        part = width // 4

        def place(slot, ref, down_ref):
            target = pl.ds(pl.multiple_of(where[slot] * part, part), part)
            for block in range(8):
                gate_up[target, block * 256 : (block + 1) * 256] = ref[
                    block * part : (block + 1) * part, :
                ]
            down[pl.ds(pl.multiple_of(where[slot] * 256, 256), 256), :] = down_ref[...]

        for slot in range(3):
            place(slot, unit_parts[slot], down_parts[slot])

        @pl.when(where[4] == 1)
        def _():
            place(3, unit_parts[3], down_parts[3])

        @pl.when(where[4] == 0)
        def _():
            place(3, unit_parts[4], down_parts[4])

    x, g = rows[...], grads[...]
    chunk = 256
    out_rows[...] = jnp.zeros_like(out_rows)
    back_rows[...] = jnp.zeros_like(back_rows)

    def forward_back(step, carry):
        first = pl.ds(pl.multiple_of(step * chunk, chunk), chunk)
        second = pl.ds(pl.multiple_of(hidden_units + step * chunk, chunk), chunk)
        gate_w, up_w, down_w = gate_up[:, first], gate_up[:, second], down[first, :]
        gate, up = mm(x, gate_w), mm(x, up_w)
        sig = 1.0 / (1.0 + jnp.exp(-gate))
        silu = gate * sig
        act = (silu * up).astype(BF)
        acts[:, first] = act
        grad_act = mm_nt(g, down_w)
        grad_gate = (grad_act * up * sig * (1.0 + gate * (1.0 - sig))).astype(BF)
        grad_up = (grad_act * silu).astype(BF)
        grad_units[:, first] = grad_gate
        grad_units[:, second] = grad_up
        out_rows[...] += mm(act, down_w)
        back_rows[...] += mm_nt(grad_gate, gate_w) + mm_nt(grad_up, up_w)
        return carry

    lax.fori_loop(0, hidden_units // chunk, forward_back, 0)
    index = 0
    for ref in own_out + other_out:
        for base in range(0, ref.shape[0], 2 * MOST):
            source = slice(index * MOST, (index + 1) * MOST)
            ref[base : base + MOST, :] = out_rows[source, :].astype(ref.dtype)
            ref[base + MOST : base + 2 * MOST, :] = back_rows[source, :].astype(ref.dtype)
            index += 1
    if not packed:
        grad_gate_up[...] = mm_tn(x, grad_units[...]).astype(BF)
        grad_down[...] = mm_tn(acts[...], g).astype(BF)
        return
    part = width // 4

    def weight_grad(step, carry):
        block = pl.ds(pl.multiple_of(step * 512, 512), 512)
        gate_up[:, block] = mm(rows_t[...], grad_units[:, block]).astype(BF)
        return carry

    rows_t[...] = x.T
    lax.fori_loop(0, 4, weight_grad, 0)
    for slot, ref in enumerate(messages):
        source = pl.ds(pl.multiple_of(where[slot] * part, part), part)
        for block in range(8):
            ref[block * part : (block + 1) * part, :] = gate_up[
                source, block * 256 : (block + 1) * 256
            ]
        mine = acts[:, pl.ds(pl.multiple_of(where[slot] * 256, 256), 256)]
        of_down = mm_tn(mine, g).astype(BF)
        for block in range(3):
            base = 8 * part + block * 256
            ref[base : base + 256, :] = of_down[:, block * 256 : (block + 1) * 256]


def combine_kernel(where, *refs, groups, columns, shard_rows, packed):
    backs = refs[:groups]
    (hidden_ref, low_ref, cot, routes, resid, small, small_t, out_weight, att,
     out_ref, grad_hidden_ref, grad_att_ref, grad_away, grad_kept, grad_resid,
     rows_y, rows_d, sums) = refs[groups:]
    kinds, mix_at, value_at, gain_two_at, square_at = columns
    for slot in range(groups):
        target = pl.ds(pl.multiple_of(where[slot] * MOST, MOST), MOST)
        rows_y[target, :] = backs[slot][:MOST, :]
        rows_d[target, :] = backs[slot][MOST:, :]
    hidden, low = hidden_ref[...], low_ref[...]
    count = low.shape[0]
    normed_input = low.astype(F32)
    grad_low_type = cot[...]
    grad = grad_low_type.astype(F32)
    logits = mm(low, small[...])
    grad_small_dot = mm(grad_low_type, small[...])
    route = as_lanes(routes[...])[:, :2].astype(jnp.int32)
    gates, hot, dispatch = routing(route, as_lanes(resid[...]), logits, groups)
    returned = [mm(dispatch[c], rows_y[...]) for c in range(2)]
    grad_back = mm(dispatch[0] + dispatch[1], rows_d[...])
    grad_dot = jnp.sum(grad * normed_input, axis=-1, keepdims=True)
    is_copy = [(route[:, c : c + 1] == groups + 1).astype(F32) for c in range(2)]
    grad_gates = [
        jnp.sum(grad * returned[c], axis=-1, keepdims=True) + is_copy[c] * grad_dot
        for c in range(2)
    ]
    direct = gates[0] * is_copy[0] + gates[1] * is_copy[1]
    mixture = gates[0] * returned[0] + gates[1] * returned[1]
    lane = lanes((count, SMALL))
    grad_logits = jnp.zeros((count, SMALL), F32)
    value_weights = jnp.zeros((count, SMALL), F32)
    for const in range(NCONST):
        first = logits[:, mix_at + 2 * const : mix_at + 2 * const + 1]
        second = logits[:, mix_at + 2 * const + 1 : mix_at + 2 * const + 2]
        top = jnp.maximum(first, second)
        first, second = jnp.exp(first - top), jnp.exp(second - top)
        mix = [first / (first + second), second / (first + second)]
        value_dot = grad_small_dot[:, value_at + const : value_at + const + 1]
        named = [(route[:, c : c + 1] == groups + 2 + const).astype(F32) for c in range(2)]
        for c in range(2):
            grad_gates[c] += named[c] * (mix[0] * grad_dot + mix[1] * value_dot)
        weight = gates[0] * named[0] + gates[1] * named[1]
        direct += weight * mix[0]
        of_value = weight * mix[1]
        mixture += of_value * small_t[value_at + const : value_at + const + 1, :]
        value_weights = jnp.where(lane == value_at + const, of_value, value_weights)
        grad_mix = [weight * grad_dot, weight * value_dot]
        common = mix[0] * grad_mix[0] + mix[1] * grad_mix[1]
        for c in range(2):
            grad_logits = jnp.where(
                lane == mix_at + 2 * const + c, mix[c] * (grad_mix[c] - common), grad_logits
            )
    outputs = hidden + mixture + direct * normed_input
    out_ref[...] = outputs.astype(BF)
    common = gates[0] * grad_gates[0] + gates[1] * grad_gates[1]
    for c in range(2):
        grad_logits = jnp.where(hot[c], gates[c] * (grad_gates[c] - common), grad_logits)
    grad_resid[...] = grad_logits.T[:kinds].astype(BF)
    high, rest = split_low(grad_logits)
    weights = small[...]
    grad_low = grad_back + direct * grad + mm_nt(high, weights) + mm_nt(rest, weights)
    scale = rms_scale(hidden)
    normed = hidden * scale
    of_gain = jnp.sum((grad_low * normed).reshape(-1, 8, normed.shape[1]), axis=0)
    of_gain = jnp.sum(of_gain, axis=0, keepdims=True)
    value_high, value_rest = split_low(value_weights)
    summed = mm_tn(low, jnp.concatenate([high, rest], axis=1))
    summed += mm_tn(grad_low_type, jnp.concatenate([value_high, value_rest], axis=1))
    summed = summed[:, :SMALL] + summed[:, SMALL:]
    wide = (SMALL, normed.shape[1])
    summed += jnp.where(rows_of(wide) == gain_two_at, of_gain, 0.0).T
    column, row = lanes(summed.shape), rows_of(summed.shape)
    mine = row // shard_rows == where[groups]
    for index, total in enumerate((jnp.sum(hidden * hidden), jnp.sum(outputs * outputs))):
        for part, value in enumerate(split_low(jnp.full((1, 1), total, F32))):
            spot = jnp.logical_and(mine, column == square_at + 2 * index + part)
            summed = jnp.where(spot, value.astype(F32), summed)
    grad_normed = grad_low * small_t[gain_two_at : gain_two_at + 1, :]
    grad_hidden = grad + scale * (
        grad_normed - normed * jnp.mean(grad_normed * normed, axis=-1, keepdims=True)
    )
    grad_hidden_ref[...] = grad_hidden
    branch = grad_hidden.astype(BF)
    grad_att_ref[...] = mm_nt(branch, out_weight[...]).astype(BF)
    width = branch.shape[1]
    sums[:, :width] = mm_tn(att[...], branch)
    sums[:, width:] = summed
    if packed:
        split_rows(where, groups + 1, sums, grad_away, grad_kept)
    else:
        grad_kept[...] = sums[...].astype(BF)
        grad_away[...] = jnp.zeros_like(grad_away)


def project_back_kernel(where, *refs, slots):
    queries, keys, values = refs[0:2], refs[2:4], refs[4:6]
    weight, rows_back, own_back = refs[6:]
    rank = where[pl.program_id(0)]
    own = where[slots]
    half = keys[0].shape[1]
    width = 2 * half

    def through(parts, base):
        result = mm_nt(parts[0][...], weight[:, base : base + half])
        return result + mm_nt(parts[1][...], weight[:, base + half : base + width])

    @pl.when(rank > own)
    def _():
        rows_back[...] = jnp.zeros_like(rows_back)

    @pl.when(rank <= own)
    def _():
        rows_back[...] = (through(keys, width) + through(values, 2 * width)).astype(BF)

        @pl.when(rank == own)
        def _():
            own_back[...] = through(queries, 0)


def finish_kernel(where, tok, small_t, grad_hidden, own_back, rows_back, out, *, gain_at):
    x = tok[...].astype(F32)
    scale = rms_scale(x)
    normed = x * scale
    grad = (own_back[...] + rows_back[...]) * small_t[gain_at : gain_at + 1, :]
    out[...] = (
        grad_hidden[...]
        + scale * (grad - normed * jnp.mean(grad * normed, axis=-1, keepdims=True))
    ).astype(BF)


def shared_kernel(where, total, other, weight, gain, qkv, out, router, gate, value, gain_one, gain_two, stream, room, *, columns, width, entries, packed):
    kinds, mix_at, value_at, gain_two_at, square_at = columns
    if packed:
        rows = room.shape[0] // 4
        for parts, rank in ((total, where[0]), (other, where[0] ^ 1)):
            both = parts[...].astype(F32)
            room[pl.ds(pl.multiple_of(rank * rows, 8), rows), :] = both[:rows]
            room[pl.ds(pl.multiple_of((rank ^ 2) * rows, 8), rows), :] = both[rows:]
    else:
        room[...] = total[...].astype(F32)
    values = room[...]
    half = width // 2
    for part in range(3):
        for side in range(2):
            at = (3 * side + part) * half
            to = part * width + side * half
            qkv[:, to : to + half] = values[:, at : at + half]
    out[...] = values[:, 3 * width : 4 * width]
    rows = values.shape[0]

    def as_columns(block):
        spare = jnp.zeros((SMALL - rows, SMALL), F32)
        return jnp.concatenate([block, spare], axis=0).T[:, :rows]

    small = values[:, 4 * width :]
    turned_small = as_columns(small)
    router[...] = turned_small[:kinds]
    gate[...] = turned_small[mix_at : mix_at + 2 * NCONST]
    value[...] = turned_small[value_at : value_at + NCONST]
    gain_two[...] = turned_small[gain_two_at : gain_two_at + 1]
    of_gain = jnp.sum(qkv[...] * weight[...].astype(F32), axis=-1, keepdims=True)
    gain_one[...] = as_columns(jnp.broadcast_to(of_gain, (rows, SMALL)))[:1] / gain[...].astype(F32)
    squares = small[:1, square_at : square_at + 4]
    hidden = squares[:, 0:1] + squares[:, 1:2]
    outputs = squares[:, 2:3] + squares[:, 3:4]
    stream[...] = jnp.sqrt(jnp.where(lanes((1, 2)) == 0, hidden, outputs) / entries)


def on_device(
    tokens,
    gain_one,
    qkv_weight,
    out_weight,
    gain_two,
    router_weight,
    const_gate,
    const_value,
    expert_gate_up,
    expert_down,
    gate_residual,
    routes,
    cotangent,
):
    parts = lax.axis_size("fsdp")
    groups = lax.axis_size("expert")
    me_fsdp = lax.axis_index("fsdp").astype(jnp.int32)
    me_expert = lax.axis_index("expert").astype(jnp.int32)
    minor, major, core = me_fsdp % 2, me_fsdp // 2, me_expert % 2
    packed = parts == 8 and groups == 4
    major_count = parts // 2
    tok = tokens[0]
    count, width = tok.shape
    length = groups * count
    pairs = width // PAIR
    kinds = router_weight.shape[1]
    mix_at, value_at = kinds, kinds + 2 * NCONST
    gain_one_at = value_at + NCONST
    gain_two_at = gain_one_at + 1
    square_at = gain_two_at + 1
    shard_rows = width // parts
    unit = FF // parts
    units = FF // 2
    fixed = lambda j, w: (0, 0)
    at_slot = lambda j, w: (j, 0)
    at_rank = lambda j, w: (w[j], 0)
    just_minor = jnp.stack([minor])

    small_parts = (router_weight.T, const_gate.T, const_value.T, gain_one[None], gain_two[None])
    frequency = 10000.0 ** (-jnp.arange(HEAD // 2, dtype=F32) / (HEAD // 2))
    angles = jnp.arange(length, dtype=F32)[:, None] * frequency[None, :]
    cosine, sine = jnp.cos(angles), jnp.sin(angles)
    cosine = jnp.concatenate([cosine, cosine, cosine, cosine], axis=1)
    sine = jnp.concatenate([-sine, sine, -sine, sine], axis=1)

    weight_args, order, across = (), [], None
    if packed:
        shared = shared_pack(qkv_weight, out_weight, small_parts)
        across = swap(tok, "expert", 2)
        tok_a, tok_b, ranks = sequence_gather(tok, across)
        away = call(
            blocks_kernel,
            shaped((8 * shard_rows, 256), BF),
            (just_minor, expert_gate_up[0]),
            name="blocks",
            micros=1,
        )
        arrived = swap(away, "fsdp", 1)
        part = call(
            pack_kernel,
            shaped((16 * shard_rows, 256), BF),
            (just_minor, expert_gate_up[0], arrived),
            name="pack_expert",
            micros=1,
        )
        down = expert_down[0]
        own_half, other_half, order, down_near, down_far = shared_gather(
            shared, down, (across, arrived), (part, tok_b, cosine, sine)
        )
        down_onward = along(down_far, OUTWARD)
        down_middle = along(after(down, down_far), MIDDLE)
        weight_args = (own_half, other_half)
        far, near = along(part, FAR), along(part, NEAR)
    else:
        qkv_full = lax.all_gather(qkv_weight, "fsdp", axis=0, tiled=True)
        out_full = lax.all_gather(out_weight, "fsdp", axis=0, tiled=True)
        small_rows = jnp.concatenate(small_parts, axis=0)
        small = lax.all_gather(small_rows, "fsdp", axis=1, tiled=True).T
        small = jnp.pad(small, ((0, 0), (0, SMALL - small.shape[1])))
        small_t = small.astype(F32).T[:32]
        weight_args = (qkv_full, small_t)
        halves = expert_gate_up[0].reshape(shard_rows, 2, major_count, 2, unit)
        away = lax.dynamic_index_in_dim(halves, 1 - minor, 3, False).reshape(shard_rows, FF)
        kept = lax.dynamic_index_in_dim(halves, minor, 3, False).reshape(shard_rows, FF)
        arrived = swap(away, "fsdp", 1)
        part = jnp.concatenate(
            [jnp.where(minor == 0, kept, arrived), jnp.where(minor == 0, arrived, kept)], axis=0
        )
        gather = functools.partial(
            lax.all_gather,
            axis_name="fsdp",
            axis=0,
            tiled=True,
            axis_index_groups=minor_groups(major_count),
        )
        gate_up_half, down_half = gather(part), gather(expert_down[0])
        tok_a, tok_b, ranks = sequence_gather(tok, across)
    where = jnp.stack(
        [jnp.asarray(r, jnp.int32) for r in ranks] + [me_expert] + order + [core]
    )

    half_columns = 2 * width + SMALL
    outs = [
        shaped((count, width), BF),
        shaped((length, width), BF),
        shaped((length, width), BF),
        shaped((width, length), BF),
    ]
    out_specs = [
        pl.BlockSpec((count, width), fixed),
        pl.BlockSpec((count, width), at_rank),
        pl.BlockSpec((count, width), at_rank),
        pl.BlockSpec((width, count), lambda j, w: (0, w[j])),
    ]
    if packed:
        weight_specs = [pl.BlockSpec((width, half_columns), fixed)] * 2
        outs += [
            shaped((width, 3 * width), BF),
            shaped((width, width), BF),
            shaped((width, SMALL), BF),
            shaped((32, width), F32),
        ]
        out_specs += [pl.BlockSpec(o.shape, fixed) for o in outs[4:]]
    else:
        weight_specs = [pl.BlockSpec((width, 3 * width), fixed), pl.BlockSpec((32, width), fixed)]
    projected = call(
        functools.partial(project_kernel, slots=groups, gain_at=gain_one_at, placed=not packed),
        outs,
        (where, tok_a, tok_b, cosine, sine) + weight_args,
        grid=(groups,),
        in_specs=[
            pl.BlockSpec((count, width), lambda j, w: (jnp.minimum(j, groups // 2 - 1), 0)),
            pl.BlockSpec((count, width), lambda j, w: (jnp.maximum(j - groups // 2, 0), 0)),
            pl.BlockSpec((count, PAIR), at_rank),
            pl.BlockSpec((count, PAIR), at_rank),
        ]
        + weight_specs,
        out_specs=out_specs,
        name="project",
        micros=10,
    )
    q, k_all, v_all, normed = projected[:4]
    if packed:
        qkv_full, out_full, small, small_t = projected[4:]
    head_rows = pl.BlockSpec((count, PAIR), lambda h, w: (0, h))
    head_keys = pl.BlockSpec((length, PAIR), lambda h, w: (0, h))
    attended, attend_weights = call(
        functools.partial(attend_kernel, slots=groups),
        [shaped((count, width), BF), shaped((pairs, length, 2 * count), BF)],
        (where, q, k_all, v_all),
        grid=(pairs,),
        in_specs=[head_rows, head_keys, head_keys],
        out_specs=[
            head_rows,
            pl.BlockSpec((1, length, 2 * count), lambda h, w: (h, 0, 0)),
        ],
        name="attend",
        micros=12,
    )

    residual, route, cot = gate_residual[0].T, routes[0].T, cotangent[0]
    if packed:
        attended = after(attended, down_onward, down_middle)
    owners = [me_fsdp ^ (2 * j + i) for i in (0, 1) for j in range(4)]
    owners += [core, me_expert // 2]
    slots = jnp.stack([me_expert ^ j for j in range(groups)] + [me_fsdp] + owners)
    block = shaped((2 * MOST, width), BF)
    hidden, low_two, *sends = call(
        functools.partial(route_kernel, groups=groups, gain_at=gain_two_at),
        [shaped((count, width), F32), shaped((count, width), BF)] + [block] * groups,
        (slots, attended, out_full, tok, small, small_t, residual, route, cot),
        scratch=[pltpu.VMEM((groups * MOST, width), BF)] * 2,
        name="route",
        micros=5,
    )
    received, other_low, other_high = exchange(sends)
    if packed:
        far, near = lax.optimization_barrier((far, near, low_two))[:2]
        onward = along(far, OUTWARD)
        middle = along(after(part, far), MIDDLE)
        inner = jnp.logical_or(major == 1, major == 2).astype(jnp.int32)
        places = jnp.stack([major, major ^ 1, major ^ 2, major ^ 3, inner])
        weights = (part, near, far, middle, onward)
        weights += (down, down_near, down_far, down_middle, down_onward)
        grads = [shaped((part.shape[0] + 3 * 256, 256), BF)] * 4
        room = [pltpu.VMEM((width, 2 * units), BF), pltpu.VMEM((units, width), BF)]
        room += [pltpu.VMEM((width, 2 * groups * MOST), BF)]
    else:
        places = just_minor
        weights = (gate_up_half, down_half)
        grads = [shaped((width, 2 * units), BF), shaped((units, width), BF)]
        room = []
    rows_total = 2 * groups * MOST
    results = call(
        functools.partial(expert_kernel, groups=groups, hidden_units=units, packed=packed),
        [shaped((groups * MOST, width), F32)] * 2 + [shaped((groups * MOST, width), BF)] * 2 + grads,
        (places,) + tuple(received) + (other_low, other_high) + weights,
        scratch=[pltpu.VMEM((rows_total, width), BF)] * 2
        + [pltpu.VMEM((rows_total, width), F32)] * 2
        + [pltpu.VMEM((rows_total, units), BF), pltpu.VMEM((rows_total, 2 * units), BF)]
        + room,
        name="expert",
        micros=18,
    )
    own_low, own_high, part_low, part_high = results[:4]
    grads = results[4:]
    high = (own_high + swap(part_high, "fsdp", 1).astype(F32)).astype(BF)
    low = (own_low + swap(part_low, "fsdp", 1).astype(F32)).astype(BF)
    backs = exchange_back(low, high, groups)

    if packed:
        first = along(grads[3], INWARD)
        middle = along(grads[3], MIDDLE)
        sent = added(grads[2], first)
        near = along(after(grads[1], first), NEAR)
        cuts = (0, 8 * shard_rows, 14 * shard_rows, sent.shape[0])
        far = [along(sent[a:b], FAR) for a, b in zip(cuts, cuts[1:])]
        backs[0] = after(backs[0], sent, middle)
    else:
        scatter = lambda v: lax.psum_scatter(
            v,
            "fsdp",
            scatter_dimension=0,
            tiled=True,
            axis_index_groups=minor_groups(major_count),
        ).astype(F32)
        shard_down = scatter(grads[1])
        part = scatter(grads[0]).reshape(2, shard_rows, FF)
        away = lax.dynamic_index_in_dim(part, 1 - minor, 0, False).astype(BF)
        kept = lax.dynamic_index_in_dim(part, minor, 0, False)
        arrived = swap(away, "fsdp", 1).astype(F32)
        first = jnp.where(minor == 0, kept, arrived).reshape(shard_rows, 2, major_count, 1, unit)
        second = jnp.where(minor == 0, arrived, kept).reshape(shard_rows, 2, major_count, 1, unit)
        shard_gate_up = jnp.concatenate([first, second], axis=3).reshape(shard_rows, 2 * FF)

    columns = (kinds, mix_at, value_at, gain_two_at, square_at)
    part_rows = width // 2 if packed else width
    out_part = shaped((part_rows, width + SMALL), BF)
    outputs, grad_hidden, grad_att, out_away, out_kept, grad_residual = call(
        functools.partial(
            combine_kernel, groups=groups, columns=columns, shard_rows=shard_rows, packed=packed
        ),
        [
            shaped((count, width), BF),
            shaped((count, width), F32),
            shaped((count, width), BF),
            out_part,
            out_part,
            shaped((kinds, count), BF),
        ],
        (slots,) + tuple(backs)
        + (hidden, low_two, cot, route, residual, small, small_t, out_full, attended),
        scratch=[pltpu.VMEM((groups * MOST, width), BF)] * 2
        + [pltpu.VMEM((width, width + SMALL), F32)],
        name="combine",
        micros=10,
    )
    head_half = pairs // 2
    back_where = jnp.stack([jnp.asarray(r, jnp.int32) for r in ranks] + [me_expert] + owners)

    def attend_back(part, grad_rows):
        base = part * head_half
        from_rows = pl.BlockSpec((count, PAIR), lambda h, w: (0, base + h))
        from_keys = pl.BlockSpec((length, PAIR), lambda h, w: (0, base + h))
        to_rows = pl.BlockSpec((count, PAIR), lambda h, w: (0, h))
        to_keys = pl.BlockSpec((length, PAIR), lambda h, w: (0, h))
        grads_part = shaped((part_rows, 3 * width // 2), BF)
        return call(
            functools.partial(attend_back_kernel, slots=groups, packed=packed),
            [
                shaped((count, width // 2), BF),
                shaped((length, width // 2), BF),
                shaped((length, width // 2), BF),
                grads_part,
                grads_part,
            ],
            (back_where, q, k_all, v_all, grad_rows, attend_weights, cosine, sine, normed, normed),
            grid=(head_half,),
            in_specs=[
                from_rows,
                from_keys,
                from_keys,
                from_rows,
                pl.BlockSpec((1, length, 2 * count), lambda h, w: (base + h, 0, 0)),
                pl.BlockSpec((length, PAIR), fixed),
                pl.BlockSpec((length, PAIR), fixed),
                pl.BlockSpec((width, length), fixed),
                pl.BlockSpec((width, count), lambda h, w: (0, w[groups])),
            ],
            out_specs=[
                to_rows,
                to_keys,
                to_keys,
                pl.BlockSpec(grads_part.shape, fixed),
                pl.BlockSpec(grads_part.shape, fixed),
            ],
            scratch=[pltpu.VMEM((width, 3 * width // 2), F32)],
            name="attend_back",
            micros=11,
        )

    dq_a, dk_a, dv_a, a_away, a_kept = attend_back(0, grad_att)
    if packed:
        a_away, a_kept, out_kept = lax.optimization_barrier(
            (a_away, a_kept, out_kept, far[0], near)
        )[:3]
        out_both = added(out_kept, swap(out_away, "expert", 1))
        a_both = added(a_kept, swap(a_away, "expert", 1))
        grad_att = after(grad_att, a_both, out_both)
    dq_b, dk_b, dv_b, b_away, b_kept = attend_back(1, grad_att)
    def project_back(dq_late):
        half_rows = pl.BlockSpec((count, width // 2), fixed)
        half_keys = pl.BlockSpec((count, width // 2), at_rank)
        return call(
            functools.partial(project_back_kernel, slots=groups),
            [shaped((length, width), BF), shaped((count, width), F32)],
            (back_where, dq_a, dq_late, dk_a, dk_b, dv_a, dv_b, qkv_full),
            grid=(groups,),
            in_specs=[half_rows] * 2 + [half_keys] * 4 + [pl.BlockSpec((width, 3 * width), fixed)],
            out_specs=[pl.BlockSpec((count, width), at_rank), pl.BlockSpec((count, width), fixed)],
            name="project_back",
            micros=6,
        )

    if packed:
        b_away = after(b_away, far[1])
        out_sum, a_sum = along_chips(out_both, (b_kept,)), along_chips(a_both, (b_kept,))
        b_both = added(b_kept, swap(b_away, "expert", 1))
        dq_b = after(dq_b, b_both)
        b_sum = along_chips(b_both, ())
        parts_all = jnp.concatenate([a_sum, b_sum, out_sum], axis=1)
        rows_back, own_back = project_back(dq_b)
        total, piece = across_major(after(parts_all, rows_back), shard_rows // 4)
        own_grads = after(grads[0], piece)
        away, kept, shard_down = call(
            sum_parts_kernel,
            [
                shaped((8 * shard_rows, 256), BF),
                shaped((8 * shard_rows, 256), F32),
                shaped((256, width), F32),
            ],
            (just_minor, own_grads, near, middle) + tuple(far),
            name="sum_parts",
            micros=3,
        )
        shard_gate_up = call(
            unpack_kernel,
            shaped((shard_rows, 2 * FF), F32),
            (just_minor, kept, swap(away, "fsdp", 1)),
            name="unpack_expert",
            micros=2,
        )
    else:
        both = jnp.concatenate([a_kept, b_kept, out_kept], axis=1)
        both = lax.psum_scatter(both, "fsdp", scatter_dimension=0, tiled=True)
        total = lax.psum(both, "expert")
        other = total
        rows_back, own_back = project_back(dq_b)
    rows_sum = sequence_scatter_sum(rows_back, count)
    grad_tokens = call(
        functools.partial(finish_kernel, gain_at=gain_one_at),
        shaped((count, width), BF),
        (just_minor, tok, small_t, grad_hidden, own_back, rows_sum),
        name="finish",
        micros=3,
    )

    if packed:
        total = after(total, grad_tokens)
        total = jnp.concatenate([total, swap(total, "expert", 2)], axis=0)
        other = swap(total, "expert", 1)
    shared_grads = call(
        functools.partial(
            shared_kernel, columns=columns, width=width, entries=length * width, packed=packed
        ),
        [
            shaped((shard_rows, 3 * width), F32),
            shaped((shard_rows, width), F32),
            shaped((kinds, shard_rows), F32),
            shaped((2 * NCONST, shard_rows), F32),
            shaped((NCONST, shard_rows), F32),
            shaped((1, shard_rows), F32),
            shaped((1, shard_rows), F32),
            shaped((1, 2), F32),
        ],
        (jnp.stack([me_expert]), total, other, qkv_weight, gain_one[None]),
        scratch=[pltpu.VMEM((shard_rows, 4 * width + SMALL), F32)],
        name="shared_grads",
        micros=3,
    )
    grad_qkv, grad_out, grad_router, grad_gate, grad_value, grad_one, grad_two, stream = shared_grads
    return (
        outputs[None],
        grad_tokens[None],
        grad_one[0],
        grad_qkv,
        grad_out,
        grad_two[0],
        grad_router.T,
        grad_gate.T,
        grad_value.T,
        shard_gate_up[None],
        shard_down[None],
        grad_residual.T[None],
        stream,
    )


def solution(mesh):
    return jax.shard_map(
        on_device,
        mesh=mesh,
        in_specs=(
            P("fsdp", "expert", None),
            P("fsdp"),
            P("fsdp", None),
            P("fsdp", None),
            P("fsdp"),
            P("fsdp", None),
            P("fsdp", None),
            P("fsdp", None),
            P("expert", "fsdp", None),
            P("expert", "fsdp", None),
            P("fsdp", "expert", None),
            P("fsdp", "expert", None),
            P("fsdp", "expert", None),
        ),
        out_specs=(
            P("fsdp", "expert", None),
            P("fsdp", "expert", None),
            P("fsdp"),
            P("fsdp", None),
            P("fsdp", None),
            P("fsdp"),
            P("fsdp", None),
            P("fsdp", None),
            P("fsdp", None),
            P("expert", "fsdp", None),
            P("expert", "fsdp", None),
            P("fsdp", "expert", None),
            P("fsdp", None),
        ),
        check_vma=False,
    )
```

```python
import functools

import jax
import jax.numpy as jnp
from jax import lax
from jax.experimental import pallas as pl
from jax.experimental.pallas import tpu as pltpu
from jax.sharding import PartitionSpec as P

HEAD = 64
FF = 2048
NCONST = 2
MOST = 80
PAIR = 2 * HEAD
SMALL = 128

epsilon = 1e-06
masked_score = -1e30
BF = jnp.bfloat16
F32 = jnp.float32


def mm(a, b):
    return jnp.dot(a, b, preferred_element_type=F32)


def mm_nt(a, b):
    return lax.dot_general(a, b, (((1,), (1,)), ((), ())), preferred_element_type=F32)


def mm_tn(a, b):
    return lax.dot_general(a, b, (((0,), (0,)), ((), ())), preferred_element_type=F32)


def split_low(values):
    high = values.astype(BF)
    return high, (values - high.astype(F32)).astype(BF)


def lanes(shape):
    return lax.broadcasted_iota(jnp.int32, shape, len(shape) - 1)


def rows_of(shape):
    return lax.broadcasted_iota(jnp.int32, shape, 0)


def rms_scale(values):
    return lax.rsqrt(jnp.mean(values * values, axis=-1, keepdims=True) + epsilon)


def turned(values, cosine, sine):
    lane = lanes(values.shape) % HEAD
    swapped = jnp.where(
        lane < HEAD // 2,
        pltpu.roll(values, PAIR - HEAD // 2, 1),
        pltpu.roll(values, HEAD // 2, 1),
    )
    return values * cosine + swapped * sine


def call(kernel, outs, args, grid=(), in_specs=None, out_specs=None, scratch=(), scalars=1, name=None, micros=2):
    whole = pl.BlockSpec(memory_space=pltpu.VMEM)
    multi = isinstance(outs, (tuple, list))
    if in_specs is None:
        in_specs = [whole] * (len(args) - scalars)
    if out_specs is None:
        out_specs = [whole] * len(outs) if multi else whole
    return pl.pallas_call(
        kernel,
        out_shape=outs,
        grid_spec=pltpu.PrefetchScalarGridSpec(
            num_scalar_prefetch=scalars,
            grid=grid,
            in_specs=in_specs,
            out_specs=out_specs,
            scratch_shapes=list(scratch),
        ),
        compiler_params=pltpu.CompilerParams(vmem_limit_bytes=56 * 1024 * 1024),
        cost_estimate=pl.CostEstimate(
            flops=micros * 90_000_000, transcendentals=0, bytes_accessed=micros * 300_000
        ),
        name=name,
    )(*args)


def shaped(shape, dtype):
    return jax.ShapeDtypeStruct(shape, dtype)


def swap(values, axis, bits):
    size = lax.axis_size(axis)
    return lax.ppermute(values, axis, [(i, i ^ bits) for i in range(size)])


def along(values, pairs):
    return lax.ppermute(
        values, "fsdp", [(2 * i + b, 2 * j + b) for i, j in pairs for b in (0, 1)]
    )


def after(values, *others):
    return lax.optimization_barrier((values,) + tuple(others))[0]


FAR = ((0, 2), (2, 0), (1, 3), (3, 1))
NEAR = ((0, 1), (1, 0), (2, 3), (3, 2))
MIDDLE = ((1, 2), (2, 1))
OUTWARD = ((2, 3), (1, 0))
INWARD = ((0, 1), (3, 2))


def minor_groups(major):
    return [[2 * i + b for i in range(major)] for b in (0, 1)]


def blocks_kernel(where, gate_up, out):
    rows = gate_up.shape[0]
    for block in range(8):
        at = (2 * block + 1 - where[0]) * 256
        out[block * rows : (block + 1) * rows, :] = gate_up[:, pl.ds(pl.multiple_of(at, 256), 256)]


def pack_kernel(where, gate_up, arrived, out):
    rows = gate_up.shape[0]
    mine = where[0]
    for block in range(8):
        at = (2 * block + mine) * 256
        own = pl.ds(pl.multiple_of(2 * block * rows + mine * rows, rows), rows)
        other = pl.ds(pl.multiple_of(2 * block * rows + (1 - mine) * rows, rows), rows)
        out[own, :] = gate_up[:, pl.ds(pl.multiple_of(at, 256), 256)]
        out[other, :] = arrived[block * rows : (block + 1) * rows, :]


def sum_parts_kernel(where, a, b, c, d0, d1, d2, away, kept, down):
    rows = away.shape[0] // 8
    mine = where[0]

    def total(start, size, d, base):
        source, shifted = pl.ds(start, size), pl.ds(start - base, size)
        return (
            a[source, :].astype(F32)
            + b[source, :].astype(F32)
            + c[source, :].astype(F32)
            + d[shifted, :].astype(F32)
        )

    for block in range(8):
        here = slice(block * rows, (block + 1) * rows)
        base = 2 * block * rows
        d, cut = ((d0, 0), (d1, 4 * rows), (d2, 10 * rows))[(block > 1) + (block > 4)]
        own = pl.multiple_of(base + mine * rows, rows)
        other = pl.multiple_of(base + (1 - mine) * rows, rows)
        away[here, :] = total(other, rows, d, cut).astype(BF)
        kept[here, :] = total(own, rows, d, cut)
    for block in range(3):
        base = 16 * rows + block * 256
        down[:, block * 256 : (block + 1) * 256] = total(base, 256, d2, 10 * rows)


def unpack_kernel(where, kept, arrived, out):
    rows = out.shape[0]
    mine = where[0]
    for block in range(8):
        here = slice(block * rows, (block + 1) * rows)
        own = pl.ds(pl.multiple_of((2 * block + mine) * 256, 256), 256)
        other = pl.ds(pl.multiple_of((2 * block + 1 - mine) * 256, 256), 256)
        out[:, own] = kept[here, :]
        out[:, other] = arrived[here, :].astype(F32)


def shared_pack(qkv, out, small):
    core = lax.axis_index("expert") % 2
    half_qkv, half_out = qkv.shape[1] // 2, out.shape[1] // 2
    rows = qkv.shape[0]

    def kernel(where, qkv_ref, out_ref, *refs):
        small_refs, (packed, room) = refs[:-2], refs[-2:]
        packed[:, :half_qkv] = qkv_ref[:, pl.ds(pl.multiple_of(where[0] * half_qkv, 128), half_qkv)]
        packed[:, half_qkv : half_qkv + half_out] = out_ref[
            :, pl.ds(pl.multiple_of(where[0] * half_out, 128), half_out)
        ]
        room[...] = jnp.zeros_like(room)
        at = 0
        for ref in small_refs:
            room[at : at + ref.shape[0], : ref.shape[1]] = ref[...].astype(F32)
            at += ref.shape[0]
        packed[:, half_qkv + half_out :] = room[...].astype(BF)

    return call(
        kernel,
        shaped((rows, half_qkv + half_out + SMALL), BF),
        (jnp.stack([core]).astype(jnp.int32), qkv, out) + small,
        scratch=[pltpu.VMEM((rows, SMALL), F32)],
        name="pack_shared",
        micros=1,
    )


def shared_gather(mine, down, early, late):
    me = lax.axis_index("fsdp")
    major = [mine, swap(mine, "fsdp", 2), swap(mine, "fsdp", 4)]
    minor = [swap(mine, "fsdp", 1)]
    major.append(swap(after(mine, minor[0]), "fsdp", 6))
    minor.append(swap(after(major[1], minor[0]), "fsdp", 1))
    minor.append(swap(after(major[2], *early), "fsdp", 1))
    minor.append(swap(after(major[3], minor[1], *late), "fsdp", 1))
    down_near = along(after(down, major[3]), NEAR)
    down_far = along(after(down, major[3]), FAR)
    slots = [2 * j for j in range(4)] + [2 * j + 1 for j in range(4)]
    own = after(jnp.concatenate(major + minor, axis=0), down_near, down_far)
    return own, swap(own, "expert", 1), [me ^ s for s in slots], down_near, down_far


def added(kept, arrived):
    return (kept.astype(F32) + arrived.astype(F32)).astype(BF)


def along_chips(both, gate):
    for axis, bits in (("expert", 2), ("fsdp", 1)):
        half = both.shape[0] // 2
        both = added(after(both[:half], *gate), swap(both[half:], axis, bits))
        gate = ()
    return both


def across_major(parts, rows):
    pieces = [swap(parts[j * rows : (j + 1) * rows], "fsdp", 2 * j) for j in (1, 2, 3)]
    total = parts[:rows].astype(F32)
    for piece in pieces:
        total += piece.astype(F32)
    return total.astype(BF), pieces[0]


def sequence_gather(values, across):
    size = lax.axis_size("expert")
    me = lax.axis_index("expert")
    if size != 4:
        every = lax.all_gather(values, "expert", axis=0, tiled=True)
        middle = every.shape[0] // 2
        return every[:middle], every[middle:], list(range(size))
    pair = jnp.concatenate([values, across], axis=0)
    return pair, swap(pair, "expert", 1), [me, me ^ 2, me ^ 1, me ^ 3]


def exchange(sends):
    half = len(sends) // 2
    received = [swap(v, "expert", j) if j else v for j, v in enumerate(sends)]
    low = swap(jnp.concatenate(received[:half], axis=0), "fsdp", 1)
    high = swap(after(jnp.concatenate(received[half:], axis=0), low), "fsdp", 1)
    return received, low, high


def exchange_back(low, high, size):
    rows = 2 * low.shape[0] // size
    if size == 4:
        upper = swap(high, "expert", 2)
        joined = swap(jnp.concatenate([low[rows:], upper[rows:]], axis=0), "expert", 1)
        return [low[:rows], joined[:rows], upper[:rows], joined[rows:]]
    pieces = [w[i : i + rows] for w in (low, high) for i in range(0, w.shape[0], rows)]
    return [swap(piece, "expert", j) if j else piece for j, piece in enumerate(pieces)]


def sequence_scatter_sum(full, rows):
    size = lax.axis_size("expert")
    me = lax.axis_index("expert")
    if size != 4:
        return lax.psum_scatter(full, "expert", scatter_dimension=0, tiled=True).astype(F32)

    def block(bits):
        return lax.dynamic_slice_in_dim(full, (me ^ bits) * rows, rows, 0)

    away = jnp.concatenate([block(1), block(3)], axis=0)
    kept = jnp.concatenate([block(0), block(2)], axis=0)
    both = kept.astype(F32) + swap(away, "expert", 1).astype(F32)
    return both[:rows] + swap(both[rows:].astype(BF), "expert", 2).astype(F32)


def project_kernel(where, *refs, slots, gain_at, placed):
    if placed:
        tok_a, tok_b, cosine, sine, weight, small_t, q, k, v, normed = refs
    else:
        tok_a, tok_b, cosine, sine, own_ref, other_ref = refs[:6]
        q, k, v, normed, weight, out_ref, small_ref, small_t = refs[6:]
    step = pl.program_id(0)
    rank = where[step]
    own = where[slots]
    width = tok_a.shape[1]

    if not placed:

        @pl.when(step == 0)
        def _():
            first = where[slots + 9] == 0
            rows = width // 8
            half_qkv, half_out = 3 * width // 2, width // 2
            for index in range(8):
                source = pl.ds(index * rows, rows)
                target = pl.ds(pl.multiple_of(where[slots + 1 + index] * rows, rows), rows)
                a, b = own_ref[source, :], other_ref[source, :]
                left = jnp.where(first, a, b)
                right = jnp.where(first, b, a)
                weight[target, :half_qkv] = left[:, :half_qkv]
                weight[target, half_qkv:] = right[:, :half_qkv]
                out_ref[target, :half_out] = left[:, half_qkv : half_qkv + half_out]
                out_ref[target, half_out:] = right[:, half_qkv : half_qkv + half_out]
                of_rows = jnp.zeros((SMALL, SMALL), F32)
                of_rows = jnp.concatenate(
                    [a[:32, half_qkv + half_out :].astype(F32), of_rows[32:]], axis=0
                ).T
                small_ref[target, :] = of_rows[:rows].astype(BF)
            small_t[...] = small_ref[...].astype(F32).T[:32]

    @pl.when(rank > own)
    def _():
        k[...] = jnp.zeros_like(k)
        v[...] = jnp.zeros_like(v)
        normed[...] = jnp.zeros_like(normed)

    @pl.when(rank <= own)
    def _():
        x = jnp.where(step < slots // 2, tok_a[...], tok_b[...]).astype(F32)
        wide = (x * rms_scale(x)) * small_t[gain_at : gain_at + 1, :]
        low = wide.astype(BF)
        normed[...] = low.T
        cos, sin = cosine[...], sine[...]
        keys = mm(low, weight[:, width : 2 * width])
        for at in range(0, width, PAIR):
            k[:, at : at + PAIR] = turned(keys[:, at : at + PAIR], cos, sin).astype(BF)
        v[...] = mm(low, weight[:, 2 * width :]).astype(BF)

        @pl.when(rank == own)
        def _():
            queries = mm(low, weight[:, :width])
            for at in range(0, width, PAIR):
                q[:, at : at + PAIR] = turned(queries[:, at : at + PAIR], cos, sin).astype(BF)


def stacked_heads(values, scale=None):
    lane = lanes(values.shape)
    if scale is not None:
        values = values * jnp.asarray(scale, values.dtype)
    zero = jnp.zeros_like(values)
    return jnp.concatenate(
        [jnp.where(lane < HEAD, values, zero), jnp.where(lane < HEAD, zero, values)], axis=0
    )


def visible_keys(own, keys, count):
    key = lax.broadcasted_iota(jnp.int32, (keys, 2 * count), 0)
    query = lax.broadcasted_iota(jnp.int32, (keys, 2 * count), 1) % count
    return key <= query + own * count


def attend_kernel(where, q, k, v, attended, kept, *, slots):
    own = where[slots]
    count, keys = q.shape[0], k.shape[0]
    query = stacked_heads(q[...], HEAD ** (-0.5))
    scores = mm_nt(k[...], query)
    scores = jnp.where(visible_keys(own, keys, count), scores, masked_score)
    top = jnp.max(scores, axis=0, keepdims=True)
    weights = jnp.exp(scores - top)
    total = jnp.sum(weights, axis=0, keepdims=True)
    weights = (weights * (1.0 / total)).astype(BF)
    kept[0] = weights
    both = mm_tn(v[...], weights).T
    lane = lanes((count, PAIR))
    attended[...] = jnp.where(lane < HEAD, both[:count], both[count:]).astype(BF)


def attend_back_kernel(where, q, k, v, grad_att, kept_weights, cosine, sine, normed, normed_own, dq, dk, dv, away, kept, sums, *, slots, packed):
    step = pl.program_id(0)
    own = where[slots]
    count = q.shape[0]
    query = stacked_heads(q[...], HEAD ** (-0.5))
    grad_rows = stacked_heads(grad_att[...])
    key_rows = k[...]
    low_weights = kept_weights[0]
    weights = low_weights.astype(F32)
    grad_weights = mm_nt(v[...], grad_rows)
    delta = jnp.sum(weights * grad_weights, axis=0, keepdims=True)
    grad_scores = (weights * (grad_weights - delta)).astype(BF)
    grad_v = mm(low_weights, grad_rows).astype(BF)
    dv[...] = grad_v
    grad_k = turned(mm(grad_scores, query), cosine[...], -sine[...]).astype(BF)
    dk[...] = grad_k
    both = mm_tn(key_rows, grad_scores).T
    lane = lanes((count, PAIR))
    grad_q = jnp.where(lane < HEAD, both[:count], both[count:]) * HEAD ** (-0.5)
    mine = pl.ds(pl.multiple_of(own * count, count), count)
    grad_q = turned(grad_q, cosine[mine, :], -sine[mine, :]).astype(BF)
    dq[...] = grad_q
    of_keys = mm(normed[...], jnp.concatenate([grad_k, grad_v], axis=1))
    of_queries = mm(normed_own[...], grad_q)
    steps = kept.shape[1] // (3 * PAIR)
    for index in range(steps):

        @pl.when(step == index)
        def _():
            for part, values in enumerate((of_queries, of_keys[:, :PAIR], of_keys[:, PAIR:])):
                at = (part * steps + index) * PAIR
                sums[:, at : at + PAIR] = values

    @pl.when(step == steps - 1)
    def _():
        if packed:
            split_rows(where, slots + 1, sums, away, kept)
        else:
            kept[...] = sums[...].astype(BF)
            away[...] = jnp.zeros_like(away)


def split_rows(where, at, values, away, kept):
    core, chip = where[at + 8], where[at + 9]
    rows = values.shape[0] // 32
    for index in range(0, 16, 2):
        target = slice(index * rows, (index + 2) * rows)
        for ref, side in ((kept, core), (away, 1 - core)):
            pieces = []
            for step in (index, index + 1):
                rank = 2 * (chip ^ (step // 8)) + side
                base = (where[at + step % 8] * 4 + rank) * rows
                pieces.append(values[pl.ds(pl.multiple_of(base, 8), rows), :])
            ref[target, :] = jnp.concatenate(pieces, axis=0).astype(BF)


def as_lanes(rows):
    rows = rows.astype(F32)
    spare = jnp.zeros((SMALL - rows.shape[0], rows.shape[1]), F32)
    return jnp.concatenate([rows, spare], axis=0).T


def routing(routes, resid, logits, groups):
    count = routes.shape[0]
    lane = lanes((count, SMALL))
    logits = logits + resid
    hot, picked = [], []
    for choice in range(2):
        route = routes[:, choice : choice + 1]
        hot.append(lane == route)
        picked.append(jnp.sum(jnp.where(hot[choice], logits, 0.0), axis=-1, keepdims=True))
    top = jnp.maximum(picked[0], picked[1])
    first, second = jnp.exp(picked[0] - top), jnp.exp(picked[1] - top)
    gates = [first / (first + second), second / (first + second)]
    named = jnp.logical_or(hot[0], hot[1]).astype(BF)
    earlier = (lanes((count, count)) < rows_of((count, count))).astype(BF)
    place = mm(earlier, named)
    dispatch = []
    column = lanes((count, groups * MOST))
    for choice in range(2):
        route = routes[:, choice : choice + 1]
        slot = jnp.sum(jnp.where(hot[choice], place, 0.0), axis=-1, keepdims=True)
        target = jnp.where(route < groups, route * MOST + slot.astype(jnp.int32), -1)
        dispatch.append((column == target).astype(BF))
    return gates, hot, dispatch


def route_kernel(where, att, out_weight, tok, small, small_t, resid, routes, cot, hidden_ref, low_ref, *rest, groups, gain_at):
    sends = rest[:groups]
    rows_x, rows_g = rest[groups], rest[groups + 1]
    hidden = tok[...].astype(F32) + mm(att[...], out_weight[...])
    hidden_ref[...] = hidden
    low = ((hidden * rms_scale(hidden)) * small_t[gain_at : gain_at + 1, :]).astype(BF)
    low_ref[...] = low
    logits = mm(low, small[...])
    route = as_lanes(routes[...])[:, :2].astype(jnp.int32)
    gates, _, dispatch = routing(route, as_lanes(resid[...]), logits, groups)
    grad = cot[...].astype(F32)
    rows_x[...] = mm_tn(dispatch[0] + dispatch[1], low).astype(BF)
    rows_g[...] = (
        mm_tn(dispatch[0], (gates[0] * grad).astype(BF))
        + mm_tn(dispatch[1], (gates[1] * grad).astype(BF))
    ).astype(BF)
    for slot in range(groups):
        source = pl.ds(pl.multiple_of(where[slot] * MOST, MOST), MOST)
        sends[slot][:MOST, :] = rows_x[source, :]
        sends[slot][MOST:, :] = rows_g[source, :]


def expert_kernel(where, *refs, groups, hidden_units, packed):
    refs = list(refs)

    def take(amount):
        taken = refs[:amount]
        del refs[:amount]
        return taken

    received = take(groups) + take(2)
    if packed:
        unit_parts, down_parts = take(5), take(5)
    else:
        gate_up, down = take(2)
    own_out, other_out = take(2), take(2)
    if packed:
        messages = take(4)
    else:
        grad_gate_up, grad_down = take(2)
    rows, grads, out_rows, back_rows, acts, grad_units = take(6)
    if packed:
        gate_up, down, rows_t = take(3)
    width = rows.shape[1]
    total = 2 * groups * MOST
    index = 0
    for ref in received:
        for base in range(0, ref.shape[0], 2 * MOST):
            target = slice(index * MOST, (index + 1) * MOST)
            rows[target, :] = ref[base : base + MOST, :]
            grads[target, :] = ref[base + MOST : base + 2 * MOST, :]
            index += 1
    if packed:
        part = width // 4

        def place(slot, ref, down_ref):
            target = pl.ds(pl.multiple_of(where[slot] * part, part), part)
            for block in range(8):
                gate_up[target, block * 256 : (block + 1) * 256] = ref[
                    block * part : (block + 1) * part, :
                ]
            down[pl.ds(pl.multiple_of(where[slot] * 256, 256), 256), :] = down_ref[...]

        for slot in range(3):
            place(slot, unit_parts[slot], down_parts[slot])

        @pl.when(where[4] == 1)
        def _():
            place(3, unit_parts[3], down_parts[3])

        @pl.when(where[4] == 0)
        def _():
            place(3, unit_parts[4], down_parts[4])

    x, g = rows[...], grads[...]
    chunk = 256
    out_rows[...] = jnp.zeros_like(out_rows)
    back_rows[...] = jnp.zeros_like(back_rows)

    def forward_back(step, carry):
        first = pl.ds(pl.multiple_of(step * chunk, chunk), chunk)
        second = pl.ds(pl.multiple_of(hidden_units + step * chunk, chunk), chunk)
        gate_w, up_w, down_w = gate_up[:, first], gate_up[:, second], down[first, :]
        gate, up = mm(x, gate_w), mm(x, up_w)
        sig = 1.0 / (1.0 + jnp.exp(-gate))
        silu = gate * sig
        act = (silu * up).astype(BF)
        acts[:, first] = act
        grad_act = mm_nt(g, down_w)
        grad_gate = (grad_act * up * sig * (1.0 + gate * (1.0 - sig))).astype(BF)
        grad_up = (grad_act * silu).astype(BF)
        grad_units[:, first] = grad_gate
        grad_units[:, second] = grad_up
        out_rows[...] += mm(act, down_w)
        back_rows[...] += mm_nt(grad_gate, gate_w) + mm_nt(grad_up, up_w)
        return carry

    lax.fori_loop(0, hidden_units // chunk, forward_back, 0)
    index = 0
    for ref in own_out + other_out:
        for base in range(0, ref.shape[0], 2 * MOST):
            source = slice(index * MOST, (index + 1) * MOST)
            ref[base : base + MOST, :] = out_rows[source, :].astype(ref.dtype)
            ref[base + MOST : base + 2 * MOST, :] = back_rows[source, :].astype(ref.dtype)
            index += 1
    if not packed:
        grad_gate_up[...] = mm_tn(x, grad_units[...]).astype(BF)
        grad_down[...] = mm_tn(acts[...], g).astype(BF)
        return
    part = width // 4

    def weight_grad(step, carry):
        block = pl.ds(pl.multiple_of(step * 512, 512), 512)
        gate_up[:, block] = mm(rows_t[...], grad_units[:, block]).astype(BF)
        return carry

    rows_t[...] = x.T
    lax.fori_loop(0, 4, weight_grad, 0)
    for slot, ref in enumerate(messages):
        source = pl.ds(pl.multiple_of(where[slot] * part, part), part)
        for block in range(8):
            ref[block * part : (block + 1) * part, :] = gate_up[
                source, block * 256 : (block + 1) * 256
            ]
        mine = acts[:, pl.ds(pl.multiple_of(where[slot] * 256, 256), 256)]
        of_down = mm_tn(mine, g).astype(BF)
        for block in range(3):
            base = 8 * part + block * 256
            ref[base : base + 256, :] = of_down[:, block * 256 : (block + 1) * 256]


def combine_kernel(where, *refs, groups, columns, shard_rows, packed):
    backs = refs[:groups]
    (hidden_ref, low_ref, cot, routes, resid, small, small_t, out_weight, att,
     out_ref, grad_hidden_ref, grad_att_ref, grad_away, grad_kept, grad_resid,
     rows_y, rows_d, sums) = refs[groups:]
    kinds, mix_at, value_at, gain_two_at, square_at = columns
    for slot in range(groups):
        target = pl.ds(pl.multiple_of(where[slot] * MOST, MOST), MOST)
        rows_y[target, :] = backs[slot][:MOST, :]
        rows_d[target, :] = backs[slot][MOST:, :]
    hidden, low = hidden_ref[...], low_ref[...]
    count = low.shape[0]
    normed_input = low.astype(F32)
    grad_low_type = cot[...]
    grad = grad_low_type.astype(F32)
    logits = mm(low, small[...])
    grad_small_dot = mm(grad_low_type, small[...])
    route = as_lanes(routes[...])[:, :2].astype(jnp.int32)
    gates, hot, dispatch = routing(route, as_lanes(resid[...]), logits, groups)
    returned = [mm(dispatch[c], rows_y[...]) for c in range(2)]
    grad_back = mm(dispatch[0] + dispatch[1], rows_d[...])
    grad_dot = jnp.sum(grad * normed_input, axis=-1, keepdims=True)
    is_copy = [(route[:, c : c + 1] == groups + 1).astype(F32) for c in range(2)]
    grad_gates = [
        jnp.sum(grad * returned[c], axis=-1, keepdims=True) + is_copy[c] * grad_dot
        for c in range(2)
    ]
    direct = gates[0] * is_copy[0] + gates[1] * is_copy[1]
    mixture = gates[0] * returned[0] + gates[1] * returned[1]
    lane = lanes((count, SMALL))
    grad_logits = jnp.zeros((count, SMALL), F32)
    value_weights = jnp.zeros((count, SMALL), F32)
    for const in range(NCONST):
        first = logits[:, mix_at + 2 * const : mix_at + 2 * const + 1]
        second = logits[:, mix_at + 2 * const + 1 : mix_at + 2 * const + 2]
        top = jnp.maximum(first, second)
        first, second = jnp.exp(first - top), jnp.exp(second - top)
        mix = [first / (first + second), second / (first + second)]
        value_dot = grad_small_dot[:, value_at + const : value_at + const + 1]
        named = [(route[:, c : c + 1] == groups + 2 + const).astype(F32) for c in range(2)]
        for c in range(2):
            grad_gates[c] += named[c] * (mix[0] * grad_dot + mix[1] * value_dot)
        weight = gates[0] * named[0] + gates[1] * named[1]
        direct += weight * mix[0]
        of_value = weight * mix[1]
        mixture += of_value * small_t[value_at + const : value_at + const + 1, :]
        value_weights = jnp.where(lane == value_at + const, of_value, value_weights)
        grad_mix = [weight * grad_dot, weight * value_dot]
        common = mix[0] * grad_mix[0] + mix[1] * grad_mix[1]
        for c in range(2):
            grad_logits = jnp.where(
                lane == mix_at + 2 * const + c, mix[c] * (grad_mix[c] - common), grad_logits
            )
    outputs = hidden + mixture + direct * normed_input
    out_ref[...] = outputs.astype(BF)
    common = gates[0] * grad_gates[0] + gates[1] * grad_gates[1]
    for c in range(2):
        grad_logits = jnp.where(hot[c], gates[c] * (grad_gates[c] - common), grad_logits)
    grad_resid[...] = grad_logits.T[:kinds].astype(BF)
    high, rest = split_low(grad_logits)
    weights = small[...]
    grad_low = grad_back + direct * grad + mm_nt(high, weights) + mm_nt(rest, weights)
    scale = rms_scale(hidden)
    normed = hidden * scale
    of_gain = jnp.sum((grad_low * normed).reshape(-1, 8, normed.shape[1]), axis=0)
    of_gain = jnp.sum(of_gain, axis=0, keepdims=True)
    value_high, value_rest = split_low(value_weights)
    summed = mm_tn(low, jnp.concatenate([high, rest], axis=1))
    summed += mm_tn(grad_low_type, jnp.concatenate([value_high, value_rest], axis=1))
    summed = summed[:, :SMALL] + summed[:, SMALL:]
    wide = (SMALL, normed.shape[1])
    summed += jnp.where(rows_of(wide) == gain_two_at, of_gain, 0.0).T
    column, row = lanes(summed.shape), rows_of(summed.shape)
    mine = row // shard_rows == where[groups]
    for index, total in enumerate((jnp.sum(hidden * hidden), jnp.sum(outputs * outputs))):
        for part, value in enumerate(split_low(jnp.full((1, 1), total, F32))):
            spot = jnp.logical_and(mine, column == square_at + 2 * index + part)
            summed = jnp.where(spot, value.astype(F32), summed)
    grad_normed = grad_low * small_t[gain_two_at : gain_two_at + 1, :]
    grad_hidden = grad + scale * (
        grad_normed - normed * jnp.mean(grad_normed * normed, axis=-1, keepdims=True)
    )
    grad_hidden_ref[...] = grad_hidden
    branch = grad_hidden.astype(BF)
    grad_att_ref[...] = mm_nt(branch, out_weight[...]).astype(BF)
    width = branch.shape[1]
    sums[:, :width] = mm_tn(att[...], branch)
    sums[:, width:] = summed
    if packed:
        split_rows(where, groups + 1, sums, grad_away, grad_kept)
    else:
        grad_kept[...] = sums[...].astype(BF)
        grad_away[...] = jnp.zeros_like(grad_away)


def project_back_kernel(where, *refs, slots):
    queries, keys, values = refs[0:2], refs[2:4], refs[4:6]
    weight, rows_back, own_back = refs[6:]
    rank = where[pl.program_id(0)]
    own = where[slots]
    half = keys[0].shape[1]
    width = 2 * half

    def through(parts, base):
        result = mm_nt(parts[0][...], weight[:, base : base + half])
        return result + mm_nt(parts[1][...], weight[:, base + half : base + width])

    @pl.when(rank > own)
    def _():
        rows_back[...] = jnp.zeros_like(rows_back)

    @pl.when(rank <= own)
    def _():
        rows_back[...] = (through(keys, width) + through(values, 2 * width)).astype(BF)

        @pl.when(rank == own)
        def _():
            own_back[...] = through(queries, 0)


def finish_kernel(where, tok, small_t, grad_hidden, own_back, rows_back, out, *, gain_at):
    x = tok[...].astype(F32)
    scale = rms_scale(x)
    normed = x * scale
    grad = (own_back[...] + rows_back[...]) * small_t[gain_at : gain_at + 1, :]
    out[...] = (
        grad_hidden[...]
        + scale * (grad - normed * jnp.mean(grad * normed, axis=-1, keepdims=True))
    ).astype(BF)


def shared_kernel(where, total, other, weight, gain, qkv, out, router, gate, value, gain_one, gain_two, stream, room, *, columns, width, entries, packed):
    kinds, mix_at, value_at, gain_two_at, square_at = columns
    if packed:
        rows = room.shape[0] // 4
        for parts, rank in ((total, where[0]), (other, where[0] ^ 1)):
            both = parts[...].astype(F32)
            room[pl.ds(pl.multiple_of(rank * rows, 8), rows), :] = both[:rows]
            room[pl.ds(pl.multiple_of((rank ^ 2) * rows, 8), rows), :] = both[rows:]
    else:
        room[...] = total[...].astype(F32)
    values = room[...]
    half = width // 2
    for part in range(3):
        for side in range(2):
            at = (3 * side + part) * half
            to = part * width + side * half
            qkv[:, to : to + half] = values[:, at : at + half]
    out[...] = values[:, 3 * width : 4 * width]
    rows = values.shape[0]

    def as_columns(block):
        spare = jnp.zeros((SMALL - rows, SMALL), F32)
        return jnp.concatenate([block, spare], axis=0).T[:, :rows]

    small = values[:, 4 * width :]
    turned_small = as_columns(small)
    router[...] = turned_small[:kinds]
    gate[...] = turned_small[mix_at : mix_at + 2 * NCONST]
    value[...] = turned_small[value_at : value_at + NCONST]
    gain_two[...] = turned_small[gain_two_at : gain_two_at + 1]
    of_gain = jnp.sum(qkv[...] * weight[...].astype(F32), axis=-1, keepdims=True)
    gain_one[...] = as_columns(jnp.broadcast_to(of_gain, (rows, SMALL)))[:1] / gain[...].astype(F32)
    squares = small[:1, square_at : square_at + 4]
    hidden = squares[:, 0:1] + squares[:, 1:2]
    outputs = squares[:, 2:3] + squares[:, 3:4]
    stream[...] = jnp.sqrt(jnp.where(lanes((1, 2)) == 0, hidden, outputs) / entries)


def on_device(
    tokens,
    gain_one,
    qkv_weight,
    out_weight,
    gain_two,
    router_weight,
    const_gate,
    const_value,
    expert_gate_up,
    expert_down,
    gate_residual,
    routes,
    cotangent,
):
    parts = lax.axis_size("fsdp")
    groups = lax.axis_size("expert")
    me_fsdp = lax.axis_index("fsdp").astype(jnp.int32)
    me_expert = lax.axis_index("expert").astype(jnp.int32)
    minor, major, core = me_fsdp % 2, me_fsdp // 2, me_expert % 2
    packed = parts == 8 and groups == 4
    major_count = parts // 2
    tok = tokens[0]
    count, width = tok.shape
    length = groups * count
    pairs = width // PAIR
    kinds = router_weight.shape[1]
    mix_at, value_at = kinds, kinds + 2 * NCONST
    gain_one_at = value_at + NCONST
    gain_two_at = gain_one_at + 1
    square_at = gain_two_at + 1
    shard_rows = width // parts
    unit = FF // parts
    units = FF // 2
    fixed = lambda j, w: (0, 0)
    at_slot = lambda j, w: (j, 0)
    at_rank = lambda j, w: (w[j], 0)
    just_minor = jnp.stack([minor])

    small_parts = (router_weight.T, const_gate.T, const_value.T, gain_one[None], gain_two[None])
    frequency = 10000.0 ** (-jnp.arange(HEAD // 2, dtype=F32) / (HEAD // 2))
    angles = jnp.arange(length, dtype=F32)[:, None] * frequency[None, :]
    cosine, sine = jnp.cos(angles), jnp.sin(angles)
    cosine = jnp.concatenate([cosine, cosine, cosine, cosine], axis=1)
    sine = jnp.concatenate([-sine, sine, -sine, sine], axis=1)

    weight_args, order, across = (), [], None
    if packed:
        shared = shared_pack(qkv_weight, out_weight, small_parts)
        across = swap(tok, "expert", 2)
        tok_a, tok_b, ranks = sequence_gather(tok, across)
        away = call(
            blocks_kernel,
            shaped((8 * shard_rows, 256), BF),
            (just_minor, expert_gate_up[0]),
            name="blocks",
            micros=1,
        )
        arrived = swap(away, "fsdp", 1)
        part = call(
            pack_kernel,
            shaped((16 * shard_rows, 256), BF),
            (just_minor, expert_gate_up[0], arrived),
            name="pack_expert",
            micros=1,
        )
        down = expert_down[0]
        own_half, other_half, order, down_near, down_far = shared_gather(
            shared, down, (across, arrived), (part, tok_b, cosine, sine)
        )
        down_onward = along(down_far, OUTWARD)
        down_middle = along(after(down, down_far), MIDDLE)
        weight_args = (own_half, other_half)
        far, near = along(part, FAR), along(part, NEAR)
    else:
        qkv_full = lax.all_gather(qkv_weight, "fsdp", axis=0, tiled=True)
        out_full = lax.all_gather(out_weight, "fsdp", axis=0, tiled=True)
        small_rows = jnp.concatenate(small_parts, axis=0)
        small = lax.all_gather(small_rows, "fsdp", axis=1, tiled=True).T
        small = jnp.pad(small, ((0, 0), (0, SMALL - small.shape[1])))
        small_t = small.astype(F32).T[:32]
        weight_args = (qkv_full, small_t)
        halves = expert_gate_up[0].reshape(shard_rows, 2, major_count, 2, unit)
        away = lax.dynamic_index_in_dim(halves, 1 - minor, 3, False).reshape(shard_rows, FF)
        kept = lax.dynamic_index_in_dim(halves, minor, 3, False).reshape(shard_rows, FF)
        arrived = swap(away, "fsdp", 1)
        part = jnp.concatenate(
            [jnp.where(minor == 0, kept, arrived), jnp.where(minor == 0, arrived, kept)], axis=0
        )
        gather = functools.partial(
            lax.all_gather,
            axis_name="fsdp",
            axis=0,
            tiled=True,
            axis_index_groups=minor_groups(major_count),
        )
        gate_up_half, down_half = gather(part), gather(expert_down[0])
        tok_a, tok_b, ranks = sequence_gather(tok, across)
    where = jnp.stack(
        [jnp.asarray(r, jnp.int32) for r in ranks] + [me_expert] + order + [core]
    )

    half_columns = 2 * width + SMALL
    outs = [
        shaped((count, width), BF),
        shaped((length, width), BF),
        shaped((length, width), BF),
        shaped((width, length), BF),
    ]
    out_specs = [
        pl.BlockSpec((count, width), fixed),
        pl.BlockSpec((count, width), at_rank),
        pl.BlockSpec((count, width), at_rank),
        pl.BlockSpec((width, count), lambda j, w: (0, w[j])),
    ]
    if packed:
        weight_specs = [pl.BlockSpec((width, half_columns), fixed)] * 2
        outs += [
            shaped((width, 3 * width), BF),
            shaped((width, width), BF),
            shaped((width, SMALL), BF),
            shaped((32, width), F32),
        ]
        out_specs += [pl.BlockSpec(o.shape, fixed) for o in outs[4:]]
    else:
        weight_specs = [pl.BlockSpec((width, 3 * width), fixed), pl.BlockSpec((32, width), fixed)]
    projected = call(
        functools.partial(project_kernel, slots=groups, gain_at=gain_one_at, placed=not packed),
        outs,
        (where, tok_a, tok_b, cosine, sine) + weight_args,
        grid=(groups,),
        in_specs=[
            pl.BlockSpec((count, width), lambda j, w: (jnp.minimum(j, groups // 2 - 1), 0)),
            pl.BlockSpec((count, width), lambda j, w: (jnp.maximum(j - groups // 2, 0), 0)),
            pl.BlockSpec((count, PAIR), at_rank),
            pl.BlockSpec((count, PAIR), at_rank),
        ]
        + weight_specs,
        out_specs=out_specs,
        name="project",
        micros=10,
    )
    q, k_all, v_all, normed = projected[:4]
    if packed:
        qkv_full, out_full, small, small_t = projected[4:]
    head_rows = pl.BlockSpec((count, PAIR), lambda h, w: (0, h))
    head_keys = pl.BlockSpec((length, PAIR), lambda h, w: (0, h))
    attended, attend_weights = call(
        functools.partial(attend_kernel, slots=groups),
        [shaped((count, width), BF), shaped((pairs, length, 2 * count), BF)],
        (where, q, k_all, v_all),
        grid=(pairs,),
        in_specs=[head_rows, head_keys, head_keys],
        out_specs=[
            head_rows,
            pl.BlockSpec((1, length, 2 * count), lambda h, w: (h, 0, 0)),
        ],
        name="attend",
        micros=12,
    )

    residual, route, cot = gate_residual[0].T, routes[0].T, cotangent[0]
    if packed:
        attended = after(attended, down_onward, down_middle)
    owners = [me_fsdp ^ (2 * j + i) for i in (0, 1) for j in range(4)]
    owners += [core, me_expert // 2]
    slots = jnp.stack([me_expert ^ j for j in range(groups)] + [me_fsdp] + owners)
    block = shaped((2 * MOST, width), BF)
    hidden, low_two, *sends = call(
        functools.partial(route_kernel, groups=groups, gain_at=gain_two_at),
        [shaped((count, width), F32), shaped((count, width), BF)] + [block] * groups,
        (slots, attended, out_full, tok, small, small_t, residual, route, cot),
        scratch=[pltpu.VMEM((groups * MOST, width), BF)] * 2,
        name="route",
        micros=5,
    )
    received, other_low, other_high = exchange(sends)
    if packed:
        far, near = lax.optimization_barrier((far, near, low_two))[:2]
        onward = along(far, OUTWARD)
        middle = along(after(part, far), MIDDLE)
        inner = jnp.logical_or(major == 1, major == 2).astype(jnp.int32)
        places = jnp.stack([major, major ^ 1, major ^ 2, major ^ 3, inner])
        weights = (part, near, far, middle, onward)
        weights += (down, down_near, down_far, down_middle, down_onward)
        grads = [shaped((part.shape[0] + 3 * 256, 256), BF)] * 4
        room = [pltpu.VMEM((width, 2 * units), BF), pltpu.VMEM((units, width), BF)]
        room += [pltpu.VMEM((width, 2 * groups * MOST), BF)]
    else:
        places = just_minor
        weights = (gate_up_half, down_half)
        grads = [shaped((width, 2 * units), BF), shaped((units, width), BF)]
        room = []
    rows_total = 2 * groups * MOST
    results = call(
        functools.partial(expert_kernel, groups=groups, hidden_units=units, packed=packed),
        [shaped((groups * MOST, width), F32)] * 2 + [shaped((groups * MOST, width), BF)] * 2 + grads,
        (places,) + tuple(received) + (other_low, other_high) + weights,
        scratch=[pltpu.VMEM((rows_total, width), BF)] * 2
        + [pltpu.VMEM((rows_total, width), F32)] * 2
        + [pltpu.VMEM((rows_total, units), BF), pltpu.VMEM((rows_total, 2 * units), BF)]
        + room,
        name="expert",
        micros=18,
    )
    own_low, own_high, part_low, part_high = results[:4]
    grads = results[4:]
    high = (own_high + swap(part_high, "fsdp", 1).astype(F32)).astype(BF)
    low = (own_low + swap(part_low, "fsdp", 1).astype(F32)).astype(BF)
    backs = exchange_back(low, high, groups)

    if packed:
        first = along(grads[3], INWARD)
        middle = along(grads[3], MIDDLE)
        sent = added(grads[2], first)
        near = along(after(grads[1], first), NEAR)
        cuts = (0, 4 * shard_rows, 10 * shard_rows, sent.shape[0])
        far = [along(sent[a:b], FAR) for a, b in zip(cuts, cuts[1:])]
        backs[0] = after(backs[0], sent, middle)
    else:
        scatter = lambda v: lax.psum_scatter(
            v,
            "fsdp",
            scatter_dimension=0,
            tiled=True,
            axis_index_groups=minor_groups(major_count),
        ).astype(F32)
        shard_down = scatter(grads[1])
        part = scatter(grads[0]).reshape(2, shard_rows, FF)
        away = lax.dynamic_index_in_dim(part, 1 - minor, 0, False).astype(BF)
        kept = lax.dynamic_index_in_dim(part, minor, 0, False)
        arrived = swap(away, "fsdp", 1).astype(F32)
        first = jnp.where(minor == 0, kept, arrived).reshape(shard_rows, 2, major_count, 1, unit)
        second = jnp.where(minor == 0, arrived, kept).reshape(shard_rows, 2, major_count, 1, unit)
        shard_gate_up = jnp.concatenate([first, second], axis=3).reshape(shard_rows, 2 * FF)

    columns = (kinds, mix_at, value_at, gain_two_at, square_at)
    part_rows = width // 2 if packed else width
    out_part = shaped((part_rows, width + SMALL), BF)
    outputs, grad_hidden, grad_att, out_away, out_kept, grad_residual = call(
        functools.partial(
            combine_kernel, groups=groups, columns=columns, shard_rows=shard_rows, packed=packed
        ),
        [
            shaped((count, width), BF),
            shaped((count, width), F32),
            shaped((count, width), BF),
            out_part,
            out_part,
            shaped((kinds, count), BF),
        ],
        (slots,) + tuple(backs)
        + (hidden, low_two, cot, route, residual, small, small_t, out_full, attended),
        scratch=[pltpu.VMEM((groups * MOST, width), BF)] * 2
        + [pltpu.VMEM((width, width + SMALL), F32)],
        name="combine",
        micros=10,
    )
    head_half = pairs // 2
    back_where = jnp.stack([jnp.asarray(r, jnp.int32) for r in ranks] + [me_expert] + owners)

    def attend_back(part, grad_rows):
        base = part * head_half
        from_rows = pl.BlockSpec((count, PAIR), lambda h, w: (0, base + h))
        from_keys = pl.BlockSpec((length, PAIR), lambda h, w: (0, base + h))
        to_rows = pl.BlockSpec((count, PAIR), lambda h, w: (0, h))
        to_keys = pl.BlockSpec((length, PAIR), lambda h, w: (0, h))
        grads_part = shaped((part_rows, 3 * width // 2), BF)
        return call(
            functools.partial(attend_back_kernel, slots=groups, packed=packed),
            [
                shaped((count, width // 2), BF),
                shaped((length, width // 2), BF),
                shaped((length, width // 2), BF),
                grads_part,
                grads_part,
            ],
            (back_where, q, k_all, v_all, grad_rows, attend_weights, cosine, sine, normed, normed),
            grid=(head_half,),
            in_specs=[
                from_rows,
                from_keys,
                from_keys,
                from_rows,
                pl.BlockSpec((1, length, 2 * count), lambda h, w: (base + h, 0, 0)),
                pl.BlockSpec((length, PAIR), fixed),
                pl.BlockSpec((length, PAIR), fixed),
                pl.BlockSpec((width, length), fixed),
                pl.BlockSpec((width, count), lambda h, w: (0, w[groups])),
            ],
            out_specs=[
                to_rows,
                to_keys,
                to_keys,
                pl.BlockSpec(grads_part.shape, fixed),
                pl.BlockSpec(grads_part.shape, fixed),
            ],
            scratch=[pltpu.VMEM((width, 3 * width // 2), F32)],
            name="attend_back",
            micros=11,
        )

    dq_a, dk_a, dv_a, a_away, a_kept = attend_back(0, grad_att)
    if packed:
        a_away, a_kept, out_kept = lax.optimization_barrier(
            (a_away, a_kept, out_kept, far[0], near)
        )[:3]
        out_both = added(out_kept, swap(out_away, "expert", 1))
        a_both = added(a_kept, swap(a_away, "expert", 1))
        grad_att = after(grad_att, a_both, out_both)
    dq_b, dk_b, dv_b, b_away, b_kept = attend_back(1, grad_att)
    def project_back(dq_late):
        half_rows = pl.BlockSpec((count, width // 2), fixed)
        half_keys = pl.BlockSpec((count, width // 2), at_rank)
        return call(
            functools.partial(project_back_kernel, slots=groups),
            [shaped((length, width), BF), shaped((count, width), F32)],
            (back_where, dq_a, dq_late, dk_a, dk_b, dv_a, dv_b, qkv_full),
            grid=(groups,),
            in_specs=[half_rows] * 2 + [half_keys] * 4 + [pl.BlockSpec((width, 3 * width), fixed)],
            out_specs=[pl.BlockSpec((count, width), at_rank), pl.BlockSpec((count, width), fixed)],
            name="project_back",
            micros=6,
        )

    if packed:
        b_away = after(b_away, far[1])
        out_sum, a_sum = along_chips(out_both, (b_kept,)), along_chips(a_both, (b_kept,))
        b_both = added(b_kept, swap(b_away, "expert", 1))
        dq_b = after(dq_b, b_both)
        b_sum = along_chips(b_both, ())
        parts_all = jnp.concatenate([a_sum, b_sum, out_sum], axis=1)
        rows_back, own_back = project_back(dq_b)
        total, piece = across_major(after(parts_all, rows_back), shard_rows // 4)
        own_grads = after(grads[0], piece)
        away, kept, shard_down = call(
            sum_parts_kernel,
            [
                shaped((8 * shard_rows, 256), BF),
                shaped((8 * shard_rows, 256), F32),
                shaped((256, width), F32),
            ],
            (just_minor, own_grads, near, middle) + tuple(far),
            name="sum_parts",
            micros=3,
        )
        shard_gate_up = call(
            unpack_kernel,
            shaped((shard_rows, 2 * FF), F32),
            (just_minor, kept, swap(away, "fsdp", 1)),
            name="unpack_expert",
            micros=2,
        )
    else:
        both = jnp.concatenate([a_kept, b_kept, out_kept], axis=1)
        both = lax.psum_scatter(both, "fsdp", scatter_dimension=0, tiled=True)
        total = lax.psum(both, "expert")
        other = total
        rows_back, own_back = project_back(dq_b)
    rows_sum = sequence_scatter_sum(rows_back, count)
    grad_tokens = call(
        functools.partial(finish_kernel, gain_at=gain_one_at),
        shaped((count, width), BF),
        (just_minor, tok, small_t, grad_hidden, own_back, rows_sum),
        name="finish",
        micros=3,
    )

    if packed:
        total = after(total, grad_tokens)
        total = jnp.concatenate([total, swap(total, "expert", 2)], axis=0)
        other = swap(total, "expert", 1)
    shared_grads = call(
        functools.partial(
            shared_kernel, columns=columns, width=width, entries=length * width, packed=packed
        ),
        [
            shaped((shard_rows, 3 * width), F32),
            shaped((shard_rows, width), F32),
            shaped((kinds, shard_rows), F32),
            shaped((2 * NCONST, shard_rows), F32),
            shaped((NCONST, shard_rows), F32),
            shaped((1, shard_rows), F32),
            shaped((1, shard_rows), F32),
            shaped((1, 2), F32),
        ],
        (jnp.stack([me_expert]), total, other, qkv_weight, gain_one[None]),
        scratch=[pltpu.VMEM((shard_rows, 4 * width + SMALL), F32)],
        name="shared_grads",
        micros=3,
    )
    grad_qkv, grad_out, grad_router, grad_gate, grad_value, grad_one, grad_two, stream = shared_grads
    return (
        outputs[None],
        grad_tokens[None],
        grad_one[0],
        grad_qkv,
        grad_out,
        grad_two[0],
        grad_router.T,
        grad_gate.T,
        grad_value.T,
        shard_gate_up[None],
        shard_down[None],
        grad_residual.T[None],
        stream,
    )


def solution(mesh):
    return jax.shard_map(
        on_device,
        mesh=mesh,
        in_specs=(
            P("fsdp", "expert", None),
            P("fsdp"),
            P("fsdp", None),
            P("fsdp", None),
            P("fsdp"),
            P("fsdp", None),
            P("fsdp", None),
            P("fsdp", None),
            P("expert", "fsdp", None),
            P("expert", "fsdp", None),
            P("fsdp", "expert", None),
            P("fsdp", "expert", None),
            P("fsdp", "expert", None),
        ),
        out_specs=(
            P("fsdp", "expert", None),
            P("fsdp", "expert", None),
            P("fsdp"),
            P("fsdp", None),
            P("fsdp", None),
            P("fsdp"),
            P("fsdp", None),
            P("fsdp", None),
            P("fsdp", None),
            P("expert", "fsdp", None),
            P("expert", "fsdp", None),
            P("fsdp", "expert", None),
            P("fsdp", None),
        ),
        check_vma=False,
    )
```
